128 devices in a mesh: owner: 16 (over y, z), kvh: 8 (over x, core).
Axes of the slice: x: 4, y: 4, z: 4, core: 2. Of those that a mesh axis runs over, the one named last changes fastest.
Arguments:
- queries: bfloat16 [32, 32, 64, 128], P('owner', None, 'kvh'), may hold values from -6 to 6
- new_keys: bfloat16 [32, 32, 8, 128], P('owner', None, 'kvh'), may hold values from -6 to 6
- new_values: bfloat16 [32, 32, 8, 128], P('owner', None, 'kvh'), may hold values from -6 to 6
- ancestors: int32 [32, 32], P('owner'), may hold values from 0 to 95, as said below
- tile_keys: bfloat16 [96, 8, 512, 128], P('owner', 'kvh'), may hold values from -6 to 6
- tile_values: bfloat16 [96, 8, 512, 128], P('owner', 'kvh'), may hold values from -6 to 6
- tile_lengths: int32 [96], P('owner'), may hold values from 2 to 512
- out_weight: bfloat16 [8192, 8192], P('kvh'), may hold values from -0.0625 to 0.0625
Outputs:
- mixed: bfloat16 [1024, 8192], P(('owner', 'kvh'))
The draws below stay inside these ranges and needn't reach their ends.
Inputs may be any that keep to these rules, and one draw needn't show every extreme that they name: `ancestors`: each row names 32 different tiles.
All inputs are finite; a program needn't handle non-finite values.
Results may differ from the reference program's by a relative error of at most 0.017.
Values may be sent and summed in bfloat16 or wider, within the bound.
No kernel may reach another device: no remote copies, remote signals or barrier semaphores. Data moves between devices by JAX's collectives and lax.ppermute only.
A program may use at most 320 MiB of HBM per device.

```python
import math
import jax
import jax.numpy as jnp
from jax import lax

D = 8192
HEAD = 128
QPG = 8
TILE = 512
HT = 32
NEW = 32
KVHEADS = 8
QHEADS = 64
PARTICLES = 32
TILES = 96
N_OWNER = 16


def ancestry(key):
    base_key = jax.random.fold_in(key, 11)
    spread_key = jax.random.fold_in(key, 12)
    favour = jax.random.randint(base_key, (TILES,), 0, 3) * 4096
    noise_part = jax.random.randint(spread_key, (PARTICLES, TILES), 0, 4096)
    scores_int = favour[None, :] + noise_part
    ordering = jnp.argsort(-scores_int, axis=1, stable=True)
    return ordering[:, :HT].astype(jnp.int32)


def draw_ancestors(key, part):
    return ancestry(key)


def drawn(key):
    coin_bits = jax.random.randint(jax.random.fold_in(key, 21), (KVHEADS, HEAD), 0, 2)
    sign_rows = (2 * coin_bits - 1).astype(jnp.float32)
    lead_row = 6.0 * sign_rows
    lowered_count = int(1.5 * math.sqrt(HEAD))
    lowered_mask = (jnp.arange(HEAD) < lowered_count).astype(jnp.float32)
    next_row = sign_rows * (6.0 - 0.25 * lowered_mask)[None, :]
    return (sign_rows, lead_row, next_row)


def chosen():
    return jnp.arange(PARTICLES) % 4 == 0


def normal_part(key, shape):
    return jnp.clip(jax.random.normal(key, shape, jnp.float32), -6.0, 6.0)


def draw_queries(key, part):
    values = normal_part(jax.random.fold_in(key, 31), (PARTICLES, NEW, QHEADS, HEAD))
    sign_rows, lead_row, next_row = drawn(key)
    levels = jnp.array([3.0, 4.0], jnp.float32)
    heads = jnp.arange(QHEADS)
    group_of = heads // QPG
    positions = jnp.arange(NEW)
    strength = levels[(group_of[None, :] + positions[:, None]) % levels.shape[0]]
    planted = sign_rows[group_of][None, :, :] * strength[:, :, None]
    token_hit = (positions == NEW - 1) | (positions == NEW // 2)
    head_hit = heads % QPG == 0
    selected = chosen()[:, None, None] & token_hit[None, :, None] & head_hit[None, None, :]
    return jnp.where(selected[..., None], planted[None], values).astype(jnp.bfloat16)


def draw_new_keys(key, part):
    values = normal_part(jax.random.fold_in(key, 32), (PARTICLES, NEW, KVHEADS, HEAD))
    sign_rows, lead_row, next_row = drawn(key)
    positions = jnp.arange(NEW)
    planted = jnp.where((positions == 0)[:, None, None], lead_row[None], next_row[None])
    selected = chosen()[:, None] & (positions < 2)[None, :]
    return jnp.where(selected[:, :, None, None], planted[None], values).astype(jnp.bfloat16)


def draw_tile_keys(key, part):
    values = normal_part(jax.random.fold_in(key, 33), (TILES, KVHEADS, TILE, HEAD))
    sign_rows, lead_row, next_row = drawn(key)
    history = ancestry(key)
    first_tiles = jnp.where(chosen(), history[:, 0], -1)
    planted_tiles = jnp.any(first_tiles[:, None] == jnp.arange(TILES)[None, :], axis=0)
    slots = jnp.arange(TILE)
    planted = jnp.where((slots == 0)[None, :, None], lead_row[:, None, :], next_row[:, None, :])
    selected = planted_tiles[:, None] & (slots < 2)[None, :]
    return jnp.where(selected[:, None, :, None], planted[None], values).astype(jnp.bfloat16)


def plant(result, key, smallest, top_value):
    longest = result.shape.index(max(result.shape))
    spots = []
    for shift in (0, 1):
        where = [jax.random.randint(jax.random.fold_in(key, axis), (), 0, length) for axis, length in enumerate(result.shape)]
        where[longest] = (where[longest] + shift) % result.shape[longest]
        spots.append(tuple(where))
    return result.at[spots[0]].set(smallest).at[spots[1]].set(top_value)


def level_of(key, shape, pieces, low, top_value):
    gain, own = 1.0, jax.random.fold_in(key, 6)
    for dim, parts in pieces:
        draws = jnp.exp(jax.random.uniform(jax.random.fold_in(own, dim), (parts,), jnp.float32, low / len(pieces), top_value / len(pieces)))
        gain = gain * jnp.repeat(draws, shape[dim] // parts).reshape([-1 if axis == dim else 1 for axis in range(len(shape))])
    return gain


def scatter_about(rng, shape, deviation, most, split=(), kind=jnp.bfloat16):
    factor_of = level_of(rng, shape, split, -0.22, 0.18) if split else 1.0
    drawn = jax.random.normal(rng, shape, jnp.float32) * deviation * factor_of
    return jnp.minimum(jnp.maximum(drawn, -most), most).astype(kind)


def setup_inputs(seed: int = 0) -> dict:
    key_list = jax.random.split(jax.random.key(seed), 9)
    queries = draw_queries(jax.random.fold_in(key_list[8], 71), 0)
    new_keys = draw_new_keys(jax.random.fold_in(key_list[8], 71), 0)
    new_values = scatter_about(key_list[2], (PARTICLES, NEW, KVHEADS, HEAD), 1.0, 6.0, ((0, 16), (2, 8)))
    ancestors = draw_ancestors(jax.random.fold_in(key_list[8], 71), 0)
    tile_keys = draw_tile_keys(jax.random.fold_in(key_list[8], 71), 0)
    tile_values = scatter_about(key_list[5], (TILES, KVHEADS, TILE, HEAD), 1.0, 6.0, ((0, 16), (1, 8)))
    tile_lengths = plant(jax.random.randint(key_list[6], (TILES,), 2, TILE + 1), jax.random.fold_in(key_list[6], 1), 2, TILE).astype(jnp.int32)
    out_weight = scatter_about(key_list[7], (QHEADS * HEAD, D), (QHEADS * HEAD) ** -0.5, 0.0625, ((0, 8),))
    return {"queries": queries, "new_keys": new_keys, "new_values": new_values, "ancestors": ancestors, "tile_keys": tile_keys, "tile_values": tile_values, "tile_lengths": tile_lengths, "out_weight": out_weight}


NEG = -1e30


def owner_partial(qrows, keys, values, live, member):
    count_p, rows, width = qrows.shape
    count, size = keys.shape[0], keys.shape[1]
    flat = qrows.reshape(count_p * rows, width)
    scores = jnp.dot(flat, keys.reshape(count * size, width).T, preferred_element_type=jnp.float32) * (width ** -0.5)
    scores = scores.reshape(count_p, rows, count * size)
    valid = jnp.repeat(member, size, axis=1)[:, None, :] & live.reshape(count * size)[None, None, :]
    masked = jnp.where(valid, scores, NEG)
    peak = jnp.max(masked, axis=2)
    weights = jnp.where(valid, jnp.exp(masked - peak[..., None]), 0.0)
    total = jnp.sum(weights, axis=2)
    summed = jnp.dot(weights.astype(jnp.bfloat16).reshape(count_p * rows, count * size),
                     values.reshape(count * size, width), preferred_element_type=jnp.float32)
    summed = summed.reshape(count_p, rows, width)
    safe = jnp.where(total > 0, total, 1.0)
    average = jnp.where(total[..., None] > 0, summed / safe[..., None], 0.0).astype(jnp.bfloat16)
    return average, peak, total


def self_partial(query, keys, values):
    count_p, new, group, width = query.shape
    scores = jnp.einsum('ntgh,nsh->ntgs', query.astype(jnp.float32), keys.astype(jnp.float32)) * (width ** -0.5)
    steps = jnp.arange(new)
    causal = (steps[:, None] >= steps[None, :])[None, :, None, :]
    masked = jnp.where(causal, scores, NEG)
    peak = jnp.max(masked, axis=3)
    weights = jnp.where(causal, jnp.exp(masked - peak[..., None]), 0.0)
    total = jnp.sum(weights, axis=3)
    summed = jnp.einsum('ntgs,nsh->ntgh', weights.astype(jnp.bfloat16).astype(jnp.float32), values.astype(jnp.float32))
    rows = new * group
    return summed.reshape(count_p, rows, width), peak.reshape(count_p, rows), total.reshape(count_p, rows)


def combine(own, average, peak, total):
    own_sum, own_peak, own_total = own
    top = jnp.maximum(own_peak, jnp.max(peak, axis=0))
    own_factor = jnp.exp(own_peak - top)
    factor = total * jnp.exp(peak - top[None])
    denom = own_total * own_factor + jnp.sum(factor, axis=0)
    numer = own_sum * own_factor[..., None] + jnp.sum(factor[..., None] * average.astype(jnp.float32), axis=0)
    return (numer / denom[..., None]).astype(jnp.bfloat16)


def reference(queries, new_keys, new_values, ancestors, tile_keys, tile_values, tile_lengths, out_weight):
    count_p, new, heads, width = queries.shape
    heads_kv = new_keys.shape[2]
    group = heads // heads_kv
    tiles, size = tile_keys.shape[0], tile_keys.shape[2]
    per_owner = tiles // N_OWNER
    member = jnp.any(ancestors[:, :, None] == jnp.arange(tiles, dtype=jnp.int32)[None, None, :], axis=1)
    member_own = member.reshape(count_p, N_OWNER, per_owner).transpose(1, 0, 2)
    live = jnp.arange(size, dtype=jnp.int32)[None, :] < tile_lengths[:, None]
    live_own = live.reshape(N_OWNER, per_owner, size)
    keys_own = tile_keys.reshape(N_OWNER, per_owner, heads_kv, size, width)
    values_own = tile_values.reshape(N_OWNER, per_owner, heads_kv, size, width)
    outputs = []
    for head in range(heads_kv):
        query = queries[:, :, head * group:(head + 1) * group, :]
        qrows = query.reshape(count_p, new * group, width)

        def one(items):
            return owner_partial(qrows, items[0], items[1], items[2], items[3])

        average, peak, total = lax.map(one, (keys_own[:, :, head], values_own[:, :, head], live_own, member_own))
        own = self_partial(query, new_keys[:, :, head], new_values[:, :, head])
        outputs.append(combine(own, average, peak, total).reshape(count_p, new, group * width))
    attention = jnp.concatenate(outputs, axis=2).reshape(count_p * new, heads * width)
    return jnp.dot(attention, out_weight, preferred_element_type=jnp.float32).astype(jnp.bfloat16)
```

```python
import functools
import math

import jax
import jax.numpy as jnp
from jax import lax
from jax.experimental import pallas as pl
from jax.experimental.pallas import tpu as pltpu
from jax.sharding import PartitionSpec as P

NEG = -1e30
CHUNKS = 2
META = 16
STEP = 128
F32 = jnp.float32
BF16 = jnp.bfloat16


def to_lanes(column, count):
    r = lax.broadcasted_iota(jnp.int32, (128, 128), 0)
    c = lax.broadcasted_iota(jnp.int32, (128, 128), 1)
    eye = r == c
    rows = []
    for b in range(count // 128):
        wide = jnp.broadcast_to(column[b * 128 : (b + 1) * 128], (128, 128))
        rows.append(jnp.sum(jnp.where(eye, wide, 0.0), axis=0, keepdims=True))
    return rows


def attend_kernel(scale, halves, member, widths, q_ref, k_ref, v_ref, o_ref, m_ref, acc_ref):
    homes = q_ref.shape[0]
    rows = q_ref.shape[1] - META
    tiles, size = k_ref.shape[0], k_ref.shape[1]
    part = rows // halves
    which = lax.broadcasted_iota(jnp.int32, (rows, 1), 0) // part

    def one_tile(h, t, width):
        q = q_ref[h, :rows, :]
        s = lax.dot_general(q, k_ref[t, :width, :], (((1,), (1,)), ((), ())), preferred_element_type=F32)
        flag = jnp.zeros((rows, 1), F32)
        for i in range(halves):
            flag = jnp.where(which == i, member[(h * halves + i) * tiles + t].astype(F32), flag)
        inside = flag > 0.5
        old = m_ref[...]
        new = jnp.where(inside, jnp.maximum(old, jnp.max(s, axis=1, keepdims=True)), old)
        shift = jnp.where(inside, new * scale, -NEG)
        p = jnp.exp2(s * scale - shift).astype(BF16)
        alpha = jnp.exp2((old - new) * scale)
        m_ref[...] = new
        acc_ref[...] = acc_ref[...] * alpha + jnp.dot(p, v_ref[t, :width, :], preferred_element_type=F32)

    @pl.loop(0, homes)
    def _(h):
        m_ref[...] = jnp.full(m_ref.shape, NEG, F32)
        acc_ref[...] = jnp.zeros(acc_ref.shape, F32)

        @pl.loop(0, tiles)
        def _(t):
            used = member[h * halves * tiles + t]
            for i in range(1, halves):
                used = used + member[(h * halves + i) * tiles + t]
            steps = jnp.where(used > 0, widths[t], 0)
            for n in range(1, size // STEP + 1):

                @pl.when(steps == n)
                def _():
                    one_tile(h, t, n * STEP)

        total = acc_ref[:, 128:129]
        some = total > 0.0
        safe = jnp.where(some, total, 1.0)
        o_ref[h, :rows, :] = jnp.where(some, acc_ref[:, :128] / safe, 0.0).astype(BF16)
        level = jnp.where(some, m_ref[...] * scale + jnp.log(safe) * (1.0 / math.log(2.0)), NEG)
        pieces = []
        for row in to_lanes(level, rows):
            high = row.astype(BF16).astype(F32)
            mid = (row - high).astype(BF16).astype(F32)
            low = row - high - mid
            pieces += [high, mid, low]
        pad = jnp.zeros((META - len(pieces), 128), F32)
        o_ref[h, rows:, :] = jnp.concatenate(pieces + [pad], axis=0).astype(BF16)


def attend(q, keys, values, member, widths, scale, halves):
    homes, held, width = q.shape
    rows = held - META
    vmem = pl.BlockSpec(memory_space=pltpu.VMEM)
    smem = pl.BlockSpec(memory_space=pltpu.SMEM)
    return pl.pallas_call(
        functools.partial(attend_kernel, scale, halves),
        out_shape=jax.ShapeDtypeStruct(q.shape, BF16),
        in_specs=[smem, smem, vmem, vmem, vmem],
        out_specs=vmem,
        scratch_shapes=[pltpu.VMEM((rows, 1), F32), pltpu.VMEM((rows, 2 * width), F32)],
        compiler_params=pltpu.CompilerParams(vmem_limit_bytes=24 << 20),
        cost_estimate=pl.CostEstimate(flops=4 << 30, bytes_accessed=4 << 20, transcendentals=6 << 20),
        name="attend",
    )(member, widths, q, keys, values)


def own_kernel(scale, group, first, q_ref, k_ref, v_ref, o_ref):
    halves, part, width = q_ref.shape
    new = k_ref.shape[1]
    rows = halves * part
    for i in range(halves):
        s = lax.dot_general(q_ref[i], k_ref[i], (((1,), (1,)), ((), ())), preferred_element_type=F32)
        row = lax.broadcasted_iota(jnp.int32, (part, new), 0) // group
        position = first(row)
        seen = position >= lax.broadcasted_iota(jnp.int32, (part, new), 1)
        s = jnp.where(seen, s, NEG)
        peak = jnp.max(s, axis=1, keepdims=True)
        weights = jnp.where(seen, jnp.exp2((s - peak) * scale), 0.0)
        total = jnp.sum(weights, axis=1, keepdims=True)
        summed = jnp.dot(weights.astype(BF16), v_ref[i], preferred_element_type=F32)
        o_ref[i * part : (i + 1) * part, :] = summed / total
        level = peak * scale + jnp.log(total) * (1.0 / math.log(2.0))
        rowed = to_lanes(level, part)
        for b, line in enumerate(rowed):
            at = rows + i * len(rowed) + b
            o_ref[at : at + 1, :] = line


def own_part(q, keys, values, scale, group, first):
    halves, part, width = q.shape
    vmem = pl.BlockSpec(memory_space=pltpu.VMEM)
    return pl.pallas_call(
        functools.partial(own_kernel, scale, group, first),
        out_shape=jax.ShapeDtypeStruct((halves * part + 8, width), F32),
        in_specs=[vmem] * 3,
        out_specs=vmem,
        cost_estimate=pl.CostEstimate(flops=1 << 22, bytes_accessed=1 << 18, transcendentals=1 << 14),
        name="own",
    )(q, keys, values)


def project_kernel(group, a_ref, own_ref, w_ref, o_ref, sum_ref, flat_ref):
    owners = a_ref.shape[0]
    rows = a_ref.shape[1] - META
    width = a_ref.shape[2]

    @pl.when(pl.program_id(0) == 0)
    def _():
        for b in range(rows // 128):
            lines = [own_ref[rows + b : rows + b + 1, :]]
            for o in range(owners):
                meta = a_ref[o, rows:, :].astype(F32)
                lines.append(meta[3 * b : 3 * b + 1] + meta[3 * b + 1 : 3 * b + 2] + meta[3 * b + 2 : 3 * b + 3])
            level = jnp.concatenate(lines + [jnp.full((128 - len(lines), 128), NEG, F32)], axis=0)
            top = jnp.max(level, axis=0, keepdims=True)
            weight = jnp.exp2(level - top)
            weight = weight / jnp.sum(weight, axis=0, keepdims=True)
            weight = weight.T
            here = slice(b * 128, (b + 1) * 128)
            acc = own_ref[here, :] * weight[:, 0:1]
            for o in range(owners):
                acc = acc + a_ref[o, here, :].astype(F32) * weight[:, o + 1 : o + 2]
            sum_ref[here, :] = acc
        for g in range(group):
            flat_ref[:, g * width : (g + 1) * width] = sum_ref[pl.ds(g, rows // group, stride=group), :].astype(BF16)

    o_ref[...] = jnp.dot(flat_ref[...], w_ref[...], preferred_element_type=F32).astype(BF16)


def project(arrived, own, weight, group):
    owners, held, width = arrived.shape
    rows = held - META
    depth, columns = weight.shape
    block = 1024
    return pl.pallas_call(
        functools.partial(project_kernel, group),
        out_shape=jax.ShapeDtypeStruct((rows // group, columns), BF16),
        grid=(columns // block,),
        in_specs=[
            pl.BlockSpec(arrived.shape, lambda j: (0, 0, 0)),
            pl.BlockSpec(own.shape, lambda j: (0, 0)),
            pl.BlockSpec((depth, block), lambda j: (0, j)),
        ],
        out_specs=pl.BlockSpec((rows // group, block), lambda j: (0, j)),
        scratch_shapes=[pltpu.VMEM((rows, width), F32), pltpu.VMEM((rows // group, depth), BF16)],
        compiler_params=pltpu.CompilerParams(vmem_limit_bytes=24 << 20),
        cost_estimate=pl.CostEstimate(flops=1 << 29, bytes_accessed=18 << 20, transcendentals=1 << 15),
        name="project",
    )(arrived, own, weight)


def local(
    queries, new_keys, new_values, ancestors, tile_keys, tile_values, tile_lengths, out_weight
):
    owners = lax.axis_size("owner")
    ranks = lax.axis_size("kvh")
    parts, new, group, width = queries.shape
    per_owner, size = tile_keys.shape[0], tile_keys.shape[2]
    tiles = per_owner * owners
    scale = width**-0.5 / math.log(2.0)
    share = parts * new // ranks
    piece = share // CHUNKS
    stretch = new // share
    split = queries.reshape(parts, stretch, CHUNKS, piece * group, width)

    member = jnp.any(ancestors[:, :, None] == jnp.arange(tiles, dtype=jnp.int32)[None, None, :], axis=1)
    meta = jnp.pad(member.astype(BF16), ((0, META - parts), (0, width - tiles)))

    arrived = []
    for c in range(CHUNKS):
        rows = split[:, :, c].reshape(-1, width)
        both = jnp.concatenate([rows, meta], axis=0)
        copies = jnp.broadcast_to(both, (owners, *both.shape))
        arrived.append(lax.all_to_all(copies, "owner", split_axis=0, concat_axis=0, tiled=True))

    slots = jnp.arange(size, dtype=jnp.int32)
    live = (slots[None, :] < tile_lengths[:, None])[:, :, None]
    keys = jnp.where(live, tile_keys[:, 0], tile_keys[:, 0, :1])
    values = jnp.concatenate(
        [jnp.where(live, tile_values[:, 0], jnp.zeros((), BF16)), jnp.broadcast_to(live, (per_owner, size, width)).astype(BF16)],
        axis=2,
    )
    widths = (tile_lengths + (STEP - 1)) // STEP

    held = arrived[0].shape[1] - META
    flags = arrived[0][:, held : held + parts, :tiles]
    mine = lax.axis_index("owner") * per_owner
    flags = lax.dynamic_slice_in_dim(flags, mine, per_owner, 2).astype(jnp.int32).reshape(-1)

    owns, backs = [], []
    for c in range(CHUNKS):
        q = split[:, :, c].reshape(parts, stretch * piece * group, width)

        def place(token, c=c):
            return (token // piece) * share + c * piece + token % piece

        owns.append(own_part(q, new_keys[:, :, 0], new_values[:, :, 0], scale, group, place))
    for c in range(CHUNKS):
        out = attend(arrived[c], keys, values, flags, widths, scale, parts)
        backs.append(lax.all_to_all(out, "owner", split_axis=0, concat_axis=0, tiled=True))
    sums = []
    for c in range(CHUNKS):
        mixed = project(backs[c], owns[c], out_weight, group)
        mixed = mixed.reshape(ranks, piece, -1)
        got = lax.all_to_all(mixed, "kvh", split_axis=0, concat_axis=0, tiled=True)
        sums.append(got.astype(F32).sum(axis=0).astype(BF16))
    return jnp.concatenate(sums, axis=0)


def solution(mesh):
    return jax.shard_map(
        local,
        mesh=mesh,
        in_specs=(
            P("owner", None, "kvh", None),
            P("owner", None, "kvh", None),
            P("owner", None, "kvh", None),
            P("owner", None),
            P("owner", "kvh", None, None),
            P("owner", "kvh", None, None),
            P("owner"),
            P("kvh", None),
        ),
        out_specs=P(("owner", "kvh"), None),
        check_vma=False,
    )
```

```python
import functools
import math

import jax
import jax.numpy as jnp
from jax import lax
from jax.experimental import pallas as pl
from jax.experimental.pallas import tpu as pltpu
from jax.sharding import PartitionSpec as P

NEG = -1e30
CHUNKS = 2
META = 16
STEP = 256
BATCH = 4
F32 = jnp.float32
BF16 = jnp.bfloat16


def to_lanes(column, count):
    r = lax.broadcasted_iota(jnp.int32, (128, 128), 0)
    c = lax.broadcasted_iota(jnp.int32, (128, 128), 1)
    eye = r == c
    rows = []
    for b in range(count // 128):
        rows.append(jnp.sum(jnp.where(eye, column[b * 128 : (b + 1) * 128], 0.0), axis=0, keepdims=True))
    return rows


def attend_kernel(scale, halves, batch, member, widths, q_ref, k_ref, v_ref, o_ref, s_ref, m_ref, acc_ref):
    homes = q_ref.shape[0]
    rows = q_ref.shape[1] - META
    tiles, width, size = k_ref.shape
    part = rows // halves
    count = batch * halves

    def blocks(b, t):
        return [(slice(i * part, (i + 1) * part), member[(b * count + i) * tiles + t] > 0) for i in range(count)]

    def for_each_tile(b, body):
        @pl.loop(0, tiles)
        def _(t):
            used = member[b * count * tiles + t]
            for i in range(1, count):
                used = used + member[(b * count + i) * tiles + t]
            steps = jnp.where(used > 0, widths[t], 0)
            for n in range(1, size // STEP + 1):

                @pl.when(steps == n)
                def _():
                    body(t, n * STEP)

    @pl.loop(0, homes // batch)
    def _(b):
        homes_here = pl.ds(b * batch, batch)
        m_ref[...] = jnp.full(m_ref.shape, NEG, F32)
        acc_ref[...] = jnp.zeros(acc_ref.shape, F32)

        def score(t, wide):
            q = q_ref[homes_here, :rows, :].reshape(batch * rows, width)
            s = jnp.dot(q, k_ref[t, :, :wide], preferred_element_type=F32)
            s_ref[t, :, :wide] = s
            for here, inside in blocks(b, t):
                x = s[here, :128]
                for j in range(128, wide, 128):
                    x = jnp.maximum(x, s[here, j : j + 128])
                m_ref[here, :] = jnp.maximum(m_ref[here, :], jnp.where(inside, x, NEG))

        for_each_tile(b, score)
        peak = jnp.max(m_ref[...], axis=1, keepdims=True) * scale
        m_ref[...] = jnp.broadcast_to(peak, m_ref.shape)

        def weigh(t, wide):
            weights = []
            for here, inside in blocks(b, t):
                shift = jnp.where(inside, m_ref[here, :], -NEG)
                weights.append(
                    jnp.concatenate(
                        [jnp.exp2(s_ref[t, here, j : j + 128] * scale - shift).astype(BF16) for j in range(0, wide, 128)],
                        axis=1,
                    )
                )
            acc_ref[...] += jnp.dot(jnp.concatenate(weights, axis=0), v_ref[t, :wide, :], preferred_element_type=F32)

        for_each_tile(b, weigh)
        pad = jnp.zeros((META - 3 * (rows // 128), 128), F32)
        for i in range(batch):
            here = slice(i * rows, (i + 1) * rows)
            total = acc_ref[here, width:]
            some = total > 0.0
            safe = jnp.where(some, total, 1.0)
            average = jnp.where(some, acc_ref[here, :width] / safe, 0.0)
            level = jnp.where(some, m_ref[here, :] + jnp.log(safe) * (1.0 / math.log(2.0)), NEG)
            pieces = []
            for row in to_lanes(level, rows):
                high = row.astype(BF16).astype(F32)
                mid = (row - high).astype(BF16).astype(F32)
                pieces += [high, mid, row - high - mid]
            o_ref[b * batch + i, :rows, :] = average.astype(BF16)
            o_ref[b * batch + i, rows:, :] = jnp.concatenate(pieces + [pad], axis=0).astype(BF16)


def attend(q, keys, values, member, widths, scale, halves):
    homes, held, width = q.shape
    tiles, _, size = keys.shape
    rows = held - META
    batch = math.gcd(homes, BATCH)
    vmem = pl.BlockSpec(memory_space=pltpu.VMEM)
    smem = pl.BlockSpec(memory_space=pltpu.SMEM)
    return pl.pallas_call(
        functools.partial(attend_kernel, scale, halves, batch),
        out_shape=jax.ShapeDtypeStruct(q.shape, BF16),
        in_specs=[smem, smem, vmem, vmem, vmem],
        out_specs=vmem,
        scratch_shapes=[
            pltpu.VMEM((tiles, batch * rows, size), F32),
            pltpu.VMEM((batch * rows, 128), F32),
            pltpu.VMEM((batch * rows, 2 * width), F32),
        ],
        compiler_params=pltpu.CompilerParams(vmem_limit_bytes=30 << 20),
        cost_estimate=pl.CostEstimate(flops=4 << 30, bytes_accessed=4 << 20, transcendentals=6 << 20),
        name="attend",
    )(member, widths, q, keys, values)


def prepare_kernel(scale, group, place, lengths, q_ref, nk_ref, nv_ref, k_ref, v_ref, kt_ref, va_ref, *own_refs):
    tiles, size, width = k_ref.shape

    @pl.loop(0, tiles)
    def _(t):
        live = lax.broadcasted_iota(jnp.int32, (size, width), 0) < lengths[t]
        k = k_ref[t].astype(F32)
        kt_ref[t] = jnp.where(live, k, k[:1]).T.astype(BF16)
        va_ref[t, :, :width] = jnp.where(live, v_ref[t].astype(F32), 0.0).astype(BF16)
        va_ref[t, :, width:] = live.astype(F32).astype(BF16)

    for c, o_ref in enumerate(own_refs):
        _, halves, part, _ = q_ref.shape
        new = nk_ref.shape[1]
        rows = halves * part
        for i in range(halves):
            s = lax.dot_general(q_ref[c, i], nk_ref[i], (((1,), (1,)), ((), ())), preferred_element_type=F32)
            row = lax.broadcasted_iota(jnp.int32, (part, new), 0) // group
            seen = place(row, c) >= lax.broadcasted_iota(jnp.int32, (part, new), 1)
            s = jnp.where(seen, s, NEG)
            peak = jnp.max(s, axis=1, keepdims=True)
            weights = jnp.where(seen, jnp.exp2((s - peak) * scale), 0.0)
            total = jnp.sum(weights, axis=1, keepdims=True)
            summed = jnp.dot(weights.astype(BF16), nv_ref[i], preferred_element_type=F32)
            o_ref[i * part : (i + 1) * part, :] = summed / total
            level = peak * scale + jnp.log(total) * (1.0 / math.log(2.0))
            rowed = to_lanes(jnp.broadcast_to(level, (part, width)), part)
            for b, line in enumerate(rowed):
                at = rows + i * len(rowed) + b
                o_ref[at : at + 1, :] = line


def prepare(lengths, q, new_keys, new_values, keys, values, scale, group, place):
    chunks, halves, part, width = q.shape
    tiles, size, _ = keys.shape
    vmem = pl.BlockSpec(memory_space=pltpu.VMEM)
    smem = pl.BlockSpec(memory_space=pltpu.SMEM)
    own = jax.ShapeDtypeStruct((halves * part + 8, width), F32)
    return pl.pallas_call(
        functools.partial(prepare_kernel, scale, group, place),
        out_shape=[
            jax.ShapeDtypeStruct((tiles, width, size), BF16),
            jax.ShapeDtypeStruct((tiles, size, 2 * width), BF16),
        ]
        + [own] * chunks,
        in_specs=[smem] + [vmem] * 5,
        out_specs=[vmem] * (2 + chunks),
        compiler_params=pltpu.CompilerParams(vmem_limit_bytes=12 << 20),
        cost_estimate=pl.CostEstimate(flops=1 << 24, bytes_accessed=16 << 20, transcendentals=1 << 15),
        name="prepare",
    )(lengths, q, new_keys, new_values, keys, values)


def merge(a_ref, own_ref, sum_ref):
    owners = a_ref.shape[0]
    rows = a_ref.shape[1] - META
    for b in range(rows // 128):
        lines = [own_ref[rows + b : rows + b + 1, :]]
        for o in range(owners):
            meta = a_ref[o, rows:, :].astype(F32)
            lines.append(meta[3 * b : 3 * b + 1] + meta[3 * b + 1 : 3 * b + 2] + meta[3 * b + 2 : 3 * b + 3])
        level = jnp.concatenate(lines + [jnp.full((128 - len(lines), 128), NEG, F32)], axis=0)
        top = jnp.max(level, axis=0, keepdims=True)
        weight = jnp.exp2(level - top)
        weight = weight / jnp.sum(weight, axis=0, keepdims=True)
        weight = weight.T
        here = slice(b * 128, (b + 1) * 128)
        acc = own_ref[here, :] * weight[:, 0:1]
        for o in range(owners):
            acc = acc + a_ref[o, here, :].astype(F32) * weight[:, o + 1 : o + 2]
        sum_ref[here, :] = acc


def combine_kernel(group, a_ref, own_ref, o_ref, sum_ref):
    rows, width = sum_ref.shape
    merge(a_ref, own_ref, sum_ref)
    for g in range(group):
        o_ref[:, g * width : (g + 1) * width] = sum_ref[pl.ds(g, rows // group, stride=group), :]


def combine(arrived, own, group):
    owners, held, width = arrived.shape
    rows = held - META
    vmem = pl.BlockSpec(memory_space=pltpu.VMEM)
    return pl.pallas_call(
        functools.partial(combine_kernel, group),
        out_shape=jax.ShapeDtypeStruct((rows // group, group * width), F32),
        in_specs=[vmem] * 2,
        out_specs=vmem,
        scratch_shapes=[pltpu.VMEM((rows, width), F32)],
        compiler_params=pltpu.CompilerParams(vmem_limit_bytes=8 << 20),
        cost_estimate=pl.CostEstimate(flops=1 << 22, bytes_accessed=2 << 20, transcendentals=1 << 14),
        name="combine",
    )(arrived, own)


def project_kernel(group, piece, *refs):
    earlier, (a_ref, own_ref, w_ref, o_ref, sum_ref, last_ref, flat_ref, held_ref, sems) = refs[:-9], refs[-9:]
    blocks, _, block = held_ref.shape
    copies = [
        pltpu.make_async_copy(w_ref.at[:, pl.ds(j * block, block)], held_ref.at[j], sems.at[j]) for j in range(blocks)
    ]
    for copy in copies:
        copy.start()
    rows, width = sum_ref.shape
    merge(a_ref, own_ref, sum_ref)
    for g in range(group):
        last_ref[:, g * width : (g + 1) * width] = sum_ref[pl.ds(g, rows // group, stride=group), :]
    pieces = [*earlier, last_ref]
    share = piece * len(pieces)
    for c, ref in enumerate(pieces):
        for k in range(ref.shape[0] // piece):
            flat_ref[k * share + c * piece : k * share + (c + 1) * piece, :] = ref[k * piece : (k + 1) * piece, :]
    flat = flat_ref[...].astype(BF16)
    for j, copy in enumerate(copies):
        copy.wait()
        o_ref[:, j * block : (j + 1) * block] = jnp.dot(flat, held_ref[j], preferred_element_type=F32).astype(BF16)


def project(earlier, arrived, own, weight, group, piece):
    owners, held, width = arrived.shape
    rows = held - META
    depth, columns = weight.shape
    tokens = rows // group
    block = 1024
    vmem = pl.BlockSpec(memory_space=pltpu.VMEM)
    return pl.pallas_call(
        functools.partial(project_kernel, group, piece),
        out_shape=jax.ShapeDtypeStruct((tokens * (len(earlier) + 1), columns), BF16),
        in_specs=[vmem] * (len(earlier) + 2) + [pl.BlockSpec(memory_space=pltpu.HBM)],
        out_specs=vmem,
        scratch_shapes=[
            pltpu.VMEM((rows, width), F32),
            pltpu.VMEM((tokens, depth), F32),
            pltpu.VMEM((tokens * (len(earlier) + 1), depth), F32),
            pltpu.VMEM((columns // block, depth, block), BF16),
            pltpu.SemaphoreType.DMA((columns // block,)),
        ],
        compiler_params=pltpu.CompilerParams(vmem_limit_bytes=32 << 20),
        cost_estimate=pl.CostEstimate(flops=1 << 30, bytes_accessed=18 << 20, transcendentals=1 << 14),
        name="project",
    )(*earlier, arrived, own, weight)


def local(
    queries, new_keys, new_values, ancestors, tile_keys, tile_values, tile_lengths, out_weight
):
    owners = lax.axis_size("owner")
    ranks = lax.axis_size("kvh")
    parts, new, group, width = queries.shape
    per_owner, size = tile_keys.shape[0], tile_keys.shape[2]
    tiles = per_owner * owners
    scale = width**-0.5 / math.log(2.0)
    share = parts * new // ranks
    piece = share // CHUNKS
    stretch = new // share
    split = queries.reshape(parts, stretch, CHUNKS, piece * group, width)

    member = jnp.any(ancestors[:, :, None] == jnp.arange(tiles, dtype=jnp.int32)[None, None, :], axis=1)
    meta = jnp.pad(member.astype(BF16), ((0, META - parts), (0, width - tiles)))

    def place(token, c):
        return (token // piece) * share + c * piece + token % piece

    def spread(c):
        both = jnp.concatenate([split[:, :, c].reshape(-1, width), meta], axis=0)
        copies = jnp.broadcast_to(both, (owners, *both.shape))
        return copies

    mine_q = jnp.moveaxis(split, 2, 0).reshape(CHUNKS, parts, stretch * piece * group, width)
    arrived = [lax.all_to_all(spread(0), "owner", split_axis=0, concat_axis=0, tiled=True)]
    keys, values, *owns = prepare(
        tile_lengths, mine_q, new_keys[:, :, 0], new_values[:, :, 0], tile_keys[:, 0], tile_values[:, 0], scale, group, place
    )
    for c in range(1, CHUNKS):
        copies, keys, values = lax.optimization_barrier((spread(c), keys, values))
        arrived.append(lax.all_to_all(copies, "owner", split_axis=0, concat_axis=0, tiled=True))
    widths = (tile_lengths + (STEP - 1)) // STEP

    held = arrived[0].shape[1] - META
    flags = arrived[0][:, held : held + parts, :tiles]
    mine = lax.axis_index("owner") * per_owner
    flags = lax.dynamic_slice_in_dim(flags, mine, per_owner, 2).astype(jnp.int32).reshape(-1)

    attention = []
    for c in range(CHUNKS):
        out = attend(arrived[c], keys, values, flags, widths, scale, parts)
        back = lax.all_to_all(out, "owner", split_axis=0, concat_axis=0, tiled=True)
        if c < CHUNKS - 1:
            attention.append(combine(back, owns[c], group))
    mixed = project(attention, back, owns[-1], out_weight, group, piece)
    mixed = mixed.reshape(ranks, share, -1)
    got = lax.all_to_all(mixed, "kvh", split_axis=0, concat_axis=0, tiled=True)
    return got.astype(F32).sum(axis=0).astype(BF16)


def solution(mesh):
    return jax.shard_map(
        local,
        mesh=mesh,
        in_specs=(
            P("owner", None, "kvh", None),
            P("owner", None, "kvh", None),
            P("owner", None, "kvh", None),
            P("owner", None),
            P("owner", "kvh", None, None),
            P("owner", "kvh", None, None),
            P("owner"),
            P("kvh", None),
        ),
        out_specs=P(("owner", "kvh"), None),
        check_vma=False,
    )
```

```python
import functools
import math

import jax
import jax.numpy as jnp
from jax import lax
from jax.experimental import pallas as pl
from jax.experimental.pallas import tpu as pltpu
from jax.sharding import PartitionSpec as P

NEG = -1e30
META = 16
STEP = 256
F32 = jnp.float32
BF16 = jnp.bfloat16
VMEM = pl.BlockSpec(memory_space=pltpu.VMEM)
SMEM = pl.BlockSpec(memory_space=pltpu.SMEM)
ANY = pl.BlockSpec(memory_space=pl.ANY)
LOG2 = 1.0 / math.log(2.0)


def to_lanes(column, count):
    r = lax.broadcasted_iota(jnp.int32, (128, 128), 0)
    c = lax.broadcasted_iota(jnp.int32, (128, 128), 1)
    eye = r == c
    rows = []
    for b in range(count // 128):
        rows.append(jnp.sum(jnp.where(eye, column[b * 128 : (b + 1) * 128], 0.0), axis=0, keepdims=True))
    return rows


def in_parts(lines):
    pieces = []
    for line in lines:
        high = line.astype(BF16).astype(F32)
        mid = (line - high).astype(BF16).astype(F32)
        pieces += [high, mid, line - high - mid]
    pad = jnp.zeros((META - len(pieces), 128), F32)
    return jnp.concatenate(pieces + [pad], axis=0).astype(BF16)


def levels(meta, b):
    return meta[3 * b : 3 * b + 1] + meta[3 * b + 1 : 3 * b + 2] + meta[3 * b + 2 : 3 * b + 3]


def prepare_kernel(scale, group, lengths, q_ref, nk_ref, nv_ref, k_ref, v_ref, kt_ref, va_ref, o_ref):
    tiles, size, width = k_ref.shape

    @pl.loop(0, tiles)
    def _(t):
        live = lax.broadcasted_iota(jnp.int32, (size, width), 0) < lengths[t]
        k = k_ref[t].astype(F32)
        kt_ref[t] = jnp.where(live, k, k[:1]).T.astype(BF16)
        va_ref[t, :, :width] = jnp.where(live, v_ref[t].astype(F32), 0.0).astype(BF16)
        va_ref[t, :, width:] = live.astype(F32).astype(BF16)

    halves, part, _ = q_ref.shape
    new = nk_ref.shape[1]
    rows = halves * part
    for i in range(halves):
        s = lax.dot_general(q_ref[i], nk_ref[i], (((1,), (1,)), ((), ())), preferred_element_type=F32)
        token = lax.broadcasted_iota(jnp.int32, (part, new), 0) // group
        seen = token >= lax.broadcasted_iota(jnp.int32, (part, new), 1)
        s = jnp.where(seen, s, NEG)
        peak = jnp.max(s, axis=1, keepdims=True)
        weights = jnp.where(seen, jnp.exp2((s - peak) * scale), 0.0)
        total = jnp.sum(weights, axis=1, keepdims=True)
        summed = jnp.dot(weights.astype(BF16), nv_ref[i], preferred_element_type=F32)
        o_ref[i * part : (i + 1) * part, :] = summed / total
        level = peak * scale + jnp.log(total) * LOG2
        rowed = to_lanes(jnp.broadcast_to(level, (part, width)), part)
        for b, line in enumerate(rowed):
            at = rows + i * len(rowed) + b
            o_ref[at : at + 1, :] = line


def prepare(lengths, q, new_keys, new_values, keys, values, scale, group):
    halves, part, width = q.shape
    tiles, size, _ = keys.shape
    return pl.pallas_call(
        functools.partial(prepare_kernel, scale, group),
        out_shape=[
            jax.ShapeDtypeStruct((tiles, width, size), BF16),
            jax.ShapeDtypeStruct((tiles, size, 2 * width), BF16),
            jax.ShapeDtypeStruct((halves * part + 8, width), F32),
        ],
        in_specs=[SMEM] + [VMEM] * 5,
        out_specs=[VMEM] * 3,
        compiler_params=pltpu.CompilerParams(vmem_limit_bytes=44 << 20),
        cost_estimate=pl.CostEstimate(flops=1 << 24, bytes_accessed=16 << 20, transcendentals=1 << 15),
        name="prepare",
    )(lengths, q, new_keys, new_values, keys, values)


def attend_kernel(
    scale, halves, facts, q_any, k_any, v_any, o_ref, q_ref, k_ref, v_ref, s_ref, m_ref, acc_ref, flag_ref, member, q_sem, k_sem, v_sem, f_sem
):
    homes, held, width = q_ref.shape
    rows = held - META
    tiles, _, size = k_ref.shape
    part = rows // halves
    count = homes * halves

    q_copy = pltpu.make_async_copy(q_any, q_ref, q_sem)
    q_copy.start()

    def k_copy(t):
        return pltpu.make_async_copy(k_any.at[t], k_ref.at[t], k_sem.at[t])

    def v_copy(t):
        return pltpu.make_async_copy(v_any.at[t], v_ref.at[t], v_sem.at[t])

    for t in range(tiles):
        k_copy(t).start()
    for t in range(tiles):
        v_copy(t).start()
    q_copy.wait()
    for h in range(homes):
        flag_ref[h * halves : (h + 1) * halves, :] = q_ref[h, rows:, :].astype(F32)[:halves].astype(jnp.int32)
    f_copy = pltpu.make_async_copy(flag_ref, member, f_sem)
    f_copy.start()
    m_ref[...] = jnp.full(m_ref.shape, NEG, F32)
    acc_ref[...] = jnp.zeros(acc_ref.shape, F32)
    f_copy.wait()
    first = facts[tiles]

    def blocks(t):
        return [(slice(i * part, (i + 1) * part), member[i, first + t] > 0) for i in range(count)]

    def for_each_tile(copy, body):
        @pl.loop(0, tiles)
        def _(t):
            copy(t).wait()
            used = member[0, first + t]
            for i in range(1, count):
                used = used + member[i, first + t]
            steps = jnp.where(used > 0, (facts[t] + (STEP - 1)) // STEP, 0)
            for n in range(1, size // STEP + 1):

                @pl.when(steps == n)
                def _():
                    body(t, n * STEP)

    def score(t, wide):
        q = q_ref[:, :rows, :].reshape(homes * rows, width)
        s = jnp.dot(q, k_ref[t, :, :wide], preferred_element_type=F32)
        s_ref[t, :, :wide] = s
        for here, inside in blocks(t):
            x = s[here, :128]
            for j in range(128, wide, 128):
                x = jnp.maximum(x, s[here, j : j + 128])
            m_ref[here, :] = jnp.maximum(m_ref[here, :], jnp.where(inside, x, NEG))

    for_each_tile(k_copy, score)
    peak = jnp.max(m_ref[...], axis=1, keepdims=True) * scale
    m_ref[...] = jnp.broadcast_to(peak, m_ref.shape)

    def weigh(t, wide):
        weights = []
        for here, inside in blocks(t):
            shift = jnp.where(inside, m_ref[here, :], -NEG)
            weights.append(
                jnp.concatenate(
                    [jnp.exp2(s_ref[t, here, j : j + 128] * scale - shift).astype(BF16) for j in range(0, wide, 128)],
                    axis=1,
                )
            )
        acc_ref[...] += jnp.dot(jnp.concatenate(weights, axis=0), v_ref[t, :wide, :], preferred_element_type=F32)

    for_each_tile(v_copy, weigh)
    for h in range(homes):
        here = slice(h * rows, (h + 1) * rows)
        total = acc_ref[here, width:]
        some = total > 0.0
        safe = jnp.where(some, total, 1.0)
        average = jnp.where(some, acc_ref[here, :width] / safe, 0.0)
        level = jnp.where(some, m_ref[here, :] + jnp.log(safe) * LOG2, NEG)
        o_ref[h, :rows, :] = average.astype(BF16)
        o_ref[h, rows:, :] = in_parts(to_lanes(level, rows))


def attend(q, keys, values, facts, scale, halves):
    homes, held, width = q.shape
    tiles, _, size = keys.shape
    rows = held - META
    return pl.pallas_call(
        functools.partial(attend_kernel, scale, halves),
        out_shape=jax.ShapeDtypeStruct(q.shape, BF16),
        in_specs=[SMEM, ANY, ANY, ANY],
        out_specs=VMEM,
        scratch_shapes=[
            pltpu.VMEM(q.shape, BF16),
            pltpu.VMEM(keys.shape, BF16),
            pltpu.VMEM(values.shape, BF16),
            pltpu.VMEM((tiles, homes * rows, size), F32),
            pltpu.VMEM((homes * rows, 128), F32),
            pltpu.VMEM((homes * rows, 2 * width), F32),
            pltpu.VMEM((homes * halves, 128), jnp.int32),
            pltpu.SMEM((homes * halves, 128), jnp.int32),
            pltpu.SemaphoreType.DMA,
            pltpu.SemaphoreType.DMA((tiles,)),
            pltpu.SemaphoreType.DMA((tiles,)),
            pltpu.SemaphoreType.DMA,
        ],
        compiler_params=pltpu.CompilerParams(vmem_limit_bytes=44 << 20),
        cost_estimate=pl.CostEstimate(flops=4 << 30, bytes_accessed=4 << 20, transcendentals=6 << 20),
        name="attend",
    )(facts, q, keys, values)


def weights_of(lines):
    level = jnp.concatenate(lines + [jnp.full((128 - len(lines), 128), 2 * NEG, F32)], axis=0)
    top = jnp.max(level, axis=0, keepdims=True)
    weight = jnp.exp2(level - top)
    total = jnp.sum(weight, axis=0, keepdims=True)
    return (weight / total).T, top + jnp.log(total) * LOG2


def merge_kernel(*refs):
    count = len(refs) // 2
    a_refs, o_refs = refs[:count], refs[count:]
    homes, held, _ = a_refs[0].shape
    rows = held - META
    for h in range(homes):
        metas = [a[h, rows:, :].astype(F32) for a in a_refs]
        lines = []
        for b in range(rows // 128):
            weight, line = weights_of([levels(meta, b) for meta in metas])
            lines.append(line)
            here = slice(b * 128, (b + 1) * 128)
            acc = a_refs[0][h, here, :].astype(F32) * weight[:, 0:1]
            for i in range(1, count):
                acc = acc + a_refs[i][h, here, :].astype(F32) * weight[:, i : i + 1]
            o_refs[h][here, :] = acc.astype(BF16)
        o_refs[h][rows:, :] = in_parts(lines)


def merge(parts):
    homes, held, width = parts[0].shape
    return pl.pallas_call(
        merge_kernel,
        out_shape=[jax.ShapeDtypeStruct((held, width), BF16)] * homes,
        in_specs=[VMEM] * len(parts),
        out_specs=[VMEM] * homes,
        compiler_params=pltpu.CompilerParams(vmem_limit_bytes=44 << 20),
        cost_estimate=pl.CostEstimate(flops=1 << 24, bytes_accessed=4 << 20, transcendentals=1 << 14),
        name="merge",
    )(*parts)


def project_kernel(group, ranks, cores, rank, *refs):
    a_refs, (own_ref, w_ref, keep_ref, give_ref, sum_ref, all_ref, flat_ref, held_ref, sems) = refs[:-9], refs[-9:]
    blocks, _, block = held_ref.shape
    copies = [
        pltpu.make_async_copy(w_ref.at[:, pl.ds(j * block, block)], held_ref.at[j], sems.at[j]) for j in range(blocks)
    ]
    for copy in copies:
        copy.start()
    rows, width = sum_ref.shape
    metas = [a[rows:, :].astype(F32) for a in a_refs]
    for b in range(rows // 128):
        weight, _ = weights_of([own_ref[rows + b : rows + b + 1, :]] + [levels(meta, b) for meta in metas])
        here = slice(b * 128, (b + 1) * 128)
        acc = own_ref[here, :] * weight[:, 0:1]
        for i, a in enumerate(a_refs):
            acc = acc + a[here, :].astype(F32) * weight[:, i + 1 : i + 2]
        sum_ref[here, :] = acc
    tokens = rows // group
    for g in range(group):
        all_ref[:, g * width : (g + 1) * width] = sum_ref[pl.ds(g, tokens, stride=group), :]
    chips = ranks // cores
    share = tokens // ranks
    chip, core = rank[0] // cores, rank[0] % cores
    for i in range(cores):
        for d in range(chips):
            to = ((chip + d) % chips) * cores + (core + i) % cores
            at = (i * chips + d) * share
            flat_ref[at : at + share, :] = all_ref[pl.ds(pl.multiple_of(to * share, share), share), :]
    flat = flat_ref[...].astype(BF16)
    half = tokens // cores
    for j, copy in enumerate(copies):
        copy.wait()
        out = jnp.dot(flat, held_ref[j], preferred_element_type=F32).astype(BF16)
        keep_ref[:, j * block : (j + 1) * block] = out[:half]
        give_ref[:, j * block : (j + 1) * block] = out[half:]


def project(parts, own, weight, rank, group, ranks, cores):
    held, width = parts[0].shape
    rows = held - META
    depth, columns = weight.shape
    tokens = rows // group
    block = 1024
    return pl.pallas_call(
        functools.partial(project_kernel, group, ranks, cores),
        out_shape=[jax.ShapeDtypeStruct((tokens // cores, columns), BF16)] * 2,
        in_specs=[SMEM] + [VMEM] * (len(parts) + 1) + [ANY],
        out_specs=[VMEM] * 2,
        scratch_shapes=[
            pltpu.VMEM((rows, width), F32),
            pltpu.VMEM((tokens, depth), F32),
            pltpu.VMEM((tokens, depth), F32),
            pltpu.VMEM((columns // block, depth, block), BF16),
            pltpu.SemaphoreType.DMA((columns // block,)),
        ],
        compiler_params=pltpu.CompilerParams(vmem_limit_bytes=54 << 20),
        cost_estimate=pl.CostEstimate(flops=1 << 30, bytes_accessed=18 << 20, transcendentals=1 << 14),
        name="project",
    )(rank, *parts, own, weight)


def local(
    queries, new_keys, new_values, ancestors, tile_keys, tile_values, tile_lengths, out_weight
):
    owners = lax.axis_size("owner")
    ranks = lax.axis_size("kvh")
    cores = 2
    chips = ranks // cores
    side = math.isqrt(owners)
    parts, new, group, width = queries.shape
    per_owner = tile_keys.shape[0]
    tiles = per_owner * owners
    scale = width**-0.5 * LOG2
    rows = parts * new * group

    def along_z(x, d):
        return lax.ppermute(x, "owner", [(o, o // side * side + (o + d) % side) for o in range(owners)])

    def along_y(x, e):
        return lax.ppermute(x, "owner", [(o, (o + e * side) % owners) for o in range(owners)])

    member = jnp.any(ancestors[:, :, None] == jnp.arange(tiles, dtype=jnp.int32)[None, None, :], axis=1)
    meta = jnp.pad(member.astype(BF16), ((0, META - parts), (0, width - tiles)))
    home = jnp.concatenate([queries.reshape(rows, width), meta], axis=0)
    mine = (lax.axis_index("owner") * per_owner).astype(jnp.int32)
    facts = jnp.concatenate([tile_lengths, mine[None]])
    rank = lax.axis_index("kvh").astype(jnp.int32)[None]

    near = [along_z(home, d) for d in range(1, side)]
    keys, values, own = prepare(
        tile_lengths,
        queries.reshape(parts, new * group, width),
        new_keys[:, :, 0],
        new_values[:, :, 0],
        tile_keys[:, 0],
        tile_values[:, 0],
        scale,
        group,
    )
    row, keys, values = lax.optimization_barrier((jnp.stack([home] + near), keys, values))
    order = sorted(range(side), key=lambda e: min(e, side - e))
    blocks = {e: along_y(row, e) if e else row for e in order}
    back = []
    for e in order:
        block = blocks[e]
        if e:
            block, out = lax.optimization_barrier((block, out))
        out = attend(block, keys, values, facts, scale, parts)
        back.append(along_y(out, -e) if e else out)
    merged = merge(back)
    final = [along_z(merged[d], -d) if d else merged[d] for d in range(side)]
    keep, give = project(final, own, out_weight, rank, group, ranks, cores)
    got = lax.ppermute(give, "kvh", [(k, k // cores * cores + (k + 1) % cores) for k in range(ranks)])
    both = keep.astype(F32) + got.astype(F32)
    share = both.shape[0] // chips
    result = both[:share]
    for d in range(1, chips):
        some = both[d * share : (d + 1) * share].astype(BF16)
        result = result + lax.ppermute(some, "kvh", [(k, (k + d * cores) % ranks) for k in range(ranks)]).astype(F32)
    return result.astype(BF16)


def solution(mesh):
    return jax.shard_map(
        local,
        mesh=mesh,
        in_specs=(
            P("owner", None, "kvh", None),
            P("owner", None, "kvh", None),
            P("owner", None, "kvh", None),
            P("owner", None),
            P("owner", "kvh", None, None),
            P("owner", "kvh", None, None),
            P("owner"),
            P("kvh", None),
        ),
        out_specs=P(("owner", "kvh"), None),
        check_vma=False,
    )
```

```python
import functools
import math

import jax
import jax.numpy as jnp
from jax import lax
from jax.experimental import pallas as pl
from jax.experimental.pallas import tpu as pltpu
from jax.sharding import PartitionSpec as P

NEG = -1e30
META = 16
STEP = 256
F32 = jnp.float32
BF16 = jnp.bfloat16
VMEM = pl.BlockSpec(memory_space=pltpu.VMEM)
SMEM = pl.BlockSpec(memory_space=pltpu.SMEM)
ANY = pl.BlockSpec(memory_space=pl.ANY)
LOG2 = 1.0 / math.log(2.0)


def to_lanes(column, count):
    r = lax.broadcasted_iota(jnp.int32, (128, 128), 0)
    c = lax.broadcasted_iota(jnp.int32, (128, 128), 1)
    eye = r == c
    rows = []
    for b in range(count // 128):
        rows.append(jnp.sum(jnp.where(eye, column[b * 128 : (b + 1) * 128], 0.0), axis=0, keepdims=True))
    return rows


def in_parts(lines):
    pieces = []
    for line in lines:
        high = line.astype(BF16).astype(F32)
        mid = (line - high).astype(BF16).astype(F32)
        pieces += [high, mid, line - high - mid]
    pad = jnp.zeros((META - len(pieces), 128), F32)
    return jnp.concatenate(pieces + [pad], axis=0).astype(BF16)


def levels(meta, b):
    return meta[3 * b : 3 * b + 1] + meta[3 * b + 1 : 3 * b + 2] + meta[3 * b + 2 : 3 * b + 3]


def prepare_kernel(scale, group, lengths, *refs):
    given, (kt_ref, va_ref, o_ref), held, sems = refs[:5], refs[5:8], refs[8:13], refs[13:]
    copies = [pltpu.make_async_copy(a, b, sem) for a, b, sem in zip(given, held, sems)]
    for copy in copies:
        copy.start()
    q_ref, nk_ref, nv_ref, k_ref, v_ref = held
    tiles, size, width = k_ref.shape
    for copy in copies:
        copy.wait()

    @pl.loop(0, tiles)
    def _(t):
        live = lax.broadcasted_iota(jnp.int32, (size, width), 0) < lengths[t]
        k = k_ref[t].astype(F32)
        kt_ref[t] = jnp.where(live, k, k[:1]).T.astype(BF16)
        va_ref[t, :, :width] = jnp.where(live, v_ref[t].astype(F32), 0.0).astype(BF16)
        va_ref[t, :, width:] = live.astype(F32).astype(BF16)

    halves, part, _ = q_ref.shape
    new = nk_ref.shape[1]
    rows = halves * part
    for i in range(halves):
        s = lax.dot_general(q_ref[i], nk_ref[i], (((1,), (1,)), ((), ())), preferred_element_type=F32)
        token = lax.broadcasted_iota(jnp.int32, (part, new), 0) // group
        seen = token >= lax.broadcasted_iota(jnp.int32, (part, new), 1)
        s = jnp.where(seen, s, NEG)
        peak = jnp.max(s, axis=1, keepdims=True)
        weights = jnp.where(seen, jnp.exp2((s - peak) * scale), 0.0)
        total = jnp.sum(weights, axis=1, keepdims=True)
        summed = jnp.dot(weights.astype(BF16), nv_ref[i], preferred_element_type=F32)
        o_ref[i * part : (i + 1) * part, :] = summed / total
        level = peak * scale + jnp.log(total) * LOG2
        rowed = to_lanes(jnp.broadcast_to(level, (part, width)), part)
        for b, line in enumerate(rowed):
            at = rows + i * len(rowed) + b
            o_ref[at : at + 1, :] = line


def prepare(lengths, q, new_keys, new_values, keys, values, scale, group):
    halves, part, width = q.shape
    tiles, size, _ = keys.shape
    return pl.pallas_call(
        functools.partial(prepare_kernel, scale, group),
        out_shape=[
            jax.ShapeDtypeStruct((tiles, width, size), BF16),
            jax.ShapeDtypeStruct((tiles, size, 2 * width), BF16),
            jax.ShapeDtypeStruct((halves * part + 8, width), F32),
        ],
        in_specs=[SMEM] + [ANY] * 5,
        out_specs=[VMEM] * 3,
        scratch_shapes=[pltpu.VMEM(a.shape, BF16) for a in (q, new_keys, new_values, keys, values)]
        + [pltpu.SemaphoreType.DMA] * 5,
        compiler_params=pltpu.CompilerParams(vmem_limit_bytes=44 << 20),
        cost_estimate=pl.CostEstimate(flops=1 << 24, bytes_accessed=16 << 20, transcendentals=1 << 15),
        name="prepare",
    )(lengths, q, new_keys, new_values, keys, values)


def attend_kernel(
    scale, halves, lengths, q_ref, k_ref, v_ref, o_ref, s_ref, m_ref, acc_ref, flag_ref, member, f_sem
):
    homes, held, width = q_ref.shape
    rows = held - META
    tiles, _, size = k_ref.shape
    part = rows // halves
    count = homes * halves

    for h in range(homes):
        flag_ref[h * halves : (h + 1) * halves, :] = q_ref[h, rows:, :].astype(F32)[:halves].astype(jnp.int32)
    f_copy = pltpu.make_async_copy(flag_ref, member, f_sem)
    f_copy.start()
    m_ref[...] = jnp.full(m_ref.shape, NEG, F32)
    acc_ref[...] = jnp.zeros(acc_ref.shape, F32)
    f_copy.wait()
    first = lax.axis_index("owner") * tiles

    def blocks(t):
        return [(slice(i * part, (i + 1) * part), member[i, first + t] > 0) for i in range(count)]

    def for_each_tile(body):
        @pl.loop(0, tiles)
        def _(t):
            used = member[0, first + t]
            for i in range(1, count):
                used = used + member[i, first + t]
            steps = jnp.where(used > 0, (lengths[t] + (STEP - 1)) // STEP, 0)
            for n in range(1, size // STEP + 1):

                @pl.when(steps == n)
                def _():
                    body(t, n * STEP)

    def score(t, wide):
        q = q_ref[:, :rows, :].reshape(homes * rows, width)
        s = jnp.dot(q, k_ref[t, :, :wide], preferred_element_type=F32)
        s_ref[t, :, :wide] = s
        for here, inside in blocks(t):
            x = s[here, :128]
            for j in range(128, wide, 128):
                x = jnp.maximum(x, s[here, j : j + 128])
            m_ref[here, :] = jnp.maximum(m_ref[here, :], jnp.where(inside, x, NEG))

    for_each_tile(score)
    peak = jnp.max(m_ref[...], axis=1, keepdims=True) * scale
    m_ref[...] = jnp.broadcast_to(peak, m_ref.shape)

    def weigh(t, wide):
        weights = []
        for here, inside in blocks(t):
            shift = jnp.where(inside, m_ref[here, :], -NEG)
            weights.append(
                jnp.concatenate(
                    [jnp.exp2(s_ref[t, here, j : j + 128] * scale - shift).astype(BF16) for j in range(0, wide, 128)],
                    axis=1,
                )
            )
        acc_ref[...] += jnp.dot(jnp.concatenate(weights, axis=0), v_ref[t, :wide, :], preferred_element_type=F32)

    for_each_tile(weigh)
    for h in range(homes):
        here = slice(h * rows, (h + 1) * rows)
        total = acc_ref[here, width:]
        o_ref[h, :rows, :] = (acc_ref[here, :width] / jnp.maximum(total, -1.0 / NEG)).astype(BF16)
        sums = jnp.concatenate(to_lanes(total, rows), axis=0)
        peaks = jnp.concatenate(to_lanes(m_ref[here, :], rows), axis=0)
        level = jnp.where(sums > 0.0, peaks + jnp.log(jnp.maximum(sums, -1.0 / NEG)) * LOG2, NEG)
        o_ref[h, rows:, :] = in_parts([level[b : b + 1] for b in range(rows // 128)])


def attend(q, keys, values, lengths, scale, halves):
    homes, held, width = q.shape
    tiles, _, size = keys.shape
    rows = held - META
    return pl.pallas_call(
        functools.partial(attend_kernel, scale, halves),
        out_shape=jax.ShapeDtypeStruct(q.shape, BF16),
        in_specs=[SMEM, VMEM, VMEM, VMEM],
        out_specs=VMEM,
        scratch_shapes=[
            pltpu.VMEM((tiles, homes * rows, size), F32),
            pltpu.VMEM((homes * rows, 128), F32),
            pltpu.VMEM((homes * rows, 2 * width), F32),
            pltpu.VMEM((homes * halves, 128), jnp.int32),
            pltpu.SMEM((homes * halves, 128), jnp.int32),
            pltpu.SemaphoreType.DMA,
        ],
        compiler_params=pltpu.CompilerParams(vmem_limit_bytes=44 << 20),
        cost_estimate=pl.CostEstimate(flops=1 << 30, bytes_accessed=1 << 20, transcendentals=1 << 18),
        name="attend",
    )(lengths, q, keys, values)


def weights_of(lines):
    level = jnp.concatenate(lines + [jnp.full((128 - len(lines), 128), 2 * NEG, F32)], axis=0)
    top = jnp.max(level, axis=0, keepdims=True)
    weight = jnp.exp2(level - top)
    total = jnp.sum(weight, axis=0, keepdims=True)
    return (weight / total).T, top + jnp.log(total) * LOG2


def merge_kernel(*refs):
    a_refs, o_refs = refs[:2], refs[2:]
    count = len(a_refs)
    homes, held, _ = a_refs[0].shape
    if len(o_refs) == 1:
        o_refs = [o_refs[0].at[h] for h in range(homes)]
    rows = held - META
    for h in range(homes):
        metas = [a[h, rows:, :].astype(F32) for a in a_refs]
        lines = []
        for b in range(rows // 128):
            weight, line = weights_of([levels(meta, b) for meta in metas])
            lines.append(line)
            here = slice(b * 128, (b + 1) * 128)
            acc = a_refs[0][h, here, :].astype(F32) * weight[:, 0:1]
            for i in range(1, count):
                acc = acc + a_refs[i][h, here, :].astype(F32) * weight[:, i : i + 1]
            o_refs[h][here, :] = acc.astype(BF16)
        o_refs[h][rows:, :] = in_parts(lines)


def merge(one, two, apart):
    homes, held, width = one.shape
    out = [jax.ShapeDtypeStruct((held, width), BF16)] * homes if apart else jax.ShapeDtypeStruct(one.shape, BF16)
    return pl.pallas_call(
        merge_kernel,
        out_shape=out,
        in_specs=[VMEM] * 2,
        out_specs=[VMEM] * homes if apart else VMEM,
        compiler_params=pltpu.CompilerParams(vmem_limit_bytes=16 << 20),
        cost_estimate=pl.CostEstimate(flops=1 << 34, bytes_accessed=4 << 20, transcendentals=1 << 14),
        name="merge",
    )(one, two)


def project_kernel(group, ranks, cores, *refs):
    a_refs, (own_ref, w_ref, keep_ref, give_ref, sum_ref, all_ref, flat_ref, held_ref, sems) = refs[:-9], refs[-9:]
    blocks, _, block = held_ref.shape
    copies = [
        pltpu.make_async_copy(w_ref.at[:, pl.ds(j * block, block)], held_ref.at[j], sems.at[j]) for j in range(blocks)
    ]
    for copy in copies:
        copy.start()
    rows, width = sum_ref.shape
    metas = [a[rows:, :].astype(F32) for a in a_refs]
    for b in range(rows // 128):
        weight, _ = weights_of([own_ref[rows + b : rows + b + 1, :]] + [levels(meta, b) for meta in metas])
        here = slice(b * 128, (b + 1) * 128)
        acc = own_ref[here, :] * weight[:, 0:1]
        for i, a in enumerate(a_refs):
            acc = acc + a[here, :].astype(F32) * weight[:, i + 1 : i + 2]
        sum_ref[here, :] = acc
    tokens = rows // group
    for g in range(group):
        all_ref[:, g * width : (g + 1) * width] = sum_ref[pl.ds(g, tokens, stride=group), :]
    chips = ranks // cores
    share = tokens // ranks
    rank = lax.axis_index("kvh")
    chip, core = rank // cores, rank % cores
    for i in range(cores):
        for d in range(chips):
            to = ((chip + d) % chips) * cores + (core + i) % cores
            at = (i * chips + d) * share
            flat_ref[at : at + share, :] = all_ref[pl.ds(pl.multiple_of(to * share, share), share), :]
    flat = flat_ref[...].astype(BF16)
    half = tokens // cores
    for j, copy in enumerate(copies):
        copy.wait()
        out = jnp.dot(flat, held_ref[j], preferred_element_type=F32).astype(BF16)
        keep_ref[:, j * block : (j + 1) * block] = out[:half]
        give_ref[:, j * block : (j + 1) * block] = out[half:]


def project(parts, own, weight, group, ranks, cores):
    held, width = parts[0].shape
    rows = held - META
    depth, columns = weight.shape
    tokens = rows // group
    block = 1024
    return pl.pallas_call(
        functools.partial(project_kernel, group, ranks, cores),
        out_shape=[jax.ShapeDtypeStruct((tokens // cores, columns), BF16)] * 2,
        in_specs=[VMEM] * (len(parts) + 1) + [ANY],
        out_specs=[VMEM] * 2,
        scratch_shapes=[
            pltpu.VMEM((rows, width), F32),
            pltpu.VMEM((tokens, depth), F32),
            pltpu.VMEM((tokens, depth), F32),
            pltpu.VMEM((columns // block, depth, block), BF16),
            pltpu.SemaphoreType.DMA((columns // block,)),
        ],
        compiler_params=pltpu.CompilerParams(vmem_limit_bytes=54 << 20),
        cost_estimate=pl.CostEstimate(flops=1 << 30, bytes_accessed=18 << 20, transcendentals=1 << 14),
        name="project",
    )(*parts, own, weight)


def local(
    queries, new_keys, new_values, ancestors, tile_keys, tile_values, tile_lengths, out_weight
):
    owners = lax.axis_size("owner")
    ranks = lax.axis_size("kvh")
    cores = 2
    chips = ranks // cores
    side = math.isqrt(owners)
    parts, new, group, width = queries.shape
    per_owner = tile_keys.shape[0]
    tiles = per_owner * owners
    scale = width**-0.5 * LOG2
    rows = parts * new * group

    def along(x, leg, step):
        pairs = []
        for o in range(owners):
            y, z = divmod(o, side)
            for k in range(ranks):
                if (k % cores + leg) % 2 == 0:
                    to = y * side + (z + step) % side
                else:
                    to = (y + step) % side * side + z
                pairs.append((o * ranks + k, to * ranks + k))
        return lax.ppermute(x, ("owner", "kvh"), pairs)

    member = jnp.any(ancestors[:, :, None] == jnp.arange(tiles, dtype=jnp.int32)[None, None, :], axis=1)
    meta = jnp.pad(member.astype(BF16), ((0, META - parts), (0, width - tiles)))
    home = jnp.concatenate([queries.reshape(rows, width), meta], axis=0)
    near = [along(home, 0, d) for d in range(1, side)]
    keys, values, own = prepare(
        tile_lengths,
        queries.reshape(parts, new * group, width),
        new_keys[:, :, 0],
        new_values[:, :, 0],
        tile_keys[:, 0],
        tile_values[:, 0],
        scale,
        group,
    )
    row, keys, values = lax.optimization_barrier((jnp.stack([home] + near), keys, values))
    order = sorted(range(side), key=lambda e: min(e, side - e))
    blocks = {e: along(row, 1, e) if e else row for e in order}
    back = []
    for e in order:
        block = blocks[e]
        if e:
            block, out = lax.optimization_barrier((block, out))
        out = attend(block, keys, values, tile_lengths, scale, parts)
        back.append(along(out, 1, -e) if e else out)
    merged = back[0]
    for i in range(1, side):
        merged = merge(merged, back[i], i == side - 1)
    final = [along(merged[d], 0, -d) if d else merged[d] for d in range(side)]
    keep, give = project(final, own, out_weight, group, ranks, cores)
    got = lax.ppermute(give, "kvh", [(k, k // cores * cores + (k + 1) % cores) for k in range(ranks)])
    both = keep.astype(F32) + got.astype(F32)
    share = both.shape[0] // chips
    result = both[:share]
    for d in range(1, chips):
        some = both[d * share : (d + 1) * share].astype(BF16)
        result = result + lax.ppermute(some, "kvh", [(k, (k + d * cores) % ranks) for k in range(ranks)]).astype(F32)
    return result.astype(BF16)


def solution(mesh):
    return jax.shard_map(
        local,
        mesh=mesh,
        in_specs=(
            P("owner", None, "kvh", None),
            P("owner", None, "kvh", None),
            P("owner", None, "kvh", None),
            P("owner", None),
            P("owner", "kvh", None, None),
            P("owner", "kvh", None, None),
            P("owner"),
            P("kvh", None),
        ),
        out_specs=P(("owner", "kvh"), None),
        check_vma=False,
    )
```

```python
import functools
import math

import jax
import jax.numpy as jnp
from jax import lax
from jax.experimental import pallas as pl
from jax.experimental.pallas import tpu as pltpu
from jax.sharding import PartitionSpec as P

NEG = -1e30
META = 16
STEP = 256
F32 = jnp.float32
BF16 = jnp.bfloat16
VMEM = pl.BlockSpec(memory_space=pltpu.VMEM)
SMEM = pl.BlockSpec(memory_space=pltpu.SMEM)
ANY = pl.BlockSpec(memory_space=pl.ANY)
LOG2 = 1.0 / math.log(2.0)


def to_lanes(column, count):
    r = lax.broadcasted_iota(jnp.int32, (128, 128), 0)
    c = lax.broadcasted_iota(jnp.int32, (128, 128), 1)
    eye = r == c
    rows = []
    for b in range(count // 128):
        rows.append(jnp.sum(jnp.where(eye, column[b * 128 : (b + 1) * 128], 0.0), axis=0, keepdims=True))
    return rows


def in_parts(lines):
    pieces = []
    for line in lines:
        high = line.astype(BF16).astype(F32)
        mid = (line - high).astype(BF16).astype(F32)
        pieces += [high, mid, line - high - mid]
    pad = jnp.zeros((META - len(pieces), 128), F32)
    return jnp.concatenate(pieces + [pad], axis=0).astype(BF16)


def levels(meta, b):
    return meta[3 * b : 3 * b + 1] + meta[3 * b + 1 : 3 * b + 2] + meta[3 * b + 2 : 3 * b + 3]


def prepare_kernel(scale, group, lengths, *refs):
    given, (kt_ref, va_ref, o_ref), held, sems = refs[:5], refs[5:8], refs[8:13], refs[13:]
    copies = [pltpu.make_async_copy(a, b, sem) for a, b, sem in zip(given, held, sems)]
    for copy in copies:
        copy.start()
    q_ref, nk_ref, nv_ref, k_ref, v_ref = held
    tiles, size, width = k_ref.shape
    for copy in copies:
        copy.wait()

    @pl.loop(0, tiles)
    def _(t):
        live = lax.broadcasted_iota(jnp.int32, (size, width), 0) < lengths[t]
        k = k_ref[t].astype(F32)
        kt_ref[t] = jnp.where(live, k, k[:1]).T.astype(BF16)
        va_ref[t, :, :width] = jnp.where(live, v_ref[t].astype(F32), 0.0).astype(BF16)
        va_ref[t, :, width:] = live.astype(F32).astype(BF16)

    halves, part, _ = q_ref.shape
    new = nk_ref.shape[1]
    rows = halves * part
    for i in range(halves):
        s = lax.dot_general(q_ref[i], nk_ref[i], (((1,), (1,)), ((), ())), preferred_element_type=F32)
        token = lax.broadcasted_iota(jnp.int32, (part, new), 0) // group
        seen = token >= lax.broadcasted_iota(jnp.int32, (part, new), 1)
        s = jnp.where(seen, s, NEG)
        peak = jnp.max(s, axis=1, keepdims=True)
        weights = jnp.where(seen, jnp.exp2((s - peak) * scale), 0.0)
        total = jnp.sum(weights, axis=1, keepdims=True)
        summed = jnp.dot(weights.astype(BF16), nv_ref[i], preferred_element_type=F32)
        o_ref[i * part : (i + 1) * part, :] = summed / total
        level = peak * scale + jnp.log(total) * LOG2
        rowed = to_lanes(jnp.broadcast_to(level, (part, width)), part)
        for b, line in enumerate(rowed):
            at = rows + i * len(rowed) + b
            o_ref[at : at + 1, :] = line


def prepare(lengths, q, new_keys, new_values, keys, values, scale, group):
    halves, part, width = q.shape
    tiles, size, _ = keys.shape
    return pl.pallas_call(
        functools.partial(prepare_kernel, scale, group),
        out_shape=[
            jax.ShapeDtypeStruct((tiles, width, size), BF16),
            jax.ShapeDtypeStruct((tiles, size, 2 * width), BF16),
            jax.ShapeDtypeStruct((halves * part + 8, width), F32),
        ],
        in_specs=[SMEM] + [ANY] * 5,
        out_specs=[VMEM] * 3,
        scratch_shapes=[pltpu.VMEM(a.shape, BF16) for a in (q, new_keys, new_values, keys, values)]
        + [pltpu.SemaphoreType.DMA] * 5,
        compiler_params=pltpu.CompilerParams(vmem_limit_bytes=44 << 20),
        cost_estimate=pl.CostEstimate(flops=1 << 24, bytes_accessed=16 << 20, transcendentals=1 << 15),
        name="prepare",
    )(lengths, *(pltpu.with_memory_space_constraint(a, pltpu.HBM) for a in (q, new_keys, new_values, keys, values)))


def attend_kernel(
    scale, halves, lengths, q_ref, k_ref, v_ref, o_ref, s_ref, m_ref, acc_ref, flag_ref, member, f_sem
):
    homes, held, width = q_ref.shape
    rows = held - META
    tiles, _, size = k_ref.shape
    part = rows // halves
    count = homes * halves

    names = jnp.concatenate([q_ref[h, rows:, :].astype(F32)[:halves] for h in range(homes)], axis=0)
    lane = lax.broadcasted_iota(jnp.int32, names.shape, 1)
    first = (lax.axis_index("owner") * tiles).astype(F32)
    flags = jnp.zeros(names.shape, F32)
    for t in range(tiles):
        inside = jnp.max(jnp.where(names == first + t, 1.0, 0.0), axis=1, keepdims=True)
        flags = jnp.where(lane == t, inside, flags)
    flag_ref[:count, :] = flags.astype(jnp.int32)
    flag_ref[count:, :] = jnp.broadcast_to(jnp.sum(flags, axis=0, keepdims=True), names.shape).astype(jnp.int32)
    f_copy = pltpu.make_async_copy(flag_ref, member, f_sem)
    f_copy.start()
    m_ref[...] = jnp.full(m_ref.shape, NEG, F32)
    acc_ref[...] = jnp.zeros(acc_ref.shape, F32)
    f_copy.wait()

    def blocks(t):
        return [(slice(i * part, (i + 1) * part), member[i, t] > 0) for i in range(count)]

    def for_each_tile(body):
        @pl.loop(0, tiles)
        def _(t):
            used = member[count, t] > 0
            for n in range(1, size // STEP + 1):
                fits = lengths[t] > (n - 1) * STEP
                if n * STEP < size:
                    fits = fits & (lengths[t] <= n * STEP)

                @pl.when(used & fits)
                def _():
                    body(t, n * STEP)

    def score(t, wide):
        q = q_ref[:, :rows, :].reshape(homes * rows, width)
        s = jnp.dot(q, k_ref[t, :, :wide], preferred_element_type=F32)
        s_ref[t, :, :wide] = s
        for here, inside in blocks(t):
            x = s[here, :128]
            for j in range(128, wide, 128):
                x = jnp.maximum(x, s[here, j : j + 128])
            m_ref[here, :] = jnp.maximum(m_ref[here, :], jnp.where(inside, x, NEG))

    for_each_tile(score)
    peak = jnp.max(m_ref[...], axis=1, keepdims=True) * scale
    m_ref[...] = jnp.broadcast_to(peak, m_ref.shape)

    def weigh(t, wide):
        weights = []
        for here, inside in blocks(t):
            shift = jnp.where(inside, m_ref[here, :], -NEG)
            weights.append(
                jnp.concatenate(
                    [jnp.exp2(s_ref[t, here, j : j + 128] * scale - shift).astype(BF16) for j in range(0, wide, 128)],
                    axis=1,
                )
            )
        acc_ref[...] += jnp.dot(jnp.concatenate(weights, axis=0), v_ref[t, :wide, :], preferred_element_type=F32)

    for_each_tile(weigh)
    for h in range(homes):
        here = slice(h * rows, (h + 1) * rows)
        total = acc_ref[here, width:]
        o_ref[h, :rows, :] = (acc_ref[here, :width] / jnp.maximum(total, -1.0 / NEG)).astype(BF16)
        sums = jnp.concatenate(to_lanes(total, rows), axis=0)
        peaks = jnp.concatenate(to_lanes(m_ref[here, :], rows), axis=0)
        level = jnp.where(sums > 0.0, peaks + jnp.log(jnp.maximum(sums, -1.0 / NEG)) * LOG2, NEG)
        o_ref[h, rows:, :] = in_parts([level[b : b + 1] for b in range(rows // 128)])


def attend(q, keys, values, lengths, scale, halves):
    homes, held, width = q.shape
    tiles, _, size = keys.shape
    rows = held - META
    return pl.pallas_call(
        functools.partial(attend_kernel, scale, halves),
        out_shape=jax.ShapeDtypeStruct(q.shape, BF16),
        in_specs=[SMEM, VMEM, VMEM, VMEM],
        out_specs=VMEM,
        scratch_shapes=[
            pltpu.VMEM((tiles, homes * rows, size), F32),
            pltpu.VMEM((homes * rows, 128), F32),
            pltpu.VMEM((homes * rows, 2 * width), F32),
            pltpu.VMEM((2 * homes * halves, 128), jnp.int32),
            pltpu.SMEM((2 * homes * halves, 128), jnp.int32),
            pltpu.SemaphoreType.DMA,
        ],
        compiler_params=pltpu.CompilerParams(vmem_limit_bytes=44 << 20),
        cost_estimate=pl.CostEstimate(flops=1 << 30, bytes_accessed=1 << 20, transcendentals=1 << 18),
        name="attend",
    )(lengths, q, keys, values)


def weights_of(lines):
    level = jnp.concatenate(lines + [jnp.full((128 - len(lines), 128), 2 * NEG, F32)], axis=0)
    top = jnp.max(level, axis=0, keepdims=True)
    weight = jnp.exp2(level - top)
    total = jnp.sum(weight, axis=0, keepdims=True)
    return (weight / total).T, top + jnp.log(total) * LOG2


def merge_kernel(*refs):
    a_refs, o_refs = refs[:2], refs[2:]
    count = len(a_refs)
    homes, held, _ = a_refs[0].shape
    if len(o_refs) == 1:
        o_refs = [o_refs[0].at[h] for h in range(homes)]
    rows = held - META
    for h in range(homes):
        metas = [a[h, rows:, :].astype(F32) for a in a_refs]
        lines = []
        for b in range(rows // 128):
            weight, line = weights_of([levels(meta, b) for meta in metas])
            lines.append(line)
            here = slice(b * 128, (b + 1) * 128)
            acc = a_refs[0][h, here, :].astype(F32) * weight[:, 0:1]
            for i in range(1, count):
                acc = acc + a_refs[i][h, here, :].astype(F32) * weight[:, i : i + 1]
            o_refs[h][here, :] = acc.astype(BF16)
        o_refs[h][rows:, :] = in_parts(lines)


def merge(one, two, apart):
    homes, held, width = one.shape
    out = [jax.ShapeDtypeStruct((held, width), BF16)] * homes if apart else jax.ShapeDtypeStruct(one.shape, BF16)
    return pl.pallas_call(
        merge_kernel,
        out_shape=out,
        in_specs=[VMEM] * 2,
        out_specs=[VMEM] * homes if apart else VMEM,
        compiler_params=pltpu.CompilerParams(vmem_limit_bytes=16 << 20),
        cost_estimate=pl.CostEstimate(flops=1 << 34, bytes_accessed=4 << 20, transcendentals=1 << 14),
        name="merge",
    )(one, two)


def project_kernel(group, ranks, cores, *refs):
    a_refs, (own_ref, w_ref, keep_ref, give_ref, sum_ref, all_ref, flat_ref, held_ref, sems) = refs[:-9], refs[-9:]
    blocks, _, block = held_ref.shape
    copies = [
        pltpu.make_async_copy(w_ref.at[:, pl.ds(j * block, block)], held_ref.at[j], sems.at[j]) for j in range(blocks)
    ]
    for copy in copies:
        copy.start()
    rows, width = sum_ref.shape
    metas = [a[rows:, :].astype(F32) for a in a_refs]
    for b in range(rows // 128):
        weight, _ = weights_of([own_ref[rows + b : rows + b + 1, :]] + [levels(meta, b) for meta in metas])
        here = slice(b * 128, (b + 1) * 128)
        acc = own_ref[here, :] * weight[:, 0:1]
        for i, a in enumerate(a_refs):
            acc = acc + a[here, :].astype(F32) * weight[:, i + 1 : i + 2]
        sum_ref[here, :] = acc
    tokens = rows // group
    for g in range(group):
        all_ref[:, g * width : (g + 1) * width] = sum_ref[pl.ds(g, tokens, stride=group), :]
    chips = ranks // cores
    share = tokens // ranks
    rank = lax.axis_index("kvh")
    chip, core = rank // cores, rank % cores
    for i in range(cores):
        for d in range(chips):
            to = ((chip + d) % chips) * cores + (core + i) % cores
            at = (i * chips + d) * share
            flat_ref[at : at + share, :] = all_ref[pl.ds(pl.multiple_of(to * share, share), share), :]
    flat = flat_ref[...].astype(BF16)
    half = tokens // cores
    for j, copy in enumerate(copies):
        copy.wait()
        out = jnp.dot(flat, held_ref[j], preferred_element_type=F32).astype(BF16)
        keep_ref[:, j * block : (j + 1) * block] = out[:half]
        give_ref[:, j * block : (j + 1) * block] = out[half:]


def project(parts, own, weight, group, ranks, cores):
    held, width = parts[0].shape
    rows = held - META
    depth, columns = weight.shape
    tokens = rows // group
    block = 1024
    return pl.pallas_call(
        functools.partial(project_kernel, group, ranks, cores),
        out_shape=[jax.ShapeDtypeStruct((tokens // cores, columns), BF16)] * 2,
        in_specs=[VMEM] * (len(parts) + 1) + [ANY],
        out_specs=[VMEM] * 2,
        scratch_shapes=[
            pltpu.VMEM((rows, width), F32),
            pltpu.VMEM((tokens, depth), F32),
            pltpu.VMEM((tokens, depth), F32),
            pltpu.VMEM((columns // block, depth, block), BF16),
            pltpu.SemaphoreType.DMA((columns // block,)),
        ],
        compiler_params=pltpu.CompilerParams(vmem_limit_bytes=50 << 20),
        cost_estimate=pl.CostEstimate(flops=1 << 30, bytes_accessed=18 << 20, transcendentals=1 << 14),
        name="project",
    )(*parts, own, weight)


def local(
    queries, new_keys, new_values, ancestors, tile_keys, tile_values, tile_lengths, out_weight
):
    owners = lax.axis_size("owner")
    ranks = lax.axis_size("kvh")
    cores = 2
    chips = ranks // cores
    side = math.isqrt(owners)
    parts, new, group, width = queries.shape
    per_owner = tile_keys.shape[0]
    scale = width**-0.5 * LOG2
    rows = parts * new * group

    def along(x, leg, step):
        pairs = []
        for o in range(owners):
            y, z = divmod(o, side)
            for k in range(ranks):
                if (k % cores + leg) % 2 == 0:
                    to = y * side + (z + step) % side
                else:
                    to = (y + step) % side * side + z
                pairs.append((o * ranks + k, to * ranks + k))
        return lax.ppermute(x, ("owner", "kvh"), pairs)

    names = jnp.pad(ancestors.astype(BF16), ((0, META - parts), (0, width - ancestors.shape[1])), constant_values=-1)
    home = jnp.concatenate([queries.reshape(rows, width), names], axis=0)
    near = [along(home, 0, d) for d in range(1, side)]
    keys, values, own = prepare(
        tile_lengths,
        queries.reshape(parts, new * group, width),
        new_keys[:, :, 0],
        new_values[:, :, 0],
        tile_keys[:, 0],
        tile_values[:, 0],
        scale,
        group,
    )
    row, keys, values = lax.optimization_barrier((jnp.stack([home] + near), keys, values))
    order = sorted(range(side), key=lambda e: min(e, side - e))
    blocks = {e: along(row, 1, e) if e else row for e in order[:-1]}
    back = []
    for e in order:
        if e == order[1]:
            late, out = lax.optimization_barrier((row, out))
            blocks[order[-1]] = along(late, 1, order[-1])
        block = blocks[e]
        if e:
            block, out = lax.optimization_barrier((block, out))
        out = attend(block, keys, values, tile_lengths, scale, parts)
        back.append(along(out, 1, -e) if e else out)
    merged = back[0]
    for i in range(1, side):
        merged = merge(merged, back[i], i == side - 1)
    final = [along(merged[d], 0, -d) if d else merged[d] for d in range(side)]
    keep, give = project(final, own, out_weight, group, ranks, cores)
    got = lax.ppermute(give, "kvh", [(k, k // cores * cores + (k + 1) % cores) for k in range(ranks)])
    share = keep.shape[0] // chips
    pieces = [
        keep[d * share : (d + 1) * share].astype(F32) + got[d * share : (d + 1) * share].astype(F32) for d in range(chips)
    ]
    result = pieces[0]
    for d in sorted(range(1, chips), key=lambda d: min(d, chips - d)):
        pairs = [(k, (k + d * cores) % ranks) for k in range(ranks)]
        result = result + lax.ppermute(pieces[d].astype(BF16), "kvh", pairs).astype(F32)
    return result.astype(BF16)


def solution(mesh):
    return jax.shard_map(
        local,
        mesh=mesh,
        in_specs=(
            P("owner", None, "kvh", None),
            P("owner", None, "kvh", None),
            P("owner", None, "kvh", None),
            P("owner", None),
            P("owner", "kvh", None, None),
            P("owner", "kvh", None, None),
            P("owner"),
            P("kvh", None),
        ),
        out_specs=P(("owner", "kvh"), None),
        check_vma=False,
    )
```

```python
import functools
import math

import jax
import jax.numpy as jnp
from jax import lax
from jax.experimental import pallas as pl
from jax.experimental.pallas import tpu as pltpu
from jax.sharding import PartitionSpec as P

NEG = -1e30
META = 16
STEP = 256
F32 = jnp.float32
BF16 = jnp.bfloat16
VMEM = pl.BlockSpec(memory_space=pltpu.VMEM)
SMEM = pl.BlockSpec(memory_space=pltpu.SMEM)
ANY = pl.BlockSpec(memory_space=pl.ANY)
LOG2 = 1.0 / math.log(2.0)


def to_lanes(column, count):
    r = lax.broadcasted_iota(jnp.int32, (128, 128), 0)
    c = lax.broadcasted_iota(jnp.int32, (128, 128), 1)
    eye = r == c
    rows = []
    for b in range(count // 128):
        rows.append(jnp.sum(jnp.where(eye, column[b * 128 : (b + 1) * 128], 0.0), axis=0, keepdims=True))
    return rows


def in_parts(lines):
    pieces = []
    for line in lines:
        high = line.astype(BF16).astype(F32)
        mid = (line - high).astype(BF16).astype(F32)
        pieces += [high, mid, line - high - mid]
    pad = jnp.zeros((META - len(pieces), 128), F32)
    return jnp.concatenate(pieces + [pad], axis=0).astype(BF16)


def levels(meta, b):
    return meta[3 * b : 3 * b + 1] + meta[3 * b + 1 : 3 * b + 2] + meta[3 * b + 2 : 3 * b + 3]


def prepare_kernel(scale, group, lengths, *refs):
    given, (kt_ref, va_ref, o_ref), held, sems = refs[:5], refs[5:8], refs[8:13], refs[13:]
    copies = [pltpu.make_async_copy(a, b, sem) for a, b, sem in zip(given, held, sems)]
    for copy in copies:
        copy.start()
    q_ref, nk_ref, nv_ref, k_ref, v_ref = held
    tiles, size, width = k_ref.shape
    for copy in copies:
        copy.wait()

    @pl.loop(0, tiles)
    def _(t):
        live = lax.broadcasted_iota(jnp.int32, (size, width), 0) < lengths[t]
        k = k_ref[t].astype(F32)
        kt_ref[t] = jnp.where(live, k, k[:1]).T.astype(BF16)
        va_ref[t, :, :width] = jnp.where(live, v_ref[t].astype(F32), 0.0).astype(BF16)
        va_ref[t, :, width:] = live.astype(F32).astype(BF16)

    halves, part, _ = q_ref.shape
    new = nk_ref.shape[1]
    rows = halves * part
    for i in range(halves):
        s = lax.dot_general(q_ref[i], nk_ref[i], (((1,), (1,)), ((), ())), preferred_element_type=F32)
        token = lax.broadcasted_iota(jnp.int32, (part, new), 0) // group
        seen = token >= lax.broadcasted_iota(jnp.int32, (part, new), 1)
        s = jnp.where(seen, s, NEG)
        peak = jnp.max(s, axis=1, keepdims=True)
        weights = jnp.where(seen, jnp.exp2((s - peak) * scale), 0.0)
        total = jnp.sum(weights, axis=1, keepdims=True)
        summed = jnp.dot(weights.astype(BF16), nv_ref[i], preferred_element_type=F32)
        o_ref[i * part : (i + 1) * part, :] = summed / total
        level = peak * scale + jnp.log(total) * LOG2
        rowed = to_lanes(jnp.broadcast_to(level, (part, width)), part)
        for b, line in enumerate(rowed):
            at = rows + i * len(rowed) + b
            o_ref[at : at + 1, :] = line


def prepare(lengths, q, new_keys, new_values, keys, values, scale, group):
    halves, part, width = q.shape
    tiles, size, _ = keys.shape
    return pl.pallas_call(
        functools.partial(prepare_kernel, scale, group),
        out_shape=[
            jax.ShapeDtypeStruct((tiles, width, size), BF16),
            jax.ShapeDtypeStruct((tiles, size, 2 * width), BF16),
            jax.ShapeDtypeStruct((halves * part + 8, width), F32),
        ],
        in_specs=[SMEM] + [ANY] * 5,
        out_specs=[VMEM] * 3,
        scratch_shapes=[pltpu.VMEM(a.shape, BF16) for a in (q, new_keys, new_values, keys, values)]
        + [pltpu.SemaphoreType.DMA] * 5,
        compiler_params=pltpu.CompilerParams(vmem_limit_bytes=44 << 20),
        cost_estimate=pl.CostEstimate(flops=1 << 24, bytes_accessed=16 << 20, transcendentals=1 << 15),
        name="prepare",
    )(lengths, *(pltpu.with_memory_space_constraint(a, pltpu.HBM) for a in (q, new_keys, new_values, keys, values)))


def attend_kernel(
    scale, halves, lengths, q_ref, k_ref, v_ref, *refs
):
    homes, held, width = q_ref.shape
    o_refs, (s_ref, m_ref, acc_ref, flag_ref, member, f_sem) = refs[:homes], refs[homes:]
    rows = held - META
    tiles, _, size = k_ref.shape
    part = rows // halves
    count = homes * halves

    names = jnp.concatenate([q_ref[h, rows:, :].astype(F32)[:halves] for h in range(homes)], axis=0)
    lane = lax.broadcasted_iota(jnp.int32, names.shape, 1)
    first = (lax.axis_index("owner") * tiles).astype(F32)
    flags = jnp.zeros(names.shape, F32)
    for t in range(tiles):
        inside = jnp.max(jnp.where(names == first + t, 1.0, 0.0), axis=1, keepdims=True)
        flags = jnp.where(lane == t, inside, flags)
    flag_ref[:count, :] = flags.astype(jnp.int32)
    flag_ref[count:, :] = jnp.broadcast_to(jnp.sum(flags, axis=0, keepdims=True), names.shape).astype(jnp.int32)
    f_copy = pltpu.make_async_copy(flag_ref, member, f_sem)
    f_copy.start()
    m_ref[...] = jnp.full(m_ref.shape, NEG, F32)
    acc_ref[...] = jnp.zeros(acc_ref.shape, F32)
    f_copy.wait()

    def blocks(t):
        return [(slice(i * part, (i + 1) * part), member[i, t] > 0) for i in range(count)]

    def for_each_tile(body):
        @pl.loop(0, tiles)
        def _(t):
            used = member[count, t] > 0
            for n in range(1, size // STEP + 1):
                fits = lengths[t] > (n - 1) * STEP
                if n * STEP < size:
                    fits = fits & (lengths[t] <= n * STEP)

                @pl.when(used & fits)
                def _():
                    body(t, n * STEP)

    def score(t, wide):
        q = q_ref[:, :rows, :].reshape(homes * rows, width)
        s = jnp.dot(q, k_ref[t, :, :wide], preferred_element_type=F32)
        s_ref[t, :, :wide] = s
        for here, inside in blocks(t):
            x = s[here, :128]
            for j in range(128, wide, 128):
                x = jnp.maximum(x, s[here, j : j + 128])
            m_ref[here, :] = jnp.maximum(m_ref[here, :], jnp.where(inside, x, NEG))

    for_each_tile(score)
    peak = jnp.max(m_ref[...], axis=1, keepdims=True) * scale
    m_ref[...] = jnp.broadcast_to(peak, m_ref.shape)

    def weigh(t, wide):
        weights = []
        for here, inside in blocks(t):
            shift = jnp.where(inside, m_ref[here, :], -NEG)
            weights.append(
                jnp.concatenate(
                    [jnp.exp2(s_ref[t, here, j : j + 128] * scale - shift).astype(BF16) for j in range(0, wide, 128)],
                    axis=1,
                )
            )
        acc_ref[...] += jnp.dot(jnp.concatenate(weights, axis=0), v_ref[t, :wide, :], preferred_element_type=F32)

    for_each_tile(weigh)
    for h in range(homes):
        here = slice(h * rows, (h + 1) * rows)
        total = acc_ref[here, width:]
        o_refs[h][:rows, :] = (acc_ref[here, :width] / jnp.maximum(total, -1.0 / NEG)).astype(BF16)
        sums = jnp.concatenate(to_lanes(total, rows), axis=0)
        peaks = jnp.concatenate(to_lanes(m_ref[here, :], rows), axis=0)
        level = jnp.where(sums > 0.0, peaks + jnp.log(jnp.maximum(sums, -1.0 / NEG)) * LOG2, NEG)
        o_refs[h][rows:, :] = in_parts([level[b : b + 1] for b in range(rows // 128)])


def attend(q, keys, values, lengths, scale, halves):
    homes, held, width = q.shape
    tiles, _, size = keys.shape
    rows = held - META
    return pl.pallas_call(
        functools.partial(attend_kernel, scale, halves),
        out_shape=[jax.ShapeDtypeStruct((held, width), BF16)] * homes,
        in_specs=[SMEM, VMEM, VMEM, VMEM],
        out_specs=[VMEM] * homes,
        scratch_shapes=[
            pltpu.VMEM((tiles, homes * rows, size), F32),
            pltpu.VMEM((homes * rows, 128), F32),
            pltpu.VMEM((homes * rows, 2 * width), F32),
            pltpu.VMEM((2 * homes * halves, 128), jnp.int32),
            pltpu.SMEM((2 * homes * halves, 128), jnp.int32),
            pltpu.SemaphoreType.DMA,
        ],
        compiler_params=pltpu.CompilerParams(vmem_limit_bytes=44 << 20),
        cost_estimate=pl.CostEstimate(flops=1 << 30, bytes_accessed=1 << 20, transcendentals=1 << 18),
        name="attend",
    )(lengths, q, keys, values)


def absorb(own_ref, parts, sum_ref):
    rows = parts[0].shape[0] - META
    metas = [a[rows:, :].astype(F32) for a in parts]
    lines = []
    for b in range(rows // 128):
        given = [own_ref[rows + b : rows + b + 1, :]] + [levels(meta, b) for meta in metas]
        level = jnp.concatenate(given + [jnp.full((128 - len(given), 128), 2 * NEG, F32)], axis=0)
        top = jnp.max(level, axis=0, keepdims=True)
        weight = jnp.exp2(level - top)
        total = jnp.sum(weight, axis=0, keepdims=True)
        weight = (weight / total).T
        lines.append(top + jnp.log(total) * LOG2)
        here = slice(b * 128, (b + 1) * 128)
        acc = own_ref[here, :] * weight[:, 0:1]
        for i, a in enumerate(parts):
            acc = acc + a[here, :].astype(F32) * weight[:, i + 1 : i + 2]
        sum_ref[here, :] = acc
    return lines


def merge_kernel(own_ref, *refs):
    parts, o_ref = refs[:-1], refs[-1]
    rows = parts[0].shape[0] - META
    for b, line in enumerate(absorb(own_ref, parts, o_ref)):
        o_ref[rows + b : rows + b + 1, :] = line


def merge(own, parts):
    return pl.pallas_call(
        merge_kernel,
        out_shape=jax.ShapeDtypeStruct(own.shape, F32),
        in_specs=[VMEM] * (len(parts) + 1),
        out_specs=VMEM,
        compiler_params=pltpu.CompilerParams(vmem_limit_bytes=16 << 20),
        cost_estimate=pl.CostEstimate(flops=1 << 34, bytes_accessed=4 << 20, transcendentals=1 << 14),
        name="merge",
    )(own, *parts)


def project_kernel(group, ranks, cores, *refs):
    a_refs, (own_ref, w_ref, keep_ref, give_ref, sum_ref, all_ref, flat_ref, held_ref, sems) = refs[:-9], refs[-9:]
    blocks, _, block = held_ref.shape
    copies = [
        pltpu.make_async_copy(w_ref.at[:, pl.ds(j * block, block)], held_ref.at[j], sems.at[j]) for j in range(blocks)
    ]
    for copy in copies:
        copy.start()
    rows, width = sum_ref.shape
    absorb(own_ref, a_refs, sum_ref)
    tokens = rows // group
    for g in range(group):
        all_ref[:, g * width : (g + 1) * width] = sum_ref[pl.ds(g, tokens, stride=group), :]
    chips = ranks // cores
    share = tokens // ranks
    rank = lax.axis_index("kvh")
    chip, core = rank // cores, rank % cores
    for i in range(cores):
        for d in range(chips):
            to = ((chip + d) % chips) * cores + (core + i) % cores
            at = (i * chips + d) * share
            flat_ref[at : at + share, :] = all_ref[pl.ds(pl.multiple_of(to * share, share), share), :]
    flat = flat_ref[...].astype(BF16)
    half = tokens // cores
    for j, copy in enumerate(copies):
        copy.wait()
        out = jnp.dot(flat, held_ref[j], preferred_element_type=F32).astype(BF16)
        keep_ref[:, j * block : (j + 1) * block] = out[:half]
        give_ref[:, j * block : (j + 1) * block] = out[half:]


def project(parts, own, weight, group, ranks, cores):
    held, width = parts[0].shape
    rows = held - META
    depth, columns = weight.shape
    tokens = rows // group
    block = 1024
    return pl.pallas_call(
        functools.partial(project_kernel, group, ranks, cores),
        out_shape=[jax.ShapeDtypeStruct((tokens // cores, columns), BF16)] * 2,
        in_specs=[VMEM] * (len(parts) + 1) + [ANY],
        out_specs=[VMEM] * 2,
        scratch_shapes=[
            pltpu.VMEM((rows, width), F32),
            pltpu.VMEM((tokens, depth), F32),
            pltpu.VMEM((tokens, depth), F32),
            pltpu.VMEM((columns // block, depth, block), BF16),
            pltpu.SemaphoreType.DMA((columns // block,)),
        ],
        compiler_params=pltpu.CompilerParams(vmem_limit_bytes=50 << 20),
        cost_estimate=pl.CostEstimate(flops=1 << 30, bytes_accessed=18 << 20, transcendentals=1 << 14),
        name="project",
    )(*parts, own, weight)


def local(
    queries, new_keys, new_values, ancestors, tile_keys, tile_values, tile_lengths, out_weight
):
    owners = lax.axis_size("owner")
    ranks = lax.axis_size("kvh")
    cores = 2
    chips = ranks // cores
    side = math.isqrt(owners)
    parts, new, group, width = queries.shape
    per_owner = tile_keys.shape[0]
    scale = width**-0.5 * LOG2
    rows = parts * new * group

    def along(x, *steps):
        pairs = []
        for o in range(owners):
            for k in range(ranks):
                dz, dy = steps if k % cores == 0 else steps[::-1]
                y, z = (o // side + dy) % side, (o + dz) % side
                pairs.append((o * ranks + k, (y * side + z) * ranks + k))
        return lax.ppermute(x, ("owner", "kvh"), pairs)

    names = jnp.pad(ancestors.astype(BF16), ((0, META - parts), (0, width - ancestors.shape[1])), constant_values=-1)
    home = jnp.concatenate([queries.reshape(rows, width), names], axis=0)
    near = [along(home, d, 0) for d in range(1, side)]
    keys, values, own = prepare(
        tile_lengths,
        queries.reshape(parts, new * group, width),
        new_keys[:, :, 0],
        new_values[:, :, 0],
        tile_keys[:, 0],
        tile_values[:, 0],
        scale,
        group,
    )
    row, keys, values = lax.optimization_barrier((jnp.stack([home] + near), keys, values))
    blocks = {1: along(row, 0, 1)}
    waves = []
    for e in range(side):
        if e == 0:
            outs = attend(row, keys, values, tile_lengths, scale, parts)
            late, outs = lax.optimization_barrier((row, outs))
            for i in range(2, side):
                blocks[i] = along(late, 0, i)
        else:
            block, outs = lax.optimization_barrier((blocks[e], outs))
            outs = attend(block, keys, values, tile_lengths, scale, parts)
        waves.append([along(out, -d, -e) if d or e else out for d, out in enumerate(outs)])
    own = merge(own, [a for wave in waves[:-1] for a in wave])
    final = waves[-1]
    keep, give = project(final, own, out_weight, group, ranks, cores)
    got = lax.ppermute(give, "kvh", [(k, k // cores * cores + (k + 1) % cores) for k in range(ranks)])
    share = keep.shape[0] // chips
    pieces = [
        keep[d * share : (d + 1) * share].astype(F32) + got[d * share : (d + 1) * share].astype(F32) for d in range(chips)
    ]
    result = pieces[0]
    for d in sorted(range(1, chips), key=lambda d: min(d, chips - d)):
        pairs = [(k, (k + d * cores) % ranks) for k in range(ranks)]
        result = result + lax.ppermute(pieces[d].astype(BF16), "kvh", pairs).astype(F32)
    return result.astype(BF16)


def solution(mesh):
    return jax.shard_map(
        local,
        mesh=mesh,
        in_specs=(
            P("owner", None, "kvh", None),
            P("owner", None, "kvh", None),
            P("owner", None, "kvh", None),
            P("owner", None),
            P("owner", "kvh", None, None),
            P("owner", "kvh", None, None),
            P("owner"),
            P("kvh", None),
        ),
        out_specs=P(("owner", "kvh"), None),
        check_vma=False,
    )
```

```python
import functools
import math

import jax
import jax.numpy as jnp
from jax import lax
from jax.experimental import pallas as pl
from jax.experimental.pallas import tpu as pltpu
from jax.sharding import PartitionSpec as P

NEG = -1e30
META = 16
STEP = 256
F32 = jnp.float32
BF16 = jnp.bfloat16
VMEM = pl.BlockSpec(memory_space=pltpu.VMEM)
SMEM = pl.BlockSpec(memory_space=pltpu.SMEM)
ANY = pl.BlockSpec(memory_space=pl.ANY)
LOG2 = 1.0 / math.log(2.0)


def to_lanes(column, count):
    r = lax.broadcasted_iota(jnp.int32, (128, 128), 0)
    c = lax.broadcasted_iota(jnp.int32, (128, 128), 1)
    eye = r == c
    rows = []
    for b in range(count // 128):
        rows.append(jnp.sum(jnp.where(eye, column[b * 128 : (b + 1) * 128], 0.0), axis=0, keepdims=True))
    return rows


def in_parts(lines):
    pieces = []
    for line in lines:
        high = line.astype(BF16).astype(F32)
        mid = (line - high).astype(BF16).astype(F32)
        pieces += [high, mid, line - high - mid]
    pad = jnp.zeros((META - len(pieces), 128), F32)
    return jnp.concatenate(pieces + [pad], axis=0).astype(BF16)


def levels(meta, b):
    return meta[3 * b : 3 * b + 1] + meta[3 * b + 1 : 3 * b + 2] + meta[3 * b + 2 : 3 * b + 3]


def pack_kernel(q_any, a_any, o_ref, a_ref, meta_ref, q_sem, a_sem):
    rows = q_any.shape[0]
    q_copy = pltpu.make_async_copy(q_any, o_ref.at[pl.ds(0, rows)], q_sem)
    a_copy = pltpu.make_async_copy(a_any, a_ref, a_sem)
    q_copy.start()
    a_copy.start()
    meta_ref[...] = jnp.full(meta_ref.shape, -1.0, F32)
    a_copy.wait()
    meta_ref[: a_ref.shape[0], : a_ref.shape[1]] = a_ref[...].astype(F32)
    o_ref[rows:, :] = meta_ref[...].astype(BF16)
    q_copy.wait()


def pack(q, ancestors):
    rows, width = q.shape
    return pl.pallas_call(
        pack_kernel,
        out_shape=jax.ShapeDtypeStruct((rows + META, width), BF16),
        in_specs=[ANY] * 2,
        out_specs=VMEM,
        scratch_shapes=[
            pltpu.VMEM(ancestors.shape, jnp.int32),
            pltpu.VMEM((META, width), F32),
            pltpu.SemaphoreType.DMA,
            pltpu.SemaphoreType.DMA,
        ],
        compiler_params=pltpu.CompilerParams(vmem_limit_bytes=4 << 20),
        cost_estimate=pl.CostEstimate(flops=1 << 10, bytes_accessed=1 << 18, transcendentals=0),
        name="pack",
    )(*(pltpu.with_memory_space_constraint(a, pltpu.HBM) for a in (q, ancestors)))


def prepare_kernel(scale, group, lengths, *refs):
    given, (kt_ref, va_ref, o_ref), held, sems = refs[:5], refs[5:8], refs[8:13], refs[13:]
    copies = [pltpu.make_async_copy(a, b, sem) for a, b, sem in zip(given, held, sems)]
    for copy in copies:
        copy.start()
    q_ref, nk_ref, nv_ref, k_ref, v_ref = held
    tiles, size, width = k_ref.shape
    for copy in copies:
        copy.wait()

    @pl.loop(0, tiles)
    def _(t):
        live = lax.broadcasted_iota(jnp.int32, (size, width), 0) < lengths[t]
        k = k_ref[t].astype(F32)
        kt_ref[t] = jnp.where(live, k, k[:1]).T.astype(BF16)
        va_ref[t, :, :width] = jnp.where(live, v_ref[t].astype(F32), 0.0).astype(BF16)
        va_ref[t, :, width:] = live.astype(F32).astype(BF16)

    halves, part, _ = q_ref.shape
    new = nk_ref.shape[1]
    rows = halves * part
    for i in range(halves):
        s = lax.dot_general(q_ref[i], nk_ref[i], (((1,), (1,)), ((), ())), preferred_element_type=F32)
        token = lax.broadcasted_iota(jnp.int32, (part, new), 0) // group
        seen = token >= lax.broadcasted_iota(jnp.int32, (part, new), 1)
        s = jnp.where(seen, s, NEG)
        peak = jnp.max(s, axis=1, keepdims=True)
        weights = jnp.where(seen, jnp.exp2((s - peak) * scale), 0.0)
        total = jnp.sum(weights, axis=1, keepdims=True)
        summed = jnp.dot(weights.astype(BF16), nv_ref[i], preferred_element_type=F32)
        o_ref[i * part : (i + 1) * part, :] = summed / total
        level = peak * scale + jnp.log(total) * LOG2
        rowed = to_lanes(jnp.broadcast_to(level, (part, width)), part)
        for b, line in enumerate(rowed):
            at = rows + i * len(rowed) + b
            o_ref[at : at + 1, :] = line


def prepare(lengths, q, new_keys, new_values, keys, values, scale, group):
    halves, part, width = q.shape
    tiles, size, _ = keys.shape
    return pl.pallas_call(
        functools.partial(prepare_kernel, scale, group),
        out_shape=[
            jax.ShapeDtypeStruct((tiles, width, size), BF16),
            jax.ShapeDtypeStruct((tiles, size, 2 * width), BF16),
            jax.ShapeDtypeStruct((halves * part + 8, width), F32),
        ],
        in_specs=[SMEM] + [ANY] * 5,
        out_specs=[VMEM] * 3,
        scratch_shapes=[pltpu.VMEM(a.shape, BF16) for a in (q, new_keys, new_values, keys, values)]
        + [pltpu.SemaphoreType.DMA] * 5,
        compiler_params=pltpu.CompilerParams(vmem_limit_bytes=44 << 20),
        cost_estimate=pl.CostEstimate(flops=1 << 24, bytes_accessed=16 << 20, transcendentals=1 << 15),
        name="prepare",
    )(lengths, *(pltpu.with_memory_space_constraint(a, pltpu.HBM) for a in (q, new_keys, new_values, keys, values)))


def attend_kernel(
    scale, halves, lengths, q_ref, k_ref, v_ref, *refs
):
    homes, held, width = q_ref.shape
    pieces, (s_ref, m_ref, acc_ref, flag_ref, member, f_sem) = refs[:-6], refs[-6:]
    o_refs = [piece.at[i] for piece in pieces for i in range(piece.shape[0])]
    rows = held - META
    tiles, _, size = k_ref.shape
    part = rows // halves
    count = homes * halves

    names = jnp.concatenate([q_ref[h, rows:, :].astype(F32)[:halves] for h in range(homes)], axis=0)
    lane = lax.broadcasted_iota(jnp.int32, names.shape, 1)
    first = (lax.axis_index("owner") * tiles).astype(F32)
    flags = jnp.zeros(names.shape, F32)
    for t in range(tiles):
        inside = jnp.max(jnp.where(names == first + t, 1.0, 0.0), axis=1, keepdims=True)
        flags = jnp.where(lane == t, inside, flags)
    flag_ref[:count, :] = flags.astype(jnp.int32)
    flag_ref[count:, :] = jnp.broadcast_to(jnp.sum(flags, axis=0, keepdims=True), names.shape).astype(jnp.int32)
    f_copy = pltpu.make_async_copy(flag_ref, member, f_sem)
    f_copy.start()
    m_ref[...] = jnp.full(m_ref.shape, NEG, F32)
    acc_ref[...] = jnp.zeros(acc_ref.shape, F32)
    f_copy.wait()

    def blocks(t):
        return [(slice(i * part, (i + 1) * part), member[i, t] > 0) for i in range(count)]

    def for_each_tile(body):
        @pl.loop(0, tiles)
        def _(t):
            used = member[count, t] > 0
            for n in range(1, size // STEP + 1):
                fits = lengths[t] > (n - 1) * STEP
                if n * STEP < size:
                    fits = fits & (lengths[t] <= n * STEP)

                @pl.when(used & fits)
                def _():
                    body(t, n * STEP)

    def score(t, wide):
        q = q_ref[:, :rows, :].reshape(homes * rows, width)
        s = jnp.dot(q, k_ref[t, :, :wide], preferred_element_type=F32)
        s_ref[t, :, :wide] = s
        for here, inside in blocks(t):
            x = s[here, :128]
            for j in range(128, wide, 128):
                x = jnp.maximum(x, s[here, j : j + 128])
            m_ref[here, :] = jnp.maximum(m_ref[here, :], jnp.where(inside, x, NEG))

    for_each_tile(score)
    peak = jnp.max(m_ref[...], axis=1, keepdims=True) * scale
    m_ref[...] = jnp.broadcast_to(peak, m_ref.shape)

    def weigh(t, wide):
        weights = []
        for here, inside in blocks(t):
            shift = jnp.where(inside, m_ref[here, :], -NEG)
            weights.append(
                jnp.concatenate(
                    [jnp.exp2(s_ref[t, here, j : j + 128] * scale - shift).astype(BF16) for j in range(0, wide, 128)],
                    axis=1,
                )
            )
        acc_ref[...] += jnp.dot(jnp.concatenate(weights, axis=0), v_ref[t, :wide, :], preferred_element_type=F32)

    for_each_tile(weigh)
    for h in range(homes):
        here = slice(h * rows, (h + 1) * rows)
        total = acc_ref[here, width:]
        o_refs[h][:rows, :] = (acc_ref[here, :width] / jnp.maximum(total, -1.0 / NEG)).astype(BF16)
        sums = jnp.concatenate(to_lanes(total, rows), axis=0)
        peaks = jnp.concatenate(to_lanes(m_ref[here, :], rows), axis=0)
        level = jnp.where(sums > 0.0, peaks + jnp.log(jnp.maximum(sums, -1.0 / NEG)) * LOG2, NEG)
        o_refs[h][rows:, :] = in_parts([level[b : b + 1] for b in range(rows // 128)])


def attend(q, keys, values, lengths, scale, halves, pieces=1):
    homes, held, width = q.shape
    tiles, _, size = keys.shape
    rows = held - META
    return pl.pallas_call(
        functools.partial(attend_kernel, scale, halves),
        out_shape=[jax.ShapeDtypeStruct((homes // pieces, held, width), BF16)] * pieces,
        in_specs=[SMEM, VMEM, VMEM, VMEM],
        out_specs=[VMEM] * pieces,
        scratch_shapes=[
            pltpu.VMEM((tiles, homes * rows, size), F32),
            pltpu.VMEM((homes * rows, 128), F32),
            pltpu.VMEM((homes * rows, 2 * width), F32),
            pltpu.VMEM((2 * homes * halves, 128), jnp.int32),
            pltpu.SMEM((2 * homes * halves, 128), jnp.int32),
            pltpu.SemaphoreType.DMA,
        ],
        compiler_params=pltpu.CompilerParams(vmem_limit_bytes=44 << 20),
        cost_estimate=pl.CostEstimate(flops=1 << 20, bytes_accessed=1 << 18, transcendentals=0),
        name="attend",
    )(lengths, q, keys, values)


def weights_of(lines):
    level = jnp.concatenate(lines + [jnp.full((128 - len(lines), 128), 2 * NEG, F32)], axis=0)
    top = jnp.max(level, axis=0, keepdims=True)
    weight = jnp.exp2(level - top)
    total = jnp.sum(weight, axis=0, keepdims=True)
    return (weight / total).T, top + jnp.log(total) * LOG2


def merge_kernel(first, one_ref, two_ref, *o_refs):
    homes, held, _ = two_ref.shape
    if len(o_refs) == 1:
        o_refs = [o_refs[0].at[h] for h in range(homes)]
    rows = held - META
    for h in range(homes):
        given = [one_ref.at[first + h], two_ref.at[h]]
        metas = [a[rows:, :].astype(F32) for a in given]
        lines = []
        for b in range(rows // 128):
            weight, line = weights_of([levels(meta, b) for meta in metas])
            lines.append(line)
            here = slice(b * 128, (b + 1) * 128)
            acc = given[0][here, :].astype(F32) * weight[:, 0:1] + given[1][here, :].astype(F32) * weight[:, 1:2]
            o_refs[h][here, :] = acc.astype(BF16)
        o_refs[h][rows:, :] = in_parts(lines)


def merge(one, two, first=0, apart=False):
    homes, held, width = two.shape
    out = [jax.ShapeDtypeStruct((held, width), BF16)] * homes if apart else jax.ShapeDtypeStruct(two.shape, BF16)
    return pl.pallas_call(
        functools.partial(merge_kernel, first),
        out_shape=out,
        in_specs=[VMEM] * 2,
        out_specs=[VMEM] * homes if apart else VMEM,
        compiler_params=pltpu.CompilerParams(vmem_limit_bytes=16 << 20),
        cost_estimate=pl.CostEstimate(flops=1 << 30, bytes_accessed=1 << 18, transcendentals=0),
        name="merge",
    )(one, two)


def project_kernel(group, ranks, cores, *refs):
    a_refs, (own_ref, w_ref, keep_ref, give_ref, sum_ref, all_ref, flat_ref, held_ref, sems) = refs[:-9], refs[-9:]
    blocks, _, block = held_ref.shape
    copies = [
        pltpu.make_async_copy(w_ref.at[:, pl.ds(j * block, block)], held_ref.at[j], sems.at[j]) for j in range(blocks)
    ]
    for copy in copies:
        copy.start()
    rows, width = sum_ref.shape
    metas = [a[rows:, :].astype(F32) for a in a_refs]
    for b in range(rows // 128):
        weight, _ = weights_of([own_ref[rows + b : rows + b + 1, :]] + [levels(meta, b) for meta in metas])
        here = slice(b * 128, (b + 1) * 128)
        acc = own_ref[here, :] * weight[:, 0:1]
        for i, a in enumerate(a_refs):
            acc = acc + a[here, :].astype(F32) * weight[:, i + 1 : i + 2]
        sum_ref[here, :] = acc
    tokens = rows // group
    for g in range(group):
        all_ref[:, g * width : (g + 1) * width] = sum_ref[pl.ds(g, tokens, stride=group), :]
    chips = ranks // cores
    share = tokens // ranks
    rank = lax.axis_index("kvh")
    chip, core = rank // cores, rank % cores
    for i in range(cores):
        for d in range(chips):
            to = ((chip + d) % chips) * cores + (core + i) % cores
            at = (i * chips + d) * share
            flat_ref[at : at + share, :] = all_ref[pl.ds(pl.multiple_of(to * share, share), share), :]
    flat = flat_ref[...].astype(BF16)
    half = tokens // cores
    for j, copy in enumerate(copies):
        copy.wait()
        out = jnp.dot(flat, held_ref[j], preferred_element_type=F32).astype(BF16)
        keep_ref[:, j * block : (j + 1) * block] = out[:half]
        give_ref[:, j * block : (j + 1) * block] = out[half:]


def project(parts, own, weight, group, ranks, cores):
    held, width = parts[0].shape
    rows = held - META
    depth, columns = weight.shape
    tokens = rows // group
    block = 1024
    return pl.pallas_call(
        functools.partial(project_kernel, group, ranks, cores),
        out_shape=[jax.ShapeDtypeStruct((tokens // cores, columns), BF16)] * 2,
        in_specs=[VMEM] * (len(parts) + 1) + [ANY],
        out_specs=[VMEM] * 2,
        scratch_shapes=[
            pltpu.VMEM((rows, width), F32),
            pltpu.VMEM((tokens, depth), F32),
            pltpu.VMEM((tokens, depth), F32),
            pltpu.VMEM((columns // block, depth, block), BF16),
            pltpu.SemaphoreType.DMA((columns // block,)),
        ],
        compiler_params=pltpu.CompilerParams(vmem_limit_bytes=50 << 20),
        cost_estimate=pl.CostEstimate(flops=1 << 30, bytes_accessed=18 << 20, transcendentals=1 << 14),
        name="project",
    )(*parts, own, weight)


def local(
    queries, new_keys, new_values, ancestors, tile_keys, tile_values, tile_lengths, out_weight
):
    owners = lax.axis_size("owner")
    ranks = lax.axis_size("kvh")
    cores = 2
    chips = ranks // cores
    side = math.isqrt(owners)
    parts, new, group, width = queries.shape
    per_owner = tile_keys.shape[0]
    scale = width**-0.5 * LOG2
    rows = parts * new * group

    def along(x, leg, step):
        pairs = []
        for o in range(owners):
            y, z = divmod(o, side)
            for k in range(ranks):
                if (k % cores + leg) % 2 == 0:
                    to = y * side + (z + step) % side
                else:
                    to = (y + step) % side * side + z
                pairs.append((o * ranks + k, to * ranks + k))
        return lax.ppermute(x, ("owner", "kvh"), pairs)

    home = pack(queries.reshape(rows, width), ancestors)
    near = [along(home, 0, d) for d in range(1, side)]
    keys, values, own = prepare(
        tile_lengths,
        queries.reshape(parts, new * group, width),
        new_keys[:, :, 0],
        new_values[:, :, 0],
        tile_keys[:, 0],
        tile_values[:, 0],
        scale,
        group,
    )
    row, keys, values = lax.optimization_barrier((jnp.stack(near + [home]), keys, values))
    order = sorted(range(side), key=lambda e: min(e, side - e))
    blocks = {e: along(row, 1, e) if e else row for e in order[:-1]}
    outs = None
    for i, e in enumerate(order):
        if i == 1:
            late, outs = lax.optimization_barrier((row, outs))
            blocks[order[-1]] = along(late, 1, order[-1])
        block = blocks[e]
        if e:
            block, outs = lax.optimization_barrier((block, outs))
        last = i == side - 1
        outs = attend(block, keys, values, tile_lengths, scale, parts, 2 if last else 1)
        back = [along(out, 1, -e) for out in outs] if e else outs
        if not last:
            merged = merge(merged, back[0]) if e else back[0]
    ready = []
    for piece in back:
        ready += merge(merged, piece, len(ready), True)
    final = [ready[-1]] + [along(ready[d - 1], 0, -d) for d in range(1, side)]
    keep, give = project(final, own, out_weight, group, ranks, cores)
    got = lax.ppermute(give, "kvh", [(k, k // cores * cores + (k + 1) % cores) for k in range(ranks)])
    share = keep.shape[0] // chips
    pieces = [
        keep[d * share : (d + 1) * share].astype(F32) + got[d * share : (d + 1) * share].astype(F32) for d in range(chips)
    ]
    result = pieces[0]
    for d in sorted(range(1, chips), key=lambda d: min(d, chips - d)):
        pairs = [(k, (k + d * cores) % ranks) for k in range(ranks)]
        result = result + lax.ppermute(pieces[d].astype(BF16), "kvh", pairs).astype(F32)
    return result.astype(BF16)


def solution(mesh):
    return jax.shard_map(
        local,
        mesh=mesh,
        in_specs=(
            P("owner", None, "kvh", None),
            P("owner", None, "kvh", None),
            P("owner", None, "kvh", None),
            P("owner", None),
            P("owner", "kvh", None, None),
            P("owner", "kvh", None, None),
            P("owner"),
            P("kvh", None),
        ),
        out_specs=P(("owner", "kvh"), None),
        check_vma=False,
    )
```

```python
import functools
import math

import jax
import jax.numpy as jnp
from jax import lax
from jax.experimental import pallas as pl
from jax.experimental.pallas import tpu as pltpu
from jax.sharding import PartitionSpec as P

NEG = -1e30
META = 16
STEP = 256
FEW = 2
F32 = jnp.float32
BF16 = jnp.bfloat16
VMEM = pl.BlockSpec(memory_space=pltpu.VMEM)
SMEM = pl.BlockSpec(memory_space=pltpu.SMEM)
ANY = pl.BlockSpec(memory_space=pl.ANY)
LOG2 = 1.0 / math.log(2.0)


def to_lanes(column, count):
    r = lax.broadcasted_iota(jnp.int32, (128, 128), 0)
    c = lax.broadcasted_iota(jnp.int32, (128, 128), 1)
    eye = r == c
    rows = []
    for b in range(count // 128):
        rows.append(jnp.sum(jnp.where(eye, column[b * 128 : (b + 1) * 128], 0.0), axis=0, keepdims=True))
    return rows


def in_parts(lines):
    pieces = []
    for line in lines:
        high = line.astype(BF16).astype(F32)
        mid = (line - high).astype(BF16).astype(F32)
        pieces += [high, mid, line - high - mid]
    pad = jnp.zeros((META - len(pieces), 128), F32)
    return jnp.concatenate(pieces + [pad], axis=0).astype(BF16)


def levels(meta, b):
    return meta[3 * b : 3 * b + 1] + meta[3 * b + 1 : 3 * b + 2] + meta[3 * b + 2 : 3 * b + 3]


def pack_kernel(q_any, a_any, o_ref, a_ref, meta_ref, q_sem, a_sem):
    rows = q_any.shape[0]
    q_copy = pltpu.make_async_copy(q_any, o_ref.at[pl.ds(0, rows)], q_sem)
    a_copy = pltpu.make_async_copy(a_any, a_ref, a_sem)
    q_copy.start()
    a_copy.start()
    meta_ref[...] = jnp.full(meta_ref.shape, -1.0, F32)
    a_copy.wait()
    meta_ref[: a_ref.shape[0], : a_ref.shape[1]] = a_ref[...].astype(F32)
    o_ref[rows:, :] = meta_ref[...].astype(BF16)
    q_copy.wait()


def pack(q, ancestors):
    rows, width = q.shape
    return pl.pallas_call(
        pack_kernel,
        out_shape=jax.ShapeDtypeStruct((rows + META, width), BF16),
        in_specs=[ANY] * 2,
        out_specs=VMEM,
        scratch_shapes=[
            pltpu.VMEM(ancestors.shape, jnp.int32),
            pltpu.VMEM((META, width), F32),
            pltpu.SemaphoreType.DMA,
            pltpu.SemaphoreType.DMA,
        ],
        compiler_params=pltpu.CompilerParams(vmem_limit_bytes=4 << 20),
        cost_estimate=pl.CostEstimate(flops=1 << 10, bytes_accessed=1 << 18, transcendentals=0),
        name="pack",
    )(*(pltpu.with_memory_space_constraint(a, pltpu.HBM) for a in (q, ancestors)))


def prepare_kernel(scale, group, lengths, *refs):
    given, (kt_ref, va_ref, o_ref), held, sems = refs[:5], refs[5:8], refs[8:13], refs[13:]
    copies = [pltpu.make_async_copy(a, b, sem) for a, b, sem in zip(given, held, sems)]
    for copy in copies:
        copy.start()
    q_ref, nk_ref, nv_ref, k_ref, v_ref = held
    tiles, size, width = k_ref.shape
    for copy in copies:
        copy.wait()

    @pl.loop(0, tiles)
    def _(t):
        live = lax.broadcasted_iota(jnp.int32, (size, width), 0) < lengths[t]
        k = k_ref[t].astype(F32)
        kt_ref[t] = jnp.where(live, k, k[:1]).T.astype(BF16)
        va_ref[t, :, :width] = jnp.where(live, v_ref[t].astype(F32), 0.0).astype(BF16)
        va_ref[t, :, width:] = live.astype(F32).astype(BF16)

    halves, part, _ = q_ref.shape
    new = nk_ref.shape[1]
    rows = halves * part
    for i in range(halves):
        s = lax.dot_general(q_ref[i], nk_ref[i], (((1,), (1,)), ((), ())), preferred_element_type=F32)
        token = lax.broadcasted_iota(jnp.int32, (part, new), 0) // group
        seen = token >= lax.broadcasted_iota(jnp.int32, (part, new), 1)
        s = jnp.where(seen, s, NEG)
        peak = jnp.max(s, axis=1, keepdims=True)
        weights = jnp.where(seen, jnp.exp2((s - peak) * scale), 0.0)
        total = jnp.sum(weights, axis=1, keepdims=True)
        summed = jnp.dot(weights.astype(BF16), nv_ref[i], preferred_element_type=F32)
        o_ref[i * part : (i + 1) * part, :] = summed / total
        level = peak * scale + jnp.log(total) * LOG2
        rowed = to_lanes(jnp.broadcast_to(level, (part, width)), part)
        for b, line in enumerate(rowed):
            at = rows + i * len(rowed) + b
            o_ref[at : at + 1, :] = line


def prepare(lengths, q, new_keys, new_values, keys, values, scale, group):
    halves, part, width = q.shape
    tiles, size, _ = keys.shape
    return pl.pallas_call(
        functools.partial(prepare_kernel, scale, group),
        out_shape=[
            jax.ShapeDtypeStruct((tiles, width, size), BF16),
            jax.ShapeDtypeStruct((tiles, size, 2 * width), BF16),
            jax.ShapeDtypeStruct((halves * part + 8, width), F32),
        ],
        in_specs=[SMEM] + [ANY] * 5,
        out_specs=[VMEM] * 3,
        scratch_shapes=[pltpu.VMEM(a.shape, BF16) for a in (q, new_keys, new_values, keys, values)]
        + [pltpu.SemaphoreType.DMA] * 5,
        compiler_params=pltpu.CompilerParams(vmem_limit_bytes=44 << 20),
        cost_estimate=pl.CostEstimate(flops=1 << 24, bytes_accessed=16 << 20, transcendentals=1 << 15),
        name="prepare",
    )(lengths, *(pltpu.with_memory_space_constraint(a, pltpu.HBM) for a in (q, new_keys, new_values, keys, values)))


def attend_kernel(
    scale, halves, lengths, q_ref, k_ref, v_ref, *refs
):
    homes, held, width = q_ref.shape
    pieces, (s_ref, m_ref, acc_ref, member) = refs[:-4], refs[-4:]
    o_refs = [piece.at[i] for piece in pieces for i in range(piece.shape[0])]
    rows = held - META
    tiles, _, size = k_ref.shape
    part = rows // halves
    count = homes * halves

    names = jnp.concatenate([q_ref[h, rows:, :].astype(F32)[:halves] for h in range(homes)], axis=0)
    first = (lax.axis_index("owner") * tiles).astype(F32)
    bit = lax.broadcasted_iota(jnp.int32, (count, 1), 0)
    for t in range(tiles):
        inside = jnp.max(jnp.where(names == first + t, 1.0, 0.0), axis=1, keepdims=True)
        power = (1 << bit).astype(F32)
        member[t] = jnp.sum(inside * power).astype(jnp.int32)
        member[tiles + t] = jnp.sum(inside).astype(jnp.int32)
    m_ref[...] = jnp.full(m_ref.shape, NEG, F32)
    acc_ref[...] = jnp.zeros(acc_ref.shape, F32)

    def for_each_tile(body):
        @pl.loop(0, tiles)
        def _(t):
            held_by = member[t]
            number = member[tiles + t]
            for n in range(1, size // STEP + 1):
                fits = lengths[t] > (n - 1) * STEP
                if n * STEP < size:
                    fits = fits & (lengths[t] <= n * STEP)

                @pl.when(fits & (number > FEW))
                def _():
                    every = [(slice(i * part, (i + 1) * part), (held_by >> i) & 1 > 0) for i in range(count)]
                    body(t, n * STEP, q_ref[:, :rows, :].reshape(homes * rows, width), slice(None), every)

                @pl.when(fits & (number > 0) & (number <= FEW))
                def _():
                    @pl.loop(0, count)
                    def _(i):
                        @pl.when((held_by >> i) & 1 > 0)
                        def _():
                            q = q_ref[i // halves, pl.ds(pl.multiple_of(i % halves * part, part), part), :]
                            body(t, n * STEP, q, pl.ds(pl.multiple_of(i * part, part), part), [(slice(None), True)])

    def score(t, wide, q, span, blocks):
        s = jnp.dot(q, k_ref[t, :, :wide], preferred_element_type=F32)
        s_ref[t, span, :wide] = s
        for here, inside in blocks:
            x = s[here, :128]
            for j in range(128, wide, 128):
                x = jnp.maximum(x, s[here, j : j + 128])
            if inside is True:
                m_ref[span, :] = jnp.maximum(m_ref[span, :], x)
            else:
                m_ref[here, :] = jnp.maximum(m_ref[here, :], jnp.where(inside, x, NEG))

    for_each_tile(score)
    peak = jnp.max(m_ref[...], axis=1, keepdims=True) * scale
    m_ref[...] = jnp.broadcast_to(peak, m_ref.shape)

    def weigh(t, wide, q, span, blocks):
        weights = []
        for here, inside in blocks:
            rows_here = span if inside is True else here
            shift = m_ref[rows_here, :]
            if inside is not True:
                shift = jnp.where(inside, shift, -NEG)
            weights.append(
                jnp.concatenate(
                    [jnp.exp2(s_ref[t, rows_here, j : j + 128] * scale - shift).astype(BF16) for j in range(0, wide, 128)],
                    axis=1,
                )
            )
        weights = weights[0] if len(weights) == 1 else jnp.concatenate(weights, axis=0)
        acc_ref[span, :] += jnp.dot(weights, v_ref[t, :wide, :], preferred_element_type=F32)

    for_each_tile(weigh)
    for h in range(homes):
        here = slice(h * rows, (h + 1) * rows)
        total = acc_ref[here, width:]
        o_refs[h][:rows, :] = (acc_ref[here, :width] / jnp.maximum(total, -1.0 / NEG)).astype(BF16)
        sums = jnp.concatenate(to_lanes(total, rows), axis=0)
        peaks = jnp.concatenate(to_lanes(m_ref[here, :], rows), axis=0)
        level = jnp.where(sums > 0.0, peaks + jnp.log(jnp.maximum(sums, -1.0 / NEG)) * LOG2, NEG)
        o_refs[h][rows:, :] = in_parts([level[b : b + 1] for b in range(rows // 128)])


def attend(q, keys, values, lengths, scale, halves, pieces=1):
    homes, held, width = q.shape
    tiles, _, size = keys.shape
    rows = held - META
    return pl.pallas_call(
        functools.partial(attend_kernel, scale, halves),
        out_shape=[jax.ShapeDtypeStruct((homes // pieces, held, width), BF16)] * pieces,
        in_specs=[SMEM, VMEM, VMEM, VMEM],
        out_specs=[VMEM] * pieces,
        scratch_shapes=[
            pltpu.VMEM((tiles, homes * rows, size), F32),
            pltpu.VMEM((homes * rows, 128), F32),
            pltpu.VMEM((homes * rows, 2 * width), F32),
            pltpu.SMEM((2 * tiles,), jnp.int32),
        ],
        compiler_params=pltpu.CompilerParams(vmem_limit_bytes=44 << 20),
        cost_estimate=pl.CostEstimate(flops=1 << 20, bytes_accessed=1 << 18, transcendentals=0),
        name="attend",
    )(lengths, q, keys, values)


def weights_of(lines):
    level = jnp.concatenate(lines + [jnp.full((128 - len(lines), 128), 2 * NEG, F32)], axis=0)
    top = jnp.max(level, axis=0, keepdims=True)
    weight = jnp.exp2(level - top)
    total = jnp.sum(weight, axis=0, keepdims=True)
    return (weight / total).T, top + jnp.log(total) * LOG2


def merge_kernel(first, one_ref, two_ref, *o_refs):
    homes, held, _ = two_ref.shape
    if len(o_refs) == 1:
        o_refs = [o_refs[0].at[h] for h in range(homes)]
    rows = held - META
    for h in range(homes):
        given = [one_ref.at[first + h], two_ref.at[h]]
        metas = [a[rows:, :].astype(F32) for a in given]
        lines = []
        for b in range(rows // 128):
            weight, line = weights_of([levels(meta, b) for meta in metas])
            lines.append(line)
            here = slice(b * 128, (b + 1) * 128)
            acc = given[0][here, :].astype(F32) * weight[:, 0:1] + given[1][here, :].astype(F32) * weight[:, 1:2]
            o_refs[h][here, :] = acc.astype(BF16)
        o_refs[h][rows:, :] = in_parts(lines)


def merge(one, two, first=0, apart=False):
    homes, held, width = two.shape
    out = [jax.ShapeDtypeStruct((held, width), BF16)] * homes if apart else jax.ShapeDtypeStruct(two.shape, BF16)
    return pl.pallas_call(
        functools.partial(merge_kernel, first),
        out_shape=out,
        in_specs=[VMEM] * 2,
        out_specs=[VMEM] * homes if apart else VMEM,
        compiler_params=pltpu.CompilerParams(vmem_limit_bytes=16 << 20),
        cost_estimate=pl.CostEstimate(flops=1 << 30, bytes_accessed=1 << 18, transcendentals=0),
        name="merge",
    )(one, two)


def project_kernel(group, ranks, cores, *refs):
    a_refs, (own_ref, w_ref, keep_ref, give_ref, sum_ref, all_ref, flat_ref, held_ref, sems) = refs[:-9], refs[-9:]
    blocks, _, block = held_ref.shape
    copies = [
        pltpu.make_async_copy(w_ref.at[:, pl.ds(j * block, block)], held_ref.at[j], sems.at[j]) for j in range(blocks)
    ]
    for copy in copies:
        copy.start()
    rows, width = sum_ref.shape
    metas = [a[rows:, :].astype(F32) for a in a_refs]
    for b in range(rows // 128):
        weight, _ = weights_of([own_ref[rows + b : rows + b + 1, :]] + [levels(meta, b) for meta in metas])
        here = slice(b * 128, (b + 1) * 128)
        acc = own_ref[here, :] * weight[:, 0:1]
        for i, a in enumerate(a_refs):
            acc = acc + a[here, :].astype(F32) * weight[:, i + 1 : i + 2]
        sum_ref[here, :] = acc
    tokens = rows // group
    for g in range(group):
        all_ref[:, g * width : (g + 1) * width] = sum_ref[pl.ds(g, tokens, stride=group), :]
    chips = ranks // cores
    share = tokens // ranks
    rank = lax.axis_index("kvh")
    chip, core = rank // cores, rank % cores
    for i in range(cores):
        for d in range(chips):
            to = ((chip + d) % chips) * cores + (core + i) % cores
            at = (i * chips + d) * share
            flat_ref[at : at + share, :] = all_ref[pl.ds(pl.multiple_of(to * share, share), share), :]
    flat = flat_ref[...].astype(BF16)
    half = tokens // cores
    for j, copy in enumerate(copies):
        copy.wait()
        out = jnp.dot(flat, held_ref[j], preferred_element_type=F32).astype(BF16)
        keep_ref[:, j * block : (j + 1) * block] = out[:half]
        give_ref[:, j * block : (j + 1) * block] = out[half:]


def project(parts, own, weight, group, ranks, cores):
    held, width = parts[0].shape
    rows = held - META
    depth, columns = weight.shape
    tokens = rows // group
    block = 1024
    return pl.pallas_call(
        functools.partial(project_kernel, group, ranks, cores),
        out_shape=[jax.ShapeDtypeStruct((tokens // cores, columns), BF16)] * 2,
        in_specs=[VMEM] * (len(parts) + 1) + [ANY],
        out_specs=[VMEM] * 2,
        scratch_shapes=[
            pltpu.VMEM((rows, width), F32),
            pltpu.VMEM((tokens, depth), F32),
            pltpu.VMEM((tokens, depth), F32),
            pltpu.VMEM((columns // block, depth, block), BF16),
            pltpu.SemaphoreType.DMA((columns // block,)),
        ],
        compiler_params=pltpu.CompilerParams(vmem_limit_bytes=50 << 20),
        cost_estimate=pl.CostEstimate(flops=1 << 30, bytes_accessed=18 << 20, transcendentals=1 << 14),
        name="project",
    )(*parts, own, weight)


def local(
    queries, new_keys, new_values, ancestors, tile_keys, tile_values, tile_lengths, out_weight
):
    owners = lax.axis_size("owner")
    ranks = lax.axis_size("kvh")
    cores = 2
    chips = ranks // cores
    side = math.isqrt(owners)
    parts, new, group, width = queries.shape
    per_owner = tile_keys.shape[0]
    scale = width**-0.5 * LOG2
    rows = parts * new * group

    def along(x, leg, step):
        pairs = []
        for o in range(owners):
            y, z = divmod(o, side)
            for k in range(ranks):
                if (k % cores + leg) % 2 == 0:
                    to = y * side + (z + step) % side
                else:
                    to = (y + step) % side * side + z
                pairs.append((o * ranks + k, to * ranks + k))
        return lax.ppermute(x, ("owner", "kvh"), pairs)

    home = pack(queries.reshape(rows, width), ancestors)
    near = [along(home, 0, d) for d in range(1, side)]
    keys, values, own = prepare(
        tile_lengths,
        queries.reshape(parts, new * group, width),
        new_keys[:, :, 0],
        new_values[:, :, 0],
        tile_keys[:, 0],
        tile_values[:, 0],
        scale,
        group,
    )
    row, keys, values = lax.optimization_barrier((jnp.stack(near + [home]), keys, values))
    order = sorted(range(side), key=lambda e: min(e, side - e))
    blocks = {e: along(row, 1, e) if e else row for e in order[:-1]}
    outs = None
    for i, e in enumerate(order):
        if i == 1:
            late, outs = lax.optimization_barrier((row, outs))
            blocks[order[-1]] = along(late, 1, order[-1])
        block = blocks[e]
        if e:
            block, outs = lax.optimization_barrier((block, outs))
        last = i == side - 1
        outs = attend(block, keys, values, tile_lengths, scale, parts, 2 if last else 1)
        back = [along(out, 1, -e) for out in outs] if e else outs
        if not last:
            merged = merge(merged, back[0]) if e else back[0]
    ready = []
    for piece in back:
        ready += merge(merged, piece, len(ready), True)
    final = [ready[-1]] + [along(ready[d - 1], 0, -d) for d in range(1, side)]
    keep, give = project(final, own, out_weight, group, ranks, cores)
    got = lax.ppermute(give, "kvh", [(k, k // cores * cores + (k + 1) % cores) for k in range(ranks)])
    share = keep.shape[0] // chips
    pieces = [
        keep[d * share : (d + 1) * share].astype(F32) + got[d * share : (d + 1) * share].astype(F32) for d in range(chips)
    ]
    result = pieces[0]
    for d in sorted(range(1, chips), key=lambda d: min(d, chips - d)):
        pairs = [(k, (k + d * cores) % ranks) for k in range(ranks)]
        result = result + lax.ppermute(pieces[d].astype(BF16), "kvh", pairs).astype(F32)
    return result.astype(BF16)


def solution(mesh):
    return jax.shard_map(
        local,
        mesh=mesh,
        in_specs=(
            P("owner", None, "kvh", None),
            P("owner", None, "kvh", None),
            P("owner", None, "kvh", None),
            P("owner", None),
            P("owner", "kvh", None, None),
            P("owner", "kvh", None, None),
            P("owner"),
            P("kvh", None),
        ),
        out_specs=P(("owner", "kvh"), None),
        check_vma=False,
    )
```

```python
import functools
import math

import jax
import jax.numpy as jnp
from jax import lax
from jax.experimental import pallas as pl
from jax.experimental.pallas import tpu as pltpu
from jax.sharding import PartitionSpec as P

NEG = -1e30
META = 16
STEP = 256
FEW = 2
F32 = jnp.float32
BF16 = jnp.bfloat16
VMEM = pl.BlockSpec(memory_space=pltpu.VMEM)
SMEM = pl.BlockSpec(memory_space=pltpu.SMEM)
ANY = pl.BlockSpec(memory_space=pl.ANY)
LOG2 = 1.0 / math.log(2.0)


def to_lanes(column, count):
    r = lax.broadcasted_iota(jnp.int32, (128, 128), 0)
    c = lax.broadcasted_iota(jnp.int32, (128, 128), 1)
    eye = r == c
    rows = []
    for b in range(count // 128):
        rows.append(jnp.sum(jnp.where(eye, column[b * 128 : (b + 1) * 128], 0.0), axis=0, keepdims=True))
    return rows


def in_parts(lines):
    pieces = []
    for line in lines:
        high = line.astype(BF16).astype(F32)
        mid = (line - high).astype(BF16).astype(F32)
        pieces += [high, mid, line - high - mid]
    pad = jnp.zeros((META - len(pieces), 128), F32)
    return jnp.concatenate(pieces + [pad], axis=0).astype(BF16)


def levels(meta, b):
    return meta[3 * b : 3 * b + 1] + meta[3 * b + 1 : 3 * b + 2] + meta[3 * b + 2 : 3 * b + 3]


def pack_kernel(q_any, a_any, o_ref, a_ref, meta_ref, q_sem, a_sem):
    rows = q_any.shape[0]
    q_copy = pltpu.make_async_copy(q_any, o_ref.at[pl.ds(0, rows)], q_sem)
    a_copy = pltpu.make_async_copy(a_any, a_ref, a_sem)
    q_copy.start()
    a_copy.start()
    meta_ref[...] = jnp.full(meta_ref.shape, -1.0, F32)
    a_copy.wait()
    meta_ref[: a_ref.shape[0], : a_ref.shape[1]] = a_ref[...].astype(F32)
    o_ref[rows:, :] = meta_ref[...].astype(BF16)
    q_copy.wait()


def pack(q, ancestors):
    rows, width = q.shape
    return pl.pallas_call(
        pack_kernel,
        out_shape=jax.ShapeDtypeStruct((rows + META, width), BF16),
        in_specs=[ANY] * 2,
        out_specs=VMEM,
        scratch_shapes=[
            pltpu.VMEM(ancestors.shape, jnp.int32),
            pltpu.VMEM((META, width), F32),
            pltpu.SemaphoreType.DMA,
            pltpu.SemaphoreType.DMA,
        ],
        compiler_params=pltpu.CompilerParams(vmem_limit_bytes=4 << 20),
        cost_estimate=pl.CostEstimate(flops=1 << 10, bytes_accessed=1 << 18, transcendentals=0),
        name="pack",
    )(*(pltpu.with_memory_space_constraint(a, pltpu.HBM) for a in (q, ancestors)))


def prepare_kernel(scale, group, lengths, *refs):
    given, (kt_ref, va_ref, o_ref), held, sems = refs[:5], refs[5:8], refs[8:13], refs[13:]
    copies = [pltpu.make_async_copy(a, b, sem) for a, b, sem in zip(given, held, sems)]
    for copy in copies:
        copy.start()
    q_ref, nk_ref, nv_ref, k_ref, v_ref = held
    tiles, size, width = k_ref.shape
    for copy in copies:
        copy.wait()

    @pl.loop(0, tiles)
    def _(t):
        live = lax.broadcasted_iota(jnp.int32, (size, width), 0) < lengths[t]
        k = k_ref[t].astype(F32)
        kt_ref[t] = jnp.where(live, k, k[:1]).T.astype(BF16)
        va_ref[t, :, :width] = jnp.where(live, v_ref[t].astype(F32), 0.0).astype(BF16)
        va_ref[t, :, width:] = live.astype(F32).astype(BF16)

    halves, part, _ = q_ref.shape
    new = nk_ref.shape[1]
    rows = halves * part
    for i in range(halves):
        s = lax.dot_general(q_ref[i], nk_ref[i], (((1,), (1,)), ((), ())), preferred_element_type=F32)
        token = lax.broadcasted_iota(jnp.int32, (part, new), 0) // group
        seen = token >= lax.broadcasted_iota(jnp.int32, (part, new), 1)
        s = jnp.where(seen, s, NEG)
        peak = jnp.max(s, axis=1, keepdims=True)
        weights = jnp.where(seen, jnp.exp2((s - peak) * scale), 0.0)
        total = jnp.sum(weights, axis=1, keepdims=True)
        summed = jnp.dot(weights.astype(BF16), nv_ref[i], preferred_element_type=F32)
        o_ref[i * part : (i + 1) * part, :] = summed / total
        level = peak * scale + jnp.log(total) * LOG2
        rowed = to_lanes(jnp.broadcast_to(level, (part, width)), part)
        for b, line in enumerate(rowed):
            at = rows + i * len(rowed) + b
            o_ref[at : at + 1, :] = line


def prepare(lengths, q, new_keys, new_values, keys, values, scale, group):
    halves, part, width = q.shape
    tiles, size, _ = keys.shape
    return pl.pallas_call(
        functools.partial(prepare_kernel, scale, group),
        out_shape=[
            jax.ShapeDtypeStruct((tiles, width, size), BF16),
            jax.ShapeDtypeStruct((tiles, size, 2 * width), BF16),
            jax.ShapeDtypeStruct((halves * part + 8, width), F32),
        ],
        in_specs=[SMEM] + [ANY] * 5,
        out_specs=[VMEM] * 3,
        scratch_shapes=[pltpu.VMEM(a.shape, BF16) for a in (q, new_keys, new_values, keys, values)]
        + [pltpu.SemaphoreType.DMA] * 5,
        compiler_params=pltpu.CompilerParams(vmem_limit_bytes=44 << 20),
        cost_estimate=pl.CostEstimate(flops=1 << 24, bytes_accessed=16 << 20, transcendentals=1 << 15),
        name="prepare",
    )(lengths, *(pltpu.with_memory_space_constraint(a, pltpu.HBM) for a in (q, new_keys, new_values, keys, values)))


def attend_kernel(
    scale, halves, lengths, q_ref, k_ref, v_ref, *refs
):
    homes, held, width = q_ref.shape
    pieces, (s_ref, m_ref, acc_ref, member) = refs[:-4], refs[-4:]
    o_refs = [piece.at[i] for piece in pieces for i in range(piece.shape[0])]
    rows = held - META
    tiles, _, size = k_ref.shape
    part = rows // halves
    count = homes * halves

    names = jnp.concatenate([q_ref[h, rows:, :].astype(F32)[:halves] for h in range(homes)], axis=0)
    first = (lax.axis_index("owner") * tiles).astype(F32)
    bit = lax.broadcasted_iota(jnp.int32, (count, 1), 0)
    for t in range(tiles):
        inside = jnp.max(jnp.where(names == first + t, 1.0, 0.0), axis=1, keepdims=True)
        power = (1 << bit).astype(F32)
        member[t] = jnp.sum(inside * power).astype(jnp.int32)
        member[tiles + t] = jnp.sum(inside).astype(jnp.int32)
    m_ref[...] = jnp.full(m_ref.shape, NEG, F32)
    acc_ref[...] = jnp.zeros(acc_ref.shape, F32)

    def for_each_tile(body):
        @pl.loop(0, tiles)
        def _(t):
            held_by = member[t]
            number = member[tiles + t]
            for n in range(1, size // STEP + 1):
                fits = lengths[t] > (n - 1) * STEP
                if n * STEP < size:
                    fits = fits & (lengths[t] <= n * STEP)

                @pl.when(fits & (number > FEW))
                def _():
                    every = [(slice(i * part, (i + 1) * part), (held_by >> i) & 1 > 0) for i in range(count)]
                    body(t, n * STEP, q_ref[:, :rows, :].reshape(homes * rows, width), slice(None), every)

                @pl.when(fits & (number > 0) & (number <= FEW))
                def _():
                    @pl.loop(0, count)
                    def _(i):
                        @pl.when((held_by >> i) & 1 > 0)
                        def _():
                            q = q_ref[i // halves, pl.ds(pl.multiple_of(i % halves * part, part), part), :]
                            body(t, n * STEP, q, pl.ds(pl.multiple_of(i * part, part), part), [(slice(None), True)])

    def score(t, wide, q, span, blocks):
        s = jnp.dot(q, k_ref[t, :, :wide], preferred_element_type=F32)
        s_ref[t, span, :wide] = s
        for here, inside in blocks:
            x = s[here, :128]
            for j in range(128, wide, 128):
                x = jnp.maximum(x, s[here, j : j + 128])
            if inside is True:
                m_ref[span, :] = jnp.maximum(m_ref[span, :], x)
            else:
                m_ref[here, :] = jnp.maximum(m_ref[here, :], jnp.where(inside, x, NEG))

    for_each_tile(score)
    peak = jnp.max(m_ref[...], axis=1, keepdims=True) * scale
    m_ref[...] = jnp.broadcast_to(peak, m_ref.shape)

    def weigh(t, wide, q, span, blocks):
        weights = []
        for here, inside in blocks:
            rows_here = span if inside is True else here
            shift = m_ref[rows_here, :]
            if inside is not True:
                shift = jnp.where(inside, shift, -NEG)
            weights.append(
                jnp.concatenate(
                    [jnp.exp2(s_ref[t, rows_here, j : j + 128] * scale - shift).astype(BF16) for j in range(0, wide, 128)],
                    axis=1,
                )
            )
        weights = weights[0] if len(weights) == 1 else jnp.concatenate(weights, axis=0)
        acc_ref[span, :] += jnp.dot(weights, v_ref[t, :wide, :], preferred_element_type=F32)

    for_each_tile(weigh)
    for h in range(homes):
        here = slice(h * rows, (h + 1) * rows)
        total = acc_ref[here, width:]
        o_refs[h][:rows, :] = (acc_ref[here, :width] / jnp.maximum(total, -1.0 / NEG)).astype(BF16)
        sums = jnp.concatenate(to_lanes(total, rows), axis=0)
        peaks = jnp.concatenate(to_lanes(m_ref[here, :], rows), axis=0)
        level = jnp.where(sums > 0.0, peaks + jnp.log(jnp.maximum(sums, -1.0 / NEG)) * LOG2, NEG)
        o_refs[h][rows:, :] = in_parts([level[b : b + 1] for b in range(rows // 128)])


def attend(q, keys, values, lengths, scale, halves, pieces):
    homes, held, width = q.shape
    tiles, _, size = keys.shape
    rows = held - META
    return pl.pallas_call(
        functools.partial(attend_kernel, scale, halves),
        out_shape=[jax.ShapeDtypeStruct((piece, held, width), BF16) for piece in pieces],
        in_specs=[SMEM, VMEM, VMEM, VMEM],
        out_specs=[VMEM] * len(pieces),
        scratch_shapes=[
            pltpu.VMEM((tiles, homes * rows, size), F32),
            pltpu.VMEM((homes * rows, 128), F32),
            pltpu.VMEM((homes * rows, 2 * width), F32),
            pltpu.SMEM((2 * tiles,), jnp.int32),
        ],
        compiler_params=pltpu.CompilerParams(vmem_limit_bytes=44 << 20),
        cost_estimate=pl.CostEstimate(flops=1 << 20, bytes_accessed=1 << 18, transcendentals=0),
        name="attend",
    )(lengths, q, keys, values)


def weights_of(lines):
    level = jnp.concatenate(lines + [jnp.full((128 - len(lines), 128), 2 * NEG, F32)], axis=0)
    top = jnp.max(level, axis=0, keepdims=True)
    weight = jnp.exp2(level - top)
    total = jnp.sum(weight, axis=0, keepdims=True)
    return (weight / total).T, top + jnp.log(total) * LOG2


def merge_kernel(one_ref, two_ref, *refs):
    homes, held, _ = two_ref.shape
    o_refs = [ref.at[i] for ref in refs for i in range(ref.shape[0])]
    rows = held - META
    for h in range(homes):
        given = [one_ref.at[h], two_ref.at[h]]
        metas = [a[rows:, :].astype(F32) for a in given]
        lines = []
        for b in range(rows // 128):
            weight, line = weights_of([levels(meta, b) for meta in metas])
            lines.append(line)
            here = slice(b * 128, (b + 1) * 128)
            acc = given[0][here, :].astype(F32) * weight[:, 0:1] + given[1][here, :].astype(F32) * weight[:, 1:2]
            o_refs[h][here, :] = acc.astype(BF16)
        o_refs[h][rows:, :] = in_parts(lines)


def merge(one, two, pieces):
    _, held, width = two.shape
    return pl.pallas_call(
        merge_kernel,
        out_shape=[jax.ShapeDtypeStruct((piece, held, width), BF16) for piece in pieces],
        in_specs=[VMEM] * 2,
        out_specs=[VMEM] * len(pieces),
        compiler_params=pltpu.CompilerParams(vmem_limit_bytes=16 << 20),
        cost_estimate=pl.CostEstimate(flops=1 << 30, bytes_accessed=1 << 18, transcendentals=0),
        name="merge",
    )(one, two)


def project_kernel(group, ranks, cores, *refs):
    a_refs, (own_ref, w_ref, keep_ref, give_ref, sum_ref, all_ref, flat_ref, held_ref, sems) = refs[:-9], refs[-9:]
    a_refs = [a.at[0] for a in a_refs]
    blocks, _, block = held_ref.shape
    copies = [
        pltpu.make_async_copy(w_ref.at[:, pl.ds(j * block, block)], held_ref.at[j], sems.at[j]) for j in range(blocks)
    ]
    for copy in copies:
        copy.start()
    rows, width = sum_ref.shape
    metas = [a[rows:, :].astype(F32) for a in a_refs]
    for b in range(rows // 128):
        weight, _ = weights_of([own_ref[rows + b : rows + b + 1, :]] + [levels(meta, b) for meta in metas])
        here = slice(b * 128, (b + 1) * 128)
        acc = own_ref[here, :] * weight[:, 0:1]
        for i, a in enumerate(a_refs):
            acc = acc + a[here, :].astype(F32) * weight[:, i + 1 : i + 2]
        sum_ref[here, :] = acc
    tokens = rows // group
    for g in range(group):
        all_ref[:, g * width : (g + 1) * width] = sum_ref[pl.ds(g, tokens, stride=group), :]
    chips = ranks // cores
    share = tokens // ranks
    rank = lax.axis_index("kvh")
    chip, core = rank // cores, rank % cores
    for i in range(cores):
        for d in range(chips):
            to = ((chip + d) % chips) * cores + (core + i) % cores
            at = (i * chips + d) * share
            flat_ref[at : at + share, :] = all_ref[pl.ds(pl.multiple_of(to * share, share), share), :]
    flat = flat_ref[...].astype(BF16)
    half = tokens // cores
    for j, copy in enumerate(copies):
        copy.wait()
        out = jnp.dot(flat, held_ref[j], preferred_element_type=F32).astype(BF16)
        keep_ref[:, j * block : (j + 1) * block] = out[:half]
        give_ref[:, j * block : (j + 1) * block] = out[half:]


def project(parts, own, weight, group, ranks, cores):
    _, held, width = parts[0].shape
    rows = held - META
    depth, columns = weight.shape
    tokens = rows // group
    block = 1024
    return pl.pallas_call(
        functools.partial(project_kernel, group, ranks, cores),
        out_shape=[jax.ShapeDtypeStruct((tokens // cores, columns), BF16)] * 2,
        in_specs=[VMEM] * (len(parts) + 1) + [ANY],
        out_specs=[VMEM] * 2,
        scratch_shapes=[
            pltpu.VMEM((rows, width), F32),
            pltpu.VMEM((tokens, depth), F32),
            pltpu.VMEM((tokens, depth), F32),
            pltpu.VMEM((columns // block, depth, block), BF16),
            pltpu.SemaphoreType.DMA((columns // block,)),
        ],
        compiler_params=pltpu.CompilerParams(vmem_limit_bytes=50 << 20),
        cost_estimate=pl.CostEstimate(flops=1 << 30, bytes_accessed=18 << 20, transcendentals=1 << 14),
        name="project",
    )(*parts, own, weight)


def local(
    queries, new_keys, new_values, ancestors, tile_keys, tile_values, tile_lengths, out_weight
):
    owners = lax.axis_size("owner")
    ranks = lax.axis_size("kvh")
    cores = 2
    chips = ranks // cores
    side = math.isqrt(owners)
    parts, new, group, width = queries.shape
    per_owner = tile_keys.shape[0]
    scale = width**-0.5 * LOG2
    rows = parts * new * group

    def along(x, *steps):
        pairs = []
        for o in range(owners):
            for k in range(ranks):
                dz, dy = steps if k % cores == 0 else steps[::-1]
                y, z = (o // side + dy) % side, (o + dz) % side
                pairs.append((o * ranks + k, (y * side + z) * ranks + k))
        return lax.ppermute(x, ("owner", "kvh"), pairs)

    home = pack(queries.reshape(rows, width), ancestors)
    near = [along(home, d, 0) for d in range(1, side)]
    keys, values, own = prepare(
        tile_lengths,
        queries.reshape(parts, new * group, width),
        new_keys[:, :, 0],
        new_values[:, :, 0],
        tile_keys[:, 0],
        tile_values[:, 0],
        scale,
        group,
    )
    row, keys, values = lax.optimization_barrier((jnp.stack(near + [home]), keys, values))
    order = sorted(range(side), key=lambda e: min(e, side - e))
    blocks = {e: along(row, 0, e) if e else row for e in order[:-1]}
    outs = None
    for i, e in enumerate(order):
        if i == 1:
            late, outs = lax.optimization_barrier((row, outs))
            blocks[order[-1]] = along(late, 0, order[-1])
        block = blocks[e]
        if e:
            block, outs = lax.optimization_barrier((block, outs))
        last = i == side - 1
        pieces = (side - 2, 1, 1) if last else (side,)
        outs = attend(block, keys, values, tile_lengths, scale, parts, pieces)
        if i == 0:
            merged = outs
        elif not last:
            merged = merge(merged[0], along(outs[0], 0, -e), (side - 2, 1, 1) if i == side - 2 else (side,))
    two, three, here = outs
    far = along(merged[1], 1 - side, 0)
    straight = along(three, 1 - side, -e)
    here = merge(merged[2], along(here, 0, -e), (1,))[0]
    near = merge(merged[0], along(two, 0, -e), (1,) * (side - 2))
    final = [here, merge(far, straight, (1,))[0]] + [along(near[d - 1], -d, 0) for d in range(1, side - 1)]
    keep, give = project(final, own, out_weight, group, ranks, cores)
    got = lax.ppermute(give, "kvh", [(k, k // cores * cores + (k + 1) % cores) for k in range(ranks)])
    share = keep.shape[0] // chips
    pieces = [
        keep[d * share : (d + 1) * share].astype(F32) + got[d * share : (d + 1) * share].astype(F32) for d in range(chips)
    ]
    result = pieces[0]
    for d in sorted(range(1, chips), key=lambda d: min(d, chips - d)):
        pairs = [(k, (k + d * cores) % ranks) for k in range(ranks)]
        result = result + lax.ppermute(pieces[d].astype(BF16), "kvh", pairs).astype(F32)
    return result.astype(BF16)


def solution(mesh):
    return jax.shard_map(
        local,
        mesh=mesh,
        in_specs=(
            P("owner", None, "kvh", None),
            P("owner", None, "kvh", None),
            P("owner", None, "kvh", None),
            P("owner", None),
            P("owner", "kvh", None, None),
            P("owner", "kvh", None, None),
            P("owner"),
            P("kvh", None),
        ),
        out_specs=P(("owner", "kvh"), None),
        check_vma=False,
    )
```

```python
import functools
import math

import jax
import jax.numpy as jnp
from jax import lax
from jax.experimental import pallas as pl
from jax.experimental.pallas import tpu as pltpu
from jax.sharding import PartitionSpec as P

NEG = -1e30
META = 16
STEP = 256
FEW = 2
F32 = jnp.float32
BF16 = jnp.bfloat16
VMEM = pl.BlockSpec(memory_space=pltpu.VMEM)
SMEM = pl.BlockSpec(memory_space=pltpu.SMEM)
ANY = pl.BlockSpec(memory_space=pl.ANY)
LOG2 = 1.0 / math.log(2.0)


def to_lanes(column, count):
    r = lax.broadcasted_iota(jnp.int32, (128, 128), 0)
    c = lax.broadcasted_iota(jnp.int32, (128, 128), 1)
    eye = r == c
    rows = []
    for b in range(count // 128):
        rows.append(jnp.sum(jnp.where(eye, column[b * 128 : (b + 1) * 128], 0.0), axis=0, keepdims=True))
    return rows


def in_parts(lines):
    pieces = []
    for line in lines:
        high = line.astype(BF16).astype(F32)
        mid = (line - high).astype(BF16).astype(F32)
        pieces += [high, mid, line - high - mid]
    pad = jnp.zeros((META - len(pieces), 128), F32)
    return jnp.concatenate(pieces + [pad], axis=0).astype(BF16)


def levels(meta, b):
    return meta[3 * b : 3 * b + 1] + meta[3 * b + 1 : 3 * b + 2] + meta[3 * b + 2 : 3 * b + 3]


def pack_kernel(q_any, a_any, o_ref, a_ref, meta_ref, q_sem, a_sem):
    rows = q_any.shape[0]
    q_copy = pltpu.make_async_copy(q_any, o_ref.at[pl.ds(0, rows)], q_sem)
    a_copy = pltpu.make_async_copy(a_any, a_ref, a_sem)
    q_copy.start()
    a_copy.start()
    meta_ref[...] = jnp.full(meta_ref.shape, -1.0, F32)
    a_copy.wait()
    meta_ref[: a_ref.shape[0], : a_ref.shape[1]] = a_ref[...].astype(F32)
    o_ref[rows:, :] = meta_ref[...].astype(BF16)
    q_copy.wait()


def pack(q, ancestors):
    rows, width = q.shape
    return pl.pallas_call(
        pack_kernel,
        out_shape=jax.ShapeDtypeStruct((rows + META, width), BF16),
        in_specs=[ANY] * 2,
        out_specs=VMEM,
        scratch_shapes=[
            pltpu.VMEM(ancestors.shape, jnp.int32),
            pltpu.VMEM((META, width), F32),
            pltpu.SemaphoreType.DMA,
            pltpu.SemaphoreType.DMA,
        ],
        compiler_params=pltpu.CompilerParams(vmem_limit_bytes=4 << 20),
        cost_estimate=pl.CostEstimate(flops=1 << 10, bytes_accessed=1 << 18, transcendentals=0),
        name="pack",
    )(*(pltpu.with_memory_space_constraint(a, pltpu.HBM) for a in (q, ancestors)))


def prepare_kernel(scale, group, lengths, *refs):
    given, (kt_ref, va_ref, o_ref), held, sems = refs[:5], refs[5:8], refs[8:13], refs[13:]
    copies = [pltpu.make_async_copy(a, b, sem) for a, b, sem in zip(given, held, sems)]
    for copy in copies:
        copy.start()
    q_ref, nk_ref, nv_ref, k_ref, v_ref = held
    tiles, size, width = k_ref.shape
    for copy in copies:
        copy.wait()

    @pl.loop(0, tiles)
    def _(t):
        live = lax.broadcasted_iota(jnp.int32, (size, width), 0) < lengths[t]
        k = k_ref[t].astype(F32)
        kt_ref[t] = jnp.where(live, k, k[:1]).T.astype(BF16)
        va_ref[t, :, :width] = jnp.where(live, v_ref[t].astype(F32), 0.0).astype(BF16)
        va_ref[t, :, width:] = live.astype(F32).astype(BF16)

    halves, part, _ = q_ref.shape
    new = nk_ref.shape[1]
    rows = halves * part
    for i in range(halves):
        s = lax.dot_general(q_ref[i], nk_ref[i], (((1,), (1,)), ((), ())), preferred_element_type=F32)
        token = lax.broadcasted_iota(jnp.int32, (part, new), 0) // group
        seen = token >= lax.broadcasted_iota(jnp.int32, (part, new), 1)
        s = jnp.where(seen, s, NEG)
        peak = jnp.max(s, axis=1, keepdims=True)
        weights = jnp.where(seen, jnp.exp2((s - peak) * scale), 0.0)
        total = jnp.sum(weights, axis=1, keepdims=True)
        summed = jnp.dot(weights.astype(BF16), nv_ref[i], preferred_element_type=F32)
        o_ref[i * part : (i + 1) * part, :] = summed / total
        level = peak * scale + jnp.log(total) * LOG2
        rowed = to_lanes(jnp.broadcast_to(level, (part, width)), part)
        for b, line in enumerate(rowed):
            at = rows + i * len(rowed) + b
            o_ref[at : at + 1, :] = line


def prepare(lengths, q, new_keys, new_values, keys, values, scale, group):
    halves, part, width = q.shape
    tiles, size, _ = keys.shape
    return pl.pallas_call(
        functools.partial(prepare_kernel, scale, group),
        out_shape=[
            jax.ShapeDtypeStruct((tiles, width, size), BF16),
            jax.ShapeDtypeStruct((tiles, size, 2 * width), BF16),
            jax.ShapeDtypeStruct((halves * part + 8, width), F32),
        ],
        in_specs=[SMEM] + [ANY] * 5,
        out_specs=[VMEM] * 3,
        scratch_shapes=[pltpu.VMEM(a.shape, BF16) for a in (q, new_keys, new_values, keys, values)]
        + [pltpu.SemaphoreType.DMA] * 5,
        compiler_params=pltpu.CompilerParams(vmem_limit_bytes=44 << 20),
        cost_estimate=pl.CostEstimate(flops=1 << 24, bytes_accessed=16 << 20, transcendentals=1 << 15),
        name="prepare",
    )(lengths, *(pltpu.with_memory_space_constraint(a, pltpu.HBM) for a in (q, new_keys, new_values, keys, values)))


def attend_kernel(
    scale, halves, lengths, q_ref, k_ref, v_ref, *refs
):
    homes, held, width = q_ref.shape
    pieces, (s_ref, m_ref, acc_ref, member) = refs[:-4], refs[-4:]
    o_refs = [piece.at[i] for piece in pieces for i in range(piece.shape[0])]
    rows = held - META
    tiles, _, size = k_ref.shape
    part = rows // halves
    count = homes * halves

    names = jnp.concatenate([q_ref[h, rows:, :].astype(F32)[:halves] for h in range(homes)], axis=0)
    first = (lax.axis_index("owner") * tiles).astype(F32)
    bit = lax.broadcasted_iota(jnp.int32, (count, 1), 0)
    for t in range(tiles):
        inside = jnp.max(jnp.where(names == first + t, 1.0, 0.0), axis=1, keepdims=True)
        power = (1 << bit).astype(F32)
        member[t] = jnp.sum(inside * power).astype(jnp.int32)
        member[tiles + t] = jnp.sum(inside).astype(jnp.int32)
    m_ref[...] = jnp.full(m_ref.shape, NEG, F32)
    acc_ref[...] = jnp.zeros(acc_ref.shape, F32)

    def for_each_tile(body):
        @pl.loop(0, tiles)
        def _(t):
            held_by = member[t]
            number = member[tiles + t]
            for n in range(1, size // STEP + 1):
                fits = lengths[t] > (n - 1) * STEP
                if n * STEP < size:
                    fits = fits & (lengths[t] <= n * STEP)

                @pl.when(fits & (number > FEW))
                def _():
                    every = [(slice(i * part, (i + 1) * part), (held_by >> i) & 1 > 0) for i in range(count)]
                    body(t, n * STEP, q_ref[:, :rows, :].reshape(homes * rows, width), slice(None), every)

                @pl.when(fits & (number > 0) & (number <= FEW))
                def _():
                    @pl.loop(0, count)
                    def _(i):
                        @pl.when((held_by >> i) & 1 > 0)
                        def _():
                            q = q_ref[i // halves, pl.ds(pl.multiple_of(i % halves * part, part), part), :]
                            body(t, n * STEP, q, pl.ds(pl.multiple_of(i * part, part), part), [(slice(None), True)])

    def score(t, wide, q, span, blocks):
        s = jnp.dot(q, k_ref[t, :, :wide], preferred_element_type=F32)
        s_ref[t, span, :wide] = s
        for here, inside in blocks:
            x = s[here, :128]
            for j in range(128, wide, 128):
                x = jnp.maximum(x, s[here, j : j + 128])
            if inside is True:
                m_ref[span, :] = jnp.maximum(m_ref[span, :], x)
            else:
                m_ref[here, :] = jnp.maximum(m_ref[here, :], jnp.where(inside, x, NEG))

    for_each_tile(score)
    peak = jnp.max(m_ref[...], axis=1, keepdims=True) * scale
    m_ref[...] = jnp.broadcast_to(peak, m_ref.shape)

    def weigh(t, wide, q, span, blocks):
        weights = []
        for here, inside in blocks:
            rows_here = span if inside is True else here
            shift = m_ref[rows_here, :]
            if inside is not True:
                shift = jnp.where(inside, shift, -NEG)
            weights.append(
                jnp.concatenate(
                    [jnp.exp2(s_ref[t, rows_here, j : j + 128] * scale - shift).astype(BF16) for j in range(0, wide, 128)],
                    axis=1,
                )
            )
        weights = weights[0] if len(weights) == 1 else jnp.concatenate(weights, axis=0)
        acc_ref[span, :] += jnp.dot(weights, v_ref[t, :wide, :], preferred_element_type=F32)

    for_each_tile(weigh)
    for h in range(homes):
        here = slice(h * rows, (h + 1) * rows)
        total = acc_ref[here, width:]
        o_refs[h][:rows, :] = (acc_ref[here, :width] / jnp.maximum(total, -1.0 / NEG)).astype(BF16)
        sums = jnp.concatenate(to_lanes(total, rows), axis=0)
        peaks = jnp.concatenate(to_lanes(m_ref[here, :], rows), axis=0)
        level = jnp.where(sums > 0.0, peaks + jnp.log(jnp.maximum(sums, -1.0 / NEG)) * LOG2, NEG)
        o_refs[h][rows:, :] = in_parts([level[b : b + 1] for b in range(rows // 128)])


def attend(q, keys, values, lengths, scale, halves, pieces):
    homes, held, width = q.shape
    tiles, _, size = keys.shape
    rows = held - META
    return pl.pallas_call(
        functools.partial(attend_kernel, scale, halves),
        out_shape=[jax.ShapeDtypeStruct((piece, held, width), BF16) for piece in pieces],
        in_specs=[SMEM, VMEM, VMEM, VMEM],
        out_specs=[VMEM] * len(pieces),
        scratch_shapes=[
            pltpu.VMEM((tiles, homes * rows, size), F32),
            pltpu.VMEM((homes * rows, 128), F32),
            pltpu.VMEM((homes * rows, 2 * width), F32),
            pltpu.SMEM((2 * tiles,), jnp.int32),
        ],
        compiler_params=pltpu.CompilerParams(vmem_limit_bytes=44 << 20),
        cost_estimate=pl.CostEstimate(flops=1 << 20, bytes_accessed=1 << 18, transcendentals=0),
        name="attend",
    )(lengths, q, keys, values)


def weights_of(lines):
    level = jnp.concatenate(lines + [jnp.full((128 - len(lines), 128), 2 * NEG, F32)], axis=0)
    top = jnp.max(level, axis=0, keepdims=True)
    weight = jnp.exp2(level - top)
    total = jnp.sum(weight, axis=0, keepdims=True)
    return (weight / total).T, top + jnp.log(total) * LOG2


def merge_kernel(one_ref, two_ref, *refs):
    homes, held, _ = two_ref.shape
    o_refs = [ref.at[i] for ref in refs for i in range(ref.shape[0])]
    rows = held - META
    for h in range(homes):
        given = [one_ref.at[h], two_ref.at[h]]
        metas = [a[rows:, :].astype(F32) for a in given]
        lines = []
        for b in range(rows // 128):
            weight, line = weights_of([levels(meta, b) for meta in metas])
            lines.append(line)
            here = slice(b * 128, (b + 1) * 128)
            acc = given[0][here, :].astype(F32) * weight[:, 0:1] + given[1][here, :].astype(F32) * weight[:, 1:2]
            o_refs[h][here, :] = acc.astype(BF16)
        o_refs[h][rows:, :] = in_parts(lines)


def merge(one, two, pieces):
    _, held, width = two.shape
    return pl.pallas_call(
        merge_kernel,
        out_shape=[jax.ShapeDtypeStruct((piece, held, width), BF16) for piece in pieces],
        in_specs=[VMEM] * 2,
        out_specs=[VMEM] * len(pieces),
        compiler_params=pltpu.CompilerParams(vmem_limit_bytes=16 << 20),
        cost_estimate=pl.CostEstimate(flops=1 << 30, bytes_accessed=1 << 18, transcendentals=0),
        name="merge",
    )(one, two)


def project_kernel(group, ranks, cores, *refs):
    a_refs, (own_ref, w_ref, keep_ref, give_ref, sum_ref, all_ref, flat_ref, held_ref, sems) = refs[:-9], refs[-9:]
    a_refs = [a.at[0] for a in a_refs]
    blocks, _, block = held_ref.shape
    copies = [
        pltpu.make_async_copy(w_ref.at[:, pl.ds(j * block, block)], held_ref.at[j], sems.at[j]) for j in range(blocks)
    ]
    for copy in copies:
        copy.start()
    rows, width = sum_ref.shape
    metas = [a[rows:, :].astype(F32) for a in a_refs]
    for b in range(rows // 128):
        weight, _ = weights_of([own_ref[rows + b : rows + b + 1, :]] + [levels(meta, b) for meta in metas])
        here = slice(b * 128, (b + 1) * 128)
        acc = own_ref[here, :] * weight[:, 0:1]
        for i, a in enumerate(a_refs):
            acc = acc + a[here, :].astype(F32) * weight[:, i + 1 : i + 2]
        sum_ref[here, :] = acc
    tokens = rows // group
    for g in range(group):
        all_ref[:, g * width : (g + 1) * width] = sum_ref[pl.ds(g, tokens, stride=group), :]
    chips = ranks // cores
    share = tokens // ranks
    rank = lax.axis_index("kvh")
    chip, core = rank // cores, rank % cores
    for i in range(cores):
        for d in range(chips):
            to = ((chip + d) % chips) * cores + (core + i) % cores
            at = (i * chips + d) * share
            flat_ref[at : at + share, :] = all_ref[pl.ds(pl.multiple_of(to * share, share), share), :]
    flat = flat_ref[...].astype(BF16)
    half = tokens // cores
    for j, copy in enumerate(copies):
        copy.wait()
        out = jnp.dot(flat, held_ref[j], preferred_element_type=F32).astype(BF16)
        keep_ref[:, j * block : (j + 1) * block] = out[:half]
        give_ref[:, j * block : (j + 1) * block] = out[half:]


def project(parts, own, weight, group, ranks, cores):
    _, held, width = parts[0].shape
    rows = held - META
    depth, columns = weight.shape
    tokens = rows // group
    block = 1024
    return pl.pallas_call(
        functools.partial(project_kernel, group, ranks, cores),
        out_shape=[jax.ShapeDtypeStruct((tokens // cores, columns), BF16)] * 2,
        in_specs=[VMEM] * (len(parts) + 1) + [ANY],
        out_specs=[VMEM] * 2,
        scratch_shapes=[
            pltpu.VMEM((rows, width), F32),
            pltpu.VMEM((tokens, depth), F32),
            pltpu.VMEM((tokens, depth), F32),
            pltpu.VMEM((columns // block, depth, block), BF16),
            pltpu.SemaphoreType.DMA((columns // block,)),
        ],
        compiler_params=pltpu.CompilerParams(vmem_limit_bytes=50 << 20),
        cost_estimate=pl.CostEstimate(flops=1 << 30, bytes_accessed=18 << 20, transcendentals=1 << 14),
        name="project",
    )(*parts, own, weight)


def local(
    queries, new_keys, new_values, ancestors, tile_keys, tile_values, tile_lengths, out_weight
):
    owners = lax.axis_size("owner")
    ranks = lax.axis_size("kvh")
    cores = 2
    chips = ranks // cores
    side = math.isqrt(owners)
    parts, new, group, width = queries.shape
    per_owner = tile_keys.shape[0]
    scale = width**-0.5 * LOG2
    rows = parts * new * group

    def along(x, *steps):
        pairs = []
        for o in range(owners):
            for k in range(ranks):
                dz, dy = steps if k % cores == 0 else steps[::-1]
                y, z = (o // side + dy) % side, (o + dz) % side
                pairs.append((o * ranks + k, (y * side + z) * ranks + k))
        return lax.ppermute(x, ("owner", "kvh"), pairs)

    home = pack(queries.reshape(rows, width), ancestors)
    near = [along(home, d, 0) for d in range(1, side)]
    keys, values, own = prepare(
        tile_lengths,
        queries.reshape(parts, new * group, width),
        new_keys[:, :, 0],
        new_values[:, :, 0],
        tile_keys[:, 0],
        tile_values[:, 0],
        scale,
        group,
    )
    row, keys, values = lax.optimization_barrier((jnp.stack(near + [home]), keys, values))
    farthest = side // 2
    blocks = {e: along(row, 0, e) if e else row for e in range(side) if e != farthest}
    outs = None
    for e in range(side):
        if e == 1:
            late, outs = lax.optimization_barrier((row, outs))
            blocks[farthest] = along(late, 0, farthest)
        block = blocks[e]
        if e:
            block, outs = lax.optimization_barrier((block, outs))
        last = e == side - 1
        pieces = (side - 2, 1, 1) if last else (side,)
        outs = attend(block, keys, values, tile_lengths, scale, parts, pieces)
        if e == 0:
            merged = outs
        elif not last:
            merged = merge(merged[0], along(outs[0], 0, -e), (side - 2, 1, 1) if e == side - 2 else (side,))
    two, three, here = outs
    far = along(merged[1], 1 - side, 0)
    straight = along(three, 1 - side, -e)
    here = merge(merged[2], along(here, 0, -e), (1,))[0]
    near = merge(merged[0], along(two, 0, -e), (1,) * (side - 2))
    final = [here, merge(far, straight, (1,))[0]] + [along(near[d - 1], -d, 0) for d in range(1, side - 1)]
    keep, give = project(final, own, out_weight, group, ranks, cores)
    got = lax.ppermute(give, "kvh", [(k, k // cores * cores + (k + 1) % cores) for k in range(ranks)])
    share = keep.shape[0] // chips
    pieces = [
        keep[d * share : (d + 1) * share].astype(F32) + got[d * share : (d + 1) * share].astype(F32) for d in range(chips)
    ]
    result = pieces[0]
    for d in sorted(range(1, chips), key=lambda d: min(d, chips - d)):
        pairs = [(k, (k + d * cores) % ranks) for k in range(ranks)]
        result = result + lax.ppermute(pieces[d].astype(BF16), "kvh", pairs).astype(F32)
    return result.astype(BF16)


def solution(mesh):
    return jax.shard_map(
        local,
        mesh=mesh,
        in_specs=(
            P("owner", None, "kvh", None),
            P("owner", None, "kvh", None),
            P("owner", None, "kvh", None),
            P("owner", None),
            P("owner", "kvh", None, None),
            P("owner", "kvh", None, None),
            P("owner"),
            P("kvh", None),
        ),
        out_specs=P(("owner", "kvh"), None),
        check_vma=False,
    )
```

```python
import functools
import math

import jax
import jax.numpy as jnp
from jax import lax
from jax.experimental import pallas as pl
from jax.experimental.pallas import tpu as pltpu
from jax.sharding import PartitionSpec as P

NEG = -1e30
META = 16
STEP = 256
FEW = 2
F32 = jnp.float32
BF16 = jnp.bfloat16
VMEM = pl.BlockSpec(memory_space=pltpu.VMEM)
SMEM = pl.BlockSpec(memory_space=pltpu.SMEM)
ANY = pl.BlockSpec(memory_space=pl.ANY)
LOG2 = 1.0 / math.log(2.0)


def to_lanes(column, count):
    r = lax.broadcasted_iota(jnp.int32, (128, 128), 0)
    c = lax.broadcasted_iota(jnp.int32, (128, 128), 1)
    eye = r == c
    rows = []
    for b in range(count // 128):
        rows.append(jnp.sum(jnp.where(eye, column[b * 128 : (b + 1) * 128], 0.0), axis=0, keepdims=True))
    return rows


def in_parts(lines):
    pieces = []
    for line in lines:
        high = line.astype(BF16).astype(F32)
        mid = (line - high).astype(BF16).astype(F32)
        pieces += [high, mid, line - high - mid]
    pad = jnp.zeros((META - len(pieces), 128), F32)
    return jnp.concatenate(pieces + [pad], axis=0).astype(BF16)


def levels(meta, b):
    return meta[3 * b : 3 * b + 1] + meta[3 * b + 1 : 3 * b + 2] + meta[3 * b + 2 : 3 * b + 3]


def pack_kernel(q_any, a_any, o_ref, a_ref, meta_ref, q_sem, a_sem):
    rows = q_any.shape[0]
    q_copy = pltpu.make_async_copy(q_any, o_ref.at[pl.ds(0, rows)], q_sem)
    a_copy = pltpu.make_async_copy(a_any, a_ref, a_sem)
    q_copy.start()
    a_copy.start()
    meta_ref[...] = jnp.full(meta_ref.shape, -1.0, F32)
    a_copy.wait()
    meta_ref[: a_ref.shape[0], : a_ref.shape[1]] = a_ref[...].astype(F32)
    o_ref[rows:, :] = meta_ref[...].astype(BF16)
    q_copy.wait()


def pack(q, ancestors):
    rows, width = q.shape
    return pl.pallas_call(
        pack_kernel,
        out_shape=jax.ShapeDtypeStruct((rows + META, width), BF16),
        in_specs=[ANY] * 2,
        out_specs=VMEM,
        scratch_shapes=[
            pltpu.VMEM(ancestors.shape, jnp.int32),
            pltpu.VMEM((META, width), F32),
            pltpu.SemaphoreType.DMA,
            pltpu.SemaphoreType.DMA,
        ],
        compiler_params=pltpu.CompilerParams(vmem_limit_bytes=4 << 20),
        cost_estimate=pl.CostEstimate(flops=1 << 10, bytes_accessed=1 << 18, transcendentals=0),
        name="pack",
    )(*(pltpu.with_memory_space_constraint(a, pltpu.HBM) for a in (q, ancestors)))


def prepare_kernel(scale, group, lengths, *refs):
    given, (kt_ref, va_ref, o_ref), held, sems = refs[:5], refs[5:8], refs[8:13], refs[13:]
    copies = [pltpu.make_async_copy(a, b, sem) for a, b, sem in zip(given, held, sems)]
    for copy in copies:
        copy.start()
    q_ref, nk_ref, nv_ref, k_ref, v_ref = held
    tiles, size, width = k_ref.shape
    for copy in copies:
        copy.wait()

    @pl.loop(0, tiles)
    def _(t):
        live = lax.broadcasted_iota(jnp.int32, (size, width), 0) < lengths[t]
        k = k_ref[t].astype(F32)
        kt_ref[t] = jnp.where(live, k, k[:1]).T.astype(BF16)
        va_ref[t, :, :width] = jnp.where(live, v_ref[t].astype(F32), 0.0).astype(BF16)
        va_ref[t, :, width:] = live.astype(F32).astype(BF16)

    halves, part, _ = q_ref.shape
    new = nk_ref.shape[1]
    rows = halves * part
    for i in range(halves):
        s = lax.dot_general(q_ref[i], nk_ref[i], (((1,), (1,)), ((), ())), preferred_element_type=F32)
        token = lax.broadcasted_iota(jnp.int32, (part, new), 0) // group
        seen = token >= lax.broadcasted_iota(jnp.int32, (part, new), 1)
        s = jnp.where(seen, s, NEG)
        peak = jnp.max(s, axis=1, keepdims=True)
        weights = jnp.where(seen, jnp.exp2((s - peak) * scale), 0.0)
        total = jnp.sum(weights, axis=1, keepdims=True)
        summed = jnp.dot(weights.astype(BF16), nv_ref[i], preferred_element_type=F32)
        o_ref[i * part : (i + 1) * part, :] = summed / total
        level = peak * scale + jnp.log(total) * LOG2
        rowed = to_lanes(jnp.broadcast_to(level, (part, width)), part)
        for b, line in enumerate(rowed):
            at = rows + i * len(rowed) + b
            o_ref[at : at + 1, :] = line


def prepare(lengths, q, new_keys, new_values, keys, values, scale, group):
    halves, part, width = q.shape
    tiles, size, _ = keys.shape
    return pl.pallas_call(
        functools.partial(prepare_kernel, scale, group),
        out_shape=[
            jax.ShapeDtypeStruct((tiles, width, size), BF16),
            jax.ShapeDtypeStruct((tiles, size, 2 * width), BF16),
            jax.ShapeDtypeStruct((halves * part + 8, width), F32),
        ],
        in_specs=[SMEM] + [ANY] * 5,
        out_specs=[VMEM] * 3,
        scratch_shapes=[pltpu.VMEM(a.shape, BF16) for a in (q, new_keys, new_values, keys, values)]
        + [pltpu.SemaphoreType.DMA] * 5,
        compiler_params=pltpu.CompilerParams(vmem_limit_bytes=44 << 20),
        cost_estimate=pl.CostEstimate(flops=1 << 24, bytes_accessed=16 << 20, transcendentals=1 << 15),
        name="prepare",
    )(lengths, *(pltpu.with_memory_space_constraint(a, pltpu.HBM) for a in (q, new_keys, new_values, keys, values)))


def attend_kernel(
    scale, halves, lengths, q_ref, k_ref, v_ref, *refs
):
    homes, held, width = q_ref.shape
    pieces, (s_ref, m_ref, acc_ref, member) = refs[:-4], refs[-4:]
    o_refs = [piece.at[i] for piece in pieces for i in range(piece.shape[0])]
    rows = held - META
    tiles, _, size = k_ref.shape
    part = rows // halves
    count = homes * halves

    names = jnp.concatenate([q_ref[h, rows:, :].astype(F32)[:halves] for h in range(homes)], axis=0)
    first = (lax.axis_index("owner") * tiles).astype(F32)
    bit = lax.broadcasted_iota(jnp.int32, (count, 1), 0)
    for t in range(tiles):
        inside = jnp.max(jnp.where(names == first + t, 1.0, 0.0), axis=1, keepdims=True)
        power = (1 << bit).astype(F32)
        member[t] = jnp.sum(inside * power).astype(jnp.int32)
        member[tiles + t] = jnp.sum(inside).astype(jnp.int32)
    m_ref[...] = jnp.full(m_ref.shape, NEG, F32)
    acc_ref[...] = jnp.zeros(acc_ref.shape, F32)

    def for_each_tile(body):
        @pl.loop(0, tiles)
        def _(t):
            held_by = member[t]
            number = member[tiles + t]
            for n in range(1, size // STEP + 1):
                fits = lengths[t] > (n - 1) * STEP
                if n * STEP < size:
                    fits = fits & (lengths[t] <= n * STEP)

                @pl.when(fits & (number > FEW))
                def _():
                    every = [(slice(i * part, (i + 1) * part), (held_by >> i) & 1 > 0) for i in range(count)]
                    body(t, n * STEP, q_ref[:, :rows, :].reshape(homes * rows, width), slice(None), every)

                @pl.when(fits & (number > 0) & (number <= FEW))
                def _():
                    @pl.loop(0, count)
                    def _(i):
                        @pl.when((held_by >> i) & 1 > 0)
                        def _():
                            q = q_ref[i // halves, pl.ds(pl.multiple_of(i % halves * part, part), part), :]
                            body(t, n * STEP, q, pl.ds(pl.multiple_of(i * part, part), part), [(slice(None), True)])

    def score(t, wide, q, span, blocks):
        s = jnp.dot(q, k_ref[t, :, :wide], preferred_element_type=F32)
        s_ref[t, span, :wide] = s
        for here, inside in blocks:
            x = s[here, :128]
            for j in range(128, wide, 128):
                x = jnp.maximum(x, s[here, j : j + 128])
            if inside is True:
                m_ref[span, :] = jnp.maximum(m_ref[span, :], x)
            else:
                m_ref[here, :] = jnp.maximum(m_ref[here, :], jnp.where(inside, x, NEG))

    for_each_tile(score)
    peak = jnp.max(m_ref[...], axis=1, keepdims=True) * scale
    m_ref[...] = jnp.broadcast_to(peak, m_ref.shape)

    def weigh(t, wide, q, span, blocks):
        weights = []
        for here, inside in blocks:
            rows_here = span if inside is True else here
            shift = m_ref[rows_here, :]
            if inside is not True:
                shift = jnp.where(inside, shift, -NEG)
            weights.append(
                jnp.concatenate(
                    [jnp.exp2(s_ref[t, rows_here, j : j + 128] * scale - shift).astype(BF16) for j in range(0, wide, 128)],
                    axis=1,
                )
            )
        weights = weights[0] if len(weights) == 1 else jnp.concatenate(weights, axis=0)
        acc_ref[span, :] += jnp.dot(weights, v_ref[t, :wide, :], preferred_element_type=F32)

    for_each_tile(weigh)
    for h in range(homes):
        here = slice(h * rows, (h + 1) * rows)
        total = acc_ref[here, width:]
        o_refs[h][:rows, :] = (acc_ref[here, :width] / jnp.maximum(total, -1.0 / NEG)).astype(BF16)
        sums = jnp.concatenate(to_lanes(total, rows), axis=0)
        peaks = jnp.concatenate(to_lanes(m_ref[here, :], rows), axis=0)
        level = jnp.where(sums > 0.0, peaks + jnp.log(jnp.maximum(sums, -1.0 / NEG)) * LOG2, NEG)
        o_refs[h][rows:, :] = in_parts([level[b : b + 1] for b in range(rows // 128)])


def attend(q, keys, values, lengths, scale, halves, pieces):
    homes, held, width = q.shape
    tiles, _, size = keys.shape
    rows = held - META
    return pl.pallas_call(
        functools.partial(attend_kernel, scale, halves),
        out_shape=[jax.ShapeDtypeStruct((piece, held, width), BF16) for piece in pieces],
        in_specs=[SMEM, VMEM, VMEM, VMEM],
        out_specs=[VMEM] * len(pieces),
        scratch_shapes=[
            pltpu.VMEM((tiles, homes * rows, size), F32),
            pltpu.VMEM((homes * rows, 128), F32),
            pltpu.VMEM((homes * rows, 2 * width), F32),
            pltpu.SMEM((2 * tiles,), jnp.int32),
        ],
        compiler_params=pltpu.CompilerParams(vmem_limit_bytes=44 << 20),
        cost_estimate=pl.CostEstimate(flops=1 << 20, bytes_accessed=1 << 18, transcendentals=0),
        name="attend",
    )(lengths, q, keys, values)


def weights_of(lines):
    level = jnp.concatenate(lines + [jnp.full((128 - len(lines), 128), 2 * NEG, F32)], axis=0)
    top = jnp.max(level, axis=0, keepdims=True)
    weight = jnp.exp2(level - top)
    total = jnp.sum(weight, axis=0, keepdims=True)
    return (weight / total).T, top + jnp.log(total) * LOG2


def merge_kernel(one_ref, two_ref, *refs):
    homes, held, _ = two_ref.shape
    o_refs = [ref.at[i] for ref in refs for i in range(ref.shape[0])]
    rows = held - META
    for h in range(homes):
        given = [one_ref.at[h], two_ref.at[h]]
        metas = [a[rows:, :].astype(F32) for a in given]
        lines = []
        for b in range(rows // 128):
            weight, line = weights_of([levels(meta, b) for meta in metas])
            lines.append(line)
            here = slice(b * 128, (b + 1) * 128)
            acc = given[0][here, :].astype(F32) * weight[:, 0:1] + given[1][here, :].astype(F32) * weight[:, 1:2]
            o_refs[h][here, :] = acc.astype(BF16)
        o_refs[h][rows:, :] = in_parts(lines)


def merge(one, two, pieces):
    _, held, width = two.shape
    return pl.pallas_call(
        merge_kernel,
        out_shape=[jax.ShapeDtypeStruct((piece, held, width), BF16) for piece in pieces],
        in_specs=[VMEM] * 2,
        out_specs=[VMEM] * len(pieces),
        compiler_params=pltpu.CompilerParams(vmem_limit_bytes=16 << 20),
        cost_estimate=pl.CostEstimate(flops=1 << 30, bytes_accessed=1 << 18, transcendentals=0),
        name="merge",
    )(one, two)


def multiply(flat, keep_ref, give_ref, held_ref, copies):
    block = held_ref.shape[2]
    half = keep_ref.shape[0]
    for j, copy in enumerate(copies):
        copy.wait()
        out = jnp.dot(flat, held_ref[j], preferred_element_type=F32).astype(BF16)
        keep_ref[:, j * block : (j + 1) * block] = out[:half]
        give_ref[:, j * block : (j + 1) * block] = out[half:]


def fetch(first, w_ref, held_ref, sems):
    blocks, _, block = held_ref.shape
    copies = []
    for j in range(blocks):
        source = w_ref.at[:, pl.ds((first + j) * block, block)]
        copies.append(pltpu.make_async_copy(source, held_ref.at[j], sems.at[j]))
        copies[-1].start()
    return copies


def project_kernel(group, ranks, cores, *refs):
    a_refs, (own_ref, w_ref, keep_ref, give_ref, bf_ref, sum_ref, all_ref, flat_ref, held_ref, sems) = refs[:-10], refs[-10:]
    copies = fetch(0, w_ref, held_ref, sems)
    a_refs = [a.at[0] for a in a_refs]
    rows, width = sum_ref.shape
    metas = [a[rows:, :].astype(F32) for a in a_refs]
    for b in range(rows // 128):
        weight, _ = weights_of([own_ref[rows + b : rows + b + 1, :]] + [levels(meta, b) for meta in metas])
        here = slice(b * 128, (b + 1) * 128)
        acc = own_ref[here, :] * weight[:, 0:1]
        for i, a in enumerate(a_refs):
            acc = acc + a[here, :].astype(F32) * weight[:, i + 1 : i + 2]
        sum_ref[here, :] = acc
    tokens = rows // group
    for g in range(group):
        all_ref[:, g * width : (g + 1) * width] = sum_ref[pl.ds(g, tokens, stride=group), :]
    chips = ranks // cores
    share = tokens // ranks
    rank = lax.axis_index("kvh")
    chip, core = rank // cores, rank % cores
    for i in range(cores):
        for d in range(chips):
            to = ((chip + d) % chips) * cores + (core + i) % cores
            at = (i * chips + d) * share
            flat_ref[at : at + share, :] = all_ref[pl.ds(pl.multiple_of(to * share, share), share), :]
    flat = flat_ref[...].astype(BF16)
    bf_ref[...] = flat
    multiply(flat, keep_ref, give_ref, held_ref, copies)


def project_more_kernel(first, flat_ref, w_ref, keep_ref, give_ref, held_ref, sems):
    copies = fetch(first, w_ref, held_ref, sems)
    multiply(flat_ref[...], keep_ref, give_ref, held_ref, copies)


def project(parts, own, weight, group, ranks, cores):
    _, held, width = parts[0].shape
    rows = held - META
    depth, columns = weight.shape
    tokens = rows // group
    block = 1024
    blocks = columns // block // 2
    half = [jax.ShapeDtypeStruct((tokens // cores, columns // 2), BF16)] * 2
    wide = [pltpu.VMEM((blocks, depth, block), BF16), pltpu.SemaphoreType.DMA((blocks,))]
    keep, give, flat = pl.pallas_call(
        functools.partial(project_kernel, group, ranks, cores),
        out_shape=half + [jax.ShapeDtypeStruct((tokens, depth), BF16)],
        in_specs=[VMEM] * (len(parts) + 1) + [ANY],
        out_specs=[VMEM] * 3,
        scratch_shapes=[
            pltpu.VMEM((rows, width), F32),
            pltpu.VMEM((tokens, depth), F32),
            pltpu.VMEM((tokens, depth), F32),
            *wide,
        ],
        compiler_params=pltpu.CompilerParams(vmem_limit_bytes=50 << 20),
        cost_estimate=pl.CostEstimate(flops=1 << 30, bytes_accessed=1 << 18, transcendentals=0),
        name="project",
    )(*parts, own, weight)

    def more(flat):
        return pl.pallas_call(
            functools.partial(project_more_kernel, blocks),
            out_shape=half,
            in_specs=[VMEM, ANY],
            out_specs=[VMEM] * 2,
            scratch_shapes=wide,
            compiler_params=pltpu.CompilerParams(vmem_limit_bytes=50 << 20),
            cost_estimate=pl.CostEstimate(flops=1 << 32, bytes_accessed=1 << 18, transcendentals=0),
            name="project_more",
        )(flat, weight)

    return keep, give, flat, more


def local(
    queries, new_keys, new_values, ancestors, tile_keys, tile_values, tile_lengths, out_weight
):
    owners = lax.axis_size("owner")
    ranks = lax.axis_size("kvh")
    cores = 2
    chips = ranks // cores
    side = math.isqrt(owners)
    parts, new, group, width = queries.shape
    per_owner = tile_keys.shape[0]
    scale = width**-0.5 * LOG2
    rows = parts * new * group

    def along(x, *steps):
        pairs = []
        for o in range(owners):
            for k in range(ranks):
                dz, dy = steps if k % cores == 0 else steps[::-1]
                y, z = (o // side + dy) % side, (o + dz) % side
                pairs.append((o * ranks + k, (y * side + z) * ranks + k))
        return lax.ppermute(x, ("owner", "kvh"), pairs)

    home = pack(queries.reshape(rows, width), ancestors)
    near = [along(home, d, 0) for d in range(1, side)]
    keys, values, own = prepare(
        tile_lengths,
        queries.reshape(parts, new * group, width),
        new_keys[:, :, 0],
        new_values[:, :, 0],
        tile_keys[:, 0],
        tile_values[:, 0],
        scale,
        group,
    )
    row, keys, values = lax.optimization_barrier((jnp.stack(near + [home]), keys, values))
    order = sorted(range(side), key=lambda e: min(e, side - e))
    blocks = {e: along(row, 0, e) if e else row for e in order[:-1]}
    outs = None
    for i, e in enumerate(order):
        if i == 1:
            late, outs = lax.optimization_barrier((row, outs))
            blocks[order[-1]] = along(late, 0, order[-1])
        block = blocks[e]
        if e:
            block, outs = lax.optimization_barrier((block, outs))
        last = i == side - 1
        pieces = (side - 2, 1, 1) if last else (side,)
        outs = attend(block, keys, values, tile_lengths, scale, parts, pieces)
        if i == 0:
            merged = outs
        elif not last:
            merged = merge(merged[0], along(outs[0], 0, -e), (side - 2, 1, 1) if i == side - 2 else (side,))
    two, three, here = outs
    far = along(merged[1], 1 - side, 0)
    straight = along(three, 1 - side, -e)
    here = merge(merged[2], along(here, 0, -e), (1,))[0]
    near = merge(merged[0], along(two, 0, -e), (1,) * (side - 2))
    final = [here, merge(far, straight, (1,))[0]] + [along(near[d - 1], -d, 0) for d in range(1, side - 1)]
    keep, give, flat, more = project(final, own, out_weight, group, ranks, cores)

    def across(give):
        return lax.ppermute(give, "kvh", [(k, k // cores * cores + (k + 1) % cores) for k in range(ranks)])

    def summed(keep, got):
        share = keep.shape[0] // chips
        pieces = [
            keep[d * share : (d + 1) * share].astype(F32) + got[d * share : (d + 1) * share].astype(F32)
            for d in range(chips)
        ]
        result = pieces[0]
        for d in sorted(range(1, chips), key=lambda d: min(d, chips - d)):
            pairs = [(k, (k + d * cores) % ranks) for k in range(ranks)]
            result = result + lax.ppermute(pieces[d].astype(BF16), "kvh", pairs).astype(F32)
        return result.astype(BF16)

    got = across(give)
    keep_more, give_more = more(flat)
    got_more = across(give_more)
    return jnp.concatenate([summed(keep, got), summed(keep_more, got_more)], axis=1)


def solution(mesh):
    return jax.shard_map(
        local,
        mesh=mesh,
        in_specs=(
            P("owner", None, "kvh", None),
            P("owner", None, "kvh", None),
            P("owner", None, "kvh", None),
            P("owner", None),
            P("owner", "kvh", None, None),
            P("owner", "kvh", None, None),
            P("owner"),
            P("kvh", None),
        ),
        out_specs=P(("owner", "kvh"), None),
        check_vma=False,
    )
```

```python
import functools
import math

import jax
import jax.numpy as jnp
from jax import lax
from jax.experimental import pallas as pl
from jax.experimental.pallas import tpu as pltpu
from jax.sharding import PartitionSpec as P

NEG = -1e30
META = 16
STEP = 256
FEW = 2
FETCH = 2048
F32 = jnp.float32
BF16 = jnp.bfloat16
VMEM = pl.BlockSpec(memory_space=pltpu.VMEM)
SMEM = pl.BlockSpec(memory_space=pltpu.SMEM)
ANY = pl.BlockSpec(memory_space=pl.ANY)
LOG2 = 1.0 / math.log(2.0)


def to_lanes(column, count):
    r = lax.broadcasted_iota(jnp.int32, (128, 128), 0)
    c = lax.broadcasted_iota(jnp.int32, (128, 128), 1)
    eye = r == c
    rows = []
    for b in range(count // 128):
        rows.append(jnp.sum(jnp.where(eye, column[b * 128 : (b + 1) * 128], 0.0), axis=0, keepdims=True))
    return rows


def in_parts(lines):
    pieces = []
    for line in lines:
        high = line.astype(BF16).astype(F32)
        mid = (line - high).astype(BF16).astype(F32)
        pieces += [high, mid, line - high - mid]
    pad = jnp.zeros((META - len(pieces), 128), F32)
    return jnp.concatenate(pieces + [pad], axis=0).astype(BF16)


def levels(meta, b):
    return meta[3 * b : 3 * b + 1] + meta[3 * b + 1 : 3 * b + 2] + meta[3 * b + 2 : 3 * b + 3]


def pack_kernel(q_any, a_any, o_ref, a_ref, meta_ref, q_sem, a_sem):
    rows = q_any.shape[0]
    q_copy = pltpu.make_async_copy(q_any, o_ref.at[pl.ds(0, rows)], q_sem)
    a_copy = pltpu.make_async_copy(a_any, a_ref, a_sem)
    q_copy.start()
    a_copy.start()
    meta_ref[...] = jnp.full(meta_ref.shape, -1.0, F32)
    a_copy.wait()
    meta_ref[: a_ref.shape[0], : a_ref.shape[1]] = a_ref[...].astype(F32)
    o_ref[rows:, :] = meta_ref[...].astype(BF16)
    q_copy.wait()


def pack(q, ancestors):
    rows, width = q.shape
    return pl.pallas_call(
        pack_kernel,
        out_shape=jax.ShapeDtypeStruct((rows + META, width), BF16),
        in_specs=[ANY] * 2,
        out_specs=VMEM,
        scratch_shapes=[
            pltpu.VMEM(ancestors.shape, jnp.int32),
            pltpu.VMEM((META, width), F32),
            pltpu.SemaphoreType.DMA,
            pltpu.SemaphoreType.DMA,
        ],
        compiler_params=pltpu.CompilerParams(vmem_limit_bytes=4 << 20),
        cost_estimate=pl.CostEstimate(flops=1 << 10, bytes_accessed=1 << 18, transcendentals=0),
        name="pack",
    )(*(pltpu.with_memory_space_constraint(a, pltpu.HBM) for a in (q, ancestors)))


def prepare_kernel(scale, group, lengths, *refs):
    given, (kt_ref, va_ref, o_ref), held, sems = refs[:5], refs[5:8], refs[8:13], refs[13:]
    copies = [pltpu.make_async_copy(a, b, sem) for a, b, sem in zip(given, held, sems)]
    for copy in copies:
        copy.start()
    q_ref, nk_ref, nv_ref, k_ref, v_ref = held
    tiles, size, width = k_ref.shape
    for copy in copies:
        copy.wait()

    @pl.loop(0, tiles)
    def _(t):
        live = lax.broadcasted_iota(jnp.int32, (size, width), 0) < lengths[t]
        k = k_ref[t].astype(F32)
        kt_ref[t] = jnp.where(live, k, k[:1]).T.astype(BF16)
        va_ref[t, :, :width] = jnp.where(live, v_ref[t].astype(F32), 0.0).astype(BF16)
        va_ref[t, :, width:] = live.astype(F32).astype(BF16)

    halves, part, _ = q_ref.shape
    new = nk_ref.shape[1]
    rows = halves * part
    for i in range(halves):
        s = lax.dot_general(q_ref[i], nk_ref[i], (((1,), (1,)), ((), ())), preferred_element_type=F32)
        token = lax.broadcasted_iota(jnp.int32, (part, new), 0) // group
        seen = token >= lax.broadcasted_iota(jnp.int32, (part, new), 1)
        s = jnp.where(seen, s, NEG)
        peak = jnp.max(s, axis=1, keepdims=True)
        weights = jnp.where(seen, jnp.exp2((s - peak) * scale), 0.0)
        total = jnp.sum(weights, axis=1, keepdims=True)
        summed = jnp.dot(weights.astype(BF16), nv_ref[i], preferred_element_type=F32)
        o_ref[i * part : (i + 1) * part, :] = summed / total
        level = peak * scale + jnp.log(total) * LOG2
        rowed = to_lanes(jnp.broadcast_to(level, (part, width)), part)
        for b, line in enumerate(rowed):
            at = rows + i * len(rowed) + b
            o_ref[at : at + 1, :] = line


def prepare(lengths, q, new_keys, new_values, keys, values, scale, group):
    halves, part, width = q.shape
    tiles, size, _ = keys.shape
    return pl.pallas_call(
        functools.partial(prepare_kernel, scale, group),
        out_shape=[
            jax.ShapeDtypeStruct((tiles, width, size), BF16),
            jax.ShapeDtypeStruct((tiles, size, 2 * width), BF16),
            jax.ShapeDtypeStruct((halves * part + 8, width), F32),
        ],
        in_specs=[SMEM] + [ANY] * 5,
        out_specs=[VMEM] * 3,
        scratch_shapes=[pltpu.VMEM(a.shape, BF16) for a in (q, new_keys, new_values, keys, values)]
        + [pltpu.SemaphoreType.DMA] * 5,
        compiler_params=pltpu.CompilerParams(vmem_limit_bytes=44 << 20),
        cost_estimate=pl.CostEstimate(flops=1 << 24, bytes_accessed=16 << 20, transcendentals=1 << 15),
        name="prepare",
    )(lengths, *(pltpu.with_memory_space_constraint(a, pltpu.HBM) for a in (q, new_keys, new_values, keys, values)))


def attend_kernel(
    scale, halves, lengths, q_ref, k_ref, v_ref, *refs
):
    homes, held, width = q_ref.shape
    pieces, (s_ref, m_ref, acc_ref, member) = refs[:-4], refs[-4:]
    o_refs = [piece.at[i] for piece in pieces for i in range(piece.shape[0])]
    rows = held - META
    tiles, _, size = k_ref.shape
    part = rows // halves
    count = homes * halves

    names = jnp.concatenate([q_ref[h, rows:, :].astype(F32)[:halves] for h in range(homes)], axis=0)
    first = (lax.axis_index("owner") * tiles).astype(F32)
    bit = lax.broadcasted_iota(jnp.int32, (count, 1), 0)
    for t in range(tiles):
        inside = jnp.max(jnp.where(names == first + t, 1.0, 0.0), axis=1, keepdims=True)
        power = (1 << bit).astype(F32)
        member[t] = jnp.sum(inside * power).astype(jnp.int32)
        member[tiles + t] = jnp.sum(inside).astype(jnp.int32)
    m_ref[...] = jnp.full(m_ref.shape, NEG, F32)
    acc_ref[...] = jnp.zeros(acc_ref.shape, F32)

    def for_each_tile(body):
        @pl.loop(0, tiles)
        def _(t):
            held_by = member[t]
            number = member[tiles + t]
            for n in range(1, size // STEP + 1):
                fits = lengths[t] > (n - 1) * STEP
                if n * STEP < size:
                    fits = fits & (lengths[t] <= n * STEP)

                @pl.when(fits & (number > FEW))
                def _():
                    every = [(slice(i * part, (i + 1) * part), (held_by >> i) & 1 > 0) for i in range(count)]
                    body(t, n * STEP, q_ref[:, :rows, :].reshape(homes * rows, width), slice(None), every)

                @pl.when(fits & (number > 0) & (number <= FEW))
                def _():
                    @pl.loop(0, count)
                    def _(i):
                        @pl.when((held_by >> i) & 1 > 0)
                        def _():
                            q = q_ref[i // halves, pl.ds(pl.multiple_of(i % halves * part, part), part), :]
                            body(t, n * STEP, q, pl.ds(pl.multiple_of(i * part, part), part), [(slice(None), True)])

    def score(t, wide, q, span, blocks):
        s = jnp.dot(q, k_ref[t, :, :wide], preferred_element_type=F32)
        s_ref[t, span, :wide] = s
        for here, inside in blocks:
            x = s[here, :128]
            for j in range(128, wide, 128):
                x = jnp.maximum(x, s[here, j : j + 128])
            if inside is True:
                m_ref[span, :] = jnp.maximum(m_ref[span, :], x)
            else:
                m_ref[here, :] = jnp.maximum(m_ref[here, :], jnp.where(inside, x, NEG))

    for_each_tile(score)
    peak = jnp.max(m_ref[...], axis=1, keepdims=True) * scale
    m_ref[...] = jnp.broadcast_to(peak, m_ref.shape)

    def weigh(t, wide, q, span, blocks):
        weights = []
        for here, inside in blocks:
            rows_here = span if inside is True else here
            shift = m_ref[rows_here, :]
            if inside is not True:
                shift = jnp.where(inside, shift, -NEG)
            weights.append(
                jnp.concatenate(
                    [jnp.exp2(s_ref[t, rows_here, j : j + 128] * scale - shift).astype(BF16) for j in range(0, wide, 128)],
                    axis=1,
                )
            )
        weights = weights[0] if len(weights) == 1 else jnp.concatenate(weights, axis=0)
        acc_ref[span, :] += jnp.dot(weights, v_ref[t, :wide, :], preferred_element_type=F32)

    for_each_tile(weigh)
    for h in range(homes):
        here = slice(h * rows, (h + 1) * rows)
        total = acc_ref[here, width:]
        o_refs[h][:rows, :] = (acc_ref[here, :width] / jnp.maximum(total, -1.0 / NEG)).astype(BF16)
        sums = jnp.concatenate(to_lanes(total, rows), axis=0)
        peaks = jnp.concatenate(to_lanes(m_ref[here, :], rows), axis=0)
        level = jnp.where(sums > 0.0, peaks + jnp.log(jnp.maximum(sums, -1.0 / NEG)) * LOG2, NEG)
        o_refs[h][rows:, :] = in_parts([level[b : b + 1] for b in range(rows // 128)])


def attend(q, keys, values, lengths, scale, halves, pieces):
    homes, held, width = q.shape
    tiles, _, size = keys.shape
    rows = held - META
    return pl.pallas_call(
        functools.partial(attend_kernel, scale, halves),
        out_shape=[jax.ShapeDtypeStruct((piece, held, width), BF16) for piece in pieces],
        in_specs=[SMEM, VMEM, VMEM, VMEM],
        out_specs=[VMEM] * len(pieces),
        scratch_shapes=[
            pltpu.VMEM((tiles, homes * rows, size), F32),
            pltpu.VMEM((homes * rows, 128), F32),
            pltpu.VMEM((homes * rows, 2 * width), F32),
            pltpu.SMEM((2 * tiles,), jnp.int32),
        ],
        compiler_params=pltpu.CompilerParams(vmem_limit_bytes=44 << 20),
        cost_estimate=pl.CostEstimate(flops=1 << 20, bytes_accessed=1 << 18, transcendentals=0),
        name="attend",
    )(lengths, q, keys, values)


def weights_of(lines):
    level = jnp.concatenate(lines + [jnp.full((128 - len(lines), 128), 2 * NEG, F32)], axis=0)
    top = jnp.max(level, axis=0, keepdims=True)
    weight = jnp.exp2(level - top)
    total = jnp.sum(weight, axis=0, keepdims=True)
    return (weight / total).T, top + jnp.log(total) * LOG2


def merge_kernel(first, one_ref, two_ref, *refs):
    homes, held, _ = two_ref.shape
    copy = None
    if first is not None:
        w_ref, *refs, part_ref, sem = refs
        copy = pltpu.make_async_copy(w_ref.at[:, pl.ds(first, part_ref.shape[1])], part_ref, sem)
        copy.start()
    o_refs = [ref.at[i] for ref in refs for i in range(ref.shape[0])]
    rows = held - META
    for h in range(homes):
        given = [one_ref.at[h], two_ref.at[h]]
        metas = [a[rows:, :].astype(F32) for a in given]
        lines = []
        for b in range(rows // 128):
            weight, line = weights_of([levels(meta, b) for meta in metas])
            lines.append(line)
            here = slice(b * 128, (b + 1) * 128)
            acc = given[0][here, :].astype(F32) * weight[:, 0:1] + given[1][here, :].astype(F32) * weight[:, 1:2]
            o_refs[h][here, :] = acc.astype(BF16)
        o_refs[h][rows:, :] = in_parts(lines)
    if copy is not None:
        copy.wait()


def merge(one, two, pieces, weight=None, first=None):
    _, held, width = two.shape
    out = [jax.ShapeDtypeStruct((piece, held, width), BF16) for piece in pieces]
    extra = []
    if weight is not None:
        out.append(jax.ShapeDtypeStruct((weight.shape[0], FETCH), BF16))
        extra = [pltpu.with_memory_space_constraint(weight, pltpu.HBM)]
    return pl.pallas_call(
        functools.partial(merge_kernel, first),
        out_shape=out,
        in_specs=[VMEM] * 2 + [ANY] * len(extra),
        out_specs=[VMEM] * len(out),
        scratch_shapes=[pltpu.SemaphoreType.DMA] * len(extra),
        compiler_params=pltpu.CompilerParams(vmem_limit_bytes=16 << 20),
        cost_estimate=pl.CostEstimate(flops=1 << 30, bytes_accessed=1 << 18, transcendentals=0),
        name="merge",
    )(one, two, *extra)


def project_kernel(group, ranks, cores, ahead, *refs):
    a_refs, (own_ref, w_ref, keep_ref, give_ref, sum_ref, all_ref, flat_ref, held_ref, sems) = refs[:-9], refs[-9:]
    ready, a_refs = a_refs[:ahead], [a.at[0] for a in a_refs[ahead:]]
    blocks, _, block = held_ref.shape
    begin = ahead * FETCH
    copies = [
        pltpu.make_async_copy(w_ref.at[:, pl.ds(begin + j * block, block)], held_ref.at[j], sems.at[j])
        for j in range(blocks)
    ]
    for copy in copies:
        copy.start()
    rows, width = sum_ref.shape
    metas = [a[rows:, :].astype(F32) for a in a_refs]
    for b in range(rows // 128):
        weight, _ = weights_of([own_ref[rows + b : rows + b + 1, :]] + [levels(meta, b) for meta in metas])
        here = slice(b * 128, (b + 1) * 128)
        acc = own_ref[here, :] * weight[:, 0:1]
        for i, a in enumerate(a_refs):
            acc = acc + a[here, :].astype(F32) * weight[:, i + 1 : i + 2]
        sum_ref[here, :] = acc
    tokens = rows // group
    for g in range(group):
        all_ref[:, g * width : (g + 1) * width] = sum_ref[pl.ds(g, tokens, stride=group), :]
    chips = ranks // cores
    share = tokens // ranks
    rank = lax.axis_index("kvh")
    chip, core = rank // cores, rank % cores
    for i in range(cores):
        for d in range(chips):
            to = ((chip + d) % chips) * cores + (core + i) % cores
            at = (i * chips + d) * share
            flat_ref[at : at + share, :] = all_ref[pl.ds(pl.multiple_of(to * share, share), share), :]
    flat = flat_ref[...].astype(BF16)
    half = tokens // cores

    def multiply(columns, at):
        out = jnp.dot(flat, columns, preferred_element_type=F32).astype(BF16)
        keep_ref[:, at : at + block] = out[:half]
        give_ref[:, at : at + block] = out[half:]

    for i, ref in enumerate(ready):
        for j in range(0, FETCH, block):
            multiply(ref[:, j : j + block], i * FETCH + j)
    for j, copy in enumerate(copies):
        copy.wait()
        multiply(held_ref[j], begin + j * block)


def project(ready, parts, own, weight, group, ranks, cores):
    _, held, width = parts[0].shape
    rows = held - META
    depth, columns = weight.shape
    tokens = rows // group
    block = 1024
    blocks = (columns - len(ready) * FETCH) // block
    return pl.pallas_call(
        functools.partial(project_kernel, group, ranks, cores, len(ready)),
        out_shape=[jax.ShapeDtypeStruct((tokens // cores, columns), BF16)] * 2,
        in_specs=[VMEM] * (len(ready) + len(parts) + 1) + [ANY],
        out_specs=[VMEM] * 2,
        scratch_shapes=[
            pltpu.VMEM((rows, width), F32),
            pltpu.VMEM((tokens, depth), F32),
            pltpu.VMEM((tokens, depth), F32),
            pltpu.VMEM((blocks, depth, block), BF16),
            pltpu.SemaphoreType.DMA((blocks,)),
        ],
        compiler_params=pltpu.CompilerParams(vmem_limit_bytes=24 << 20),
        cost_estimate=pl.CostEstimate(flops=1 << 30, bytes_accessed=18 << 20, transcendentals=1 << 14),
        name="project",
    )(*ready, *parts, own, pltpu.with_memory_space_constraint(weight, pltpu.HBM))


def local(
    queries, new_keys, new_values, ancestors, tile_keys, tile_values, tile_lengths, out_weight
):
    owners = lax.axis_size("owner")
    ranks = lax.axis_size("kvh")
    cores = 2
    chips = ranks // cores
    side = math.isqrt(owners)
    parts, new, group, width = queries.shape
    per_owner = tile_keys.shape[0]
    scale = width**-0.5 * LOG2
    rows = parts * new * group

    def along(x, *steps):
        pairs = []
        for o in range(owners):
            for k in range(ranks):
                dz, dy = steps if k % cores == 0 else steps[::-1]
                y, z = (o // side + dy) % side, (o + dz) % side
                pairs.append((o * ranks + k, (y * side + z) * ranks + k))
        return lax.ppermute(x, ("owner", "kvh"), pairs)

    home = pack(queries.reshape(rows, width), ancestors)
    near = [along(home, d, 0) for d in range(1, side)]
    keys, values, own = prepare(
        tile_lengths,
        queries.reshape(parts, new * group, width),
        new_keys[:, :, 0],
        new_values[:, :, 0],
        tile_keys[:, 0],
        tile_values[:, 0],
        scale,
        group,
    )
    row, keys, values = lax.optimization_barrier((jnp.stack(near + [home]), keys, values))
    order = sorted(range(side), key=lambda e: min(e, side - e))
    blocks = {e: along(row, 0, e) if e else row for e in order[:-1]}
    outs = None
    for i, e in enumerate(order):
        if i == 1:
            late, outs = lax.optimization_barrier((row, outs))
            blocks[order[-1]] = along(late, 0, order[-1])
        block = blocks[e]
        if e:
            block, outs = lax.optimization_barrier((block, outs))
        last = i == side - 1
        pieces = (side - 2, 1, 1) if last else (side,)
        outs = attend(block, keys, values, tile_lengths, scale, parts, pieces)
        if i == 0:
            merged = outs
        elif e == order[-2]:
            *merged, ready = merge(merged[0], along(outs[0], 0, -e), (side - 2, 1, 1), out_weight, 0)
        elif not last:
            merged = merge(merged[0], along(outs[0], 0, -e), (side,))
    two, three, here = outs
    far = along(merged[1], 1 - side, 0)
    straight = along(three, 1 - side, -e)
    here = merge(merged[2], along(here, 0, -e), (1,))[0]
    near = merge(merged[0], along(two, 0, -e), (1,) * (side - 2))
    beside, more = merge(far, straight, (1,), out_weight, FETCH)
    final = [here, beside] + [along(near[d - 1], -d, 0) for d in range(1, side - 1)]
    keep, give = project([ready, more], final, own, out_weight, group, ranks, cores)
    got = lax.ppermute(give, "kvh", [(k, k // cores * cores + (k + 1) % cores) for k in range(ranks)])
    share = keep.shape[0] // chips
    pieces = [
        keep[d * share : (d + 1) * share].astype(F32) + got[d * share : (d + 1) * share].astype(F32) for d in range(chips)
    ]
    result = pieces[0]
    for d in sorted(range(1, chips), key=lambda d: min(d, chips - d)):
        pairs = [(k, (k + d * cores) % ranks) for k in range(ranks)]
        result = result + lax.ppermute(pieces[d].astype(BF16), "kvh", pairs).astype(F32)
    return result.astype(BF16)


def solution(mesh):
    return jax.shard_map(
        local,
        mesh=mesh,
        in_specs=(
            P("owner", None, "kvh", None),
            P("owner", None, "kvh", None),
            P("owner", None, "kvh", None),
            P("owner", None),
            P("owner", "kvh", None, None),
            P("owner", "kvh", None, None),
            P("owner"),
            P("kvh", None),
        ),
        out_specs=P(("owner", "kvh"), None),
        check_vma=False,
    )
```

```python
import functools
import math

import jax
import jax.numpy as jnp
from jax import lax
from jax.experimental import pallas as pl
from jax.experimental.pallas import tpu as pltpu
from jax.sharding import PartitionSpec as P

NEG = -1e30
META = 16
STEP = 256
FEW = 2
FETCH = 2048
F32 = jnp.float32
BF16 = jnp.bfloat16
VMEM = pl.BlockSpec(memory_space=pltpu.VMEM)
SMEM = pl.BlockSpec(memory_space=pltpu.SMEM)
ANY = pl.BlockSpec(memory_space=pl.ANY)
LOG2 = 1.0 / math.log(2.0)


def to_lanes(column, count):
    r = lax.broadcasted_iota(jnp.int32, (128, 128), 0)
    c = lax.broadcasted_iota(jnp.int32, (128, 128), 1)
    eye = r == c
    rows = []
    for b in range(count // 128):
        rows.append(jnp.sum(jnp.where(eye, column[b * 128 : (b + 1) * 128], 0.0), axis=0, keepdims=True))
    return rows


def in_parts(lines):
    pieces = []
    for line in lines:
        high = line.astype(BF16).astype(F32)
        mid = (line - high).astype(BF16).astype(F32)
        pieces += [high, mid, line - high - mid]
    pad = jnp.zeros((META - len(pieces), 128), F32)
    return jnp.concatenate(pieces + [pad], axis=0).astype(BF16)


def levels(meta, b):
    return meta[3 * b : 3 * b + 1] + meta[3 * b + 1 : 3 * b + 2] + meta[3 * b + 2 : 3 * b + 3]


def pack_kernel(q_any, a_any, o_ref, a_ref, meta_ref, q_sem, a_sem):
    rows = q_any.shape[0]
    q_copy = pltpu.make_async_copy(q_any, o_ref.at[pl.ds(0, rows)], q_sem)
    a_copy = pltpu.make_async_copy(a_any, a_ref, a_sem)
    q_copy.start()
    a_copy.start()
    meta_ref[...] = jnp.full(meta_ref.shape, -1.0, F32)
    a_copy.wait()
    meta_ref[: a_ref.shape[0], : a_ref.shape[1]] = a_ref[...].astype(F32)
    o_ref[rows:, :] = meta_ref[...].astype(BF16)
    q_copy.wait()


def pack(q, ancestors):
    rows, width = q.shape
    return pl.pallas_call(
        pack_kernel,
        out_shape=jax.ShapeDtypeStruct((rows + META, width), BF16),
        in_specs=[ANY] * 2,
        out_specs=VMEM,
        scratch_shapes=[
            pltpu.VMEM(ancestors.shape, jnp.int32),
            pltpu.VMEM((META, width), F32),
            pltpu.SemaphoreType.DMA,
            pltpu.SemaphoreType.DMA,
        ],
        compiler_params=pltpu.CompilerParams(vmem_limit_bytes=4 << 20),
        cost_estimate=pl.CostEstimate(flops=1 << 10, bytes_accessed=1 << 18, transcendentals=0),
        name="pack",
    )(*(pltpu.with_memory_space_constraint(a, pltpu.HBM) for a in (q, ancestors)))


def prepare_kernel(scale, group, lengths, *refs):
    given, (kt_ref, va_ref, o_ref), held, sems = refs[:5], refs[5:8], refs[8:13], refs[13:]
    copies = [pltpu.make_async_copy(a, b, sem) for a, b, sem in zip(given, held, sems)]
    for copy in copies:
        copy.start()
    q_ref, nk_ref, nv_ref, k_ref, v_ref = held
    tiles, size, width = k_ref.shape
    for copy in copies:
        copy.wait()

    @pl.loop(0, tiles)
    def _(t):
        live = lax.broadcasted_iota(jnp.int32, (size, width), 0) < lengths[t]
        k = k_ref[t].astype(F32)
        kt_ref[t] = jnp.where(live, k, k[:1]).T.astype(BF16)
        va_ref[t, :, :width] = jnp.where(live, v_ref[t].astype(F32), 0.0).astype(BF16)
        va_ref[t, :, width:] = live.astype(F32).astype(BF16)

    halves, part, _ = q_ref.shape
    new = nk_ref.shape[1]
    rows = halves * part
    for i in range(halves):
        s = lax.dot_general(q_ref[i], nk_ref[i], (((1,), (1,)), ((), ())), preferred_element_type=F32)
        token = lax.broadcasted_iota(jnp.int32, (part, new), 0) // group
        seen = token >= lax.broadcasted_iota(jnp.int32, (part, new), 1)
        s = jnp.where(seen, s, NEG)
        peak = jnp.max(s, axis=1, keepdims=True)
        weights = jnp.where(seen, jnp.exp2((s - peak) * scale), 0.0)
        total = jnp.sum(weights, axis=1, keepdims=True)
        summed = jnp.dot(weights.astype(BF16), nv_ref[i], preferred_element_type=F32)
        o_ref[i * part : (i + 1) * part, :] = summed / total
        level = peak * scale + jnp.log(total) * LOG2
        rowed = to_lanes(jnp.broadcast_to(level, (part, width)), part)
        for b, line in enumerate(rowed):
            at = rows + i * len(rowed) + b
            o_ref[at : at + 1, :] = line


def prepare(lengths, q, new_keys, new_values, keys, values, scale, group):
    halves, part, width = q.shape
    tiles, size, _ = keys.shape
    return pl.pallas_call(
        functools.partial(prepare_kernel, scale, group),
        out_shape=[
            jax.ShapeDtypeStruct((tiles, width, size), BF16),
            jax.ShapeDtypeStruct((tiles, size, 2 * width), BF16),
            jax.ShapeDtypeStruct((halves * part + 8, width), F32),
        ],
        in_specs=[SMEM] + [ANY] * 5,
        out_specs=[VMEM] * 3,
        scratch_shapes=[pltpu.VMEM(a.shape, BF16) for a in (q, new_keys, new_values, keys, values)]
        + [pltpu.SemaphoreType.DMA] * 5,
        compiler_params=pltpu.CompilerParams(vmem_limit_bytes=44 << 20),
        cost_estimate=pl.CostEstimate(flops=1 << 24, bytes_accessed=16 << 20, transcendentals=1 << 15),
        name="prepare",
    )(lengths, *(pltpu.with_memory_space_constraint(a, pltpu.HBM) for a in (q, new_keys, new_values, keys, values)))


def attend_kernel(
    scale, halves, lengths, q_ref, k_ref, v_ref, *refs
):
    homes, held, width = q_ref.shape
    pieces, (s_ref, m_ref, acc_ref, member) = refs[:-4], refs[-4:]
    o_refs = [piece.at[i] for piece in pieces for i in range(piece.shape[0])]
    rows = held - META
    tiles, _, size = k_ref.shape
    part = rows // halves
    count = homes * halves

    names = jnp.concatenate([q_ref[h, rows:, :].astype(F32)[:halves] for h in range(homes)], axis=0)
    first = (lax.axis_index("owner") * tiles).astype(F32)
    bit = lax.broadcasted_iota(jnp.int32, (count, 1), 0)
    for t in range(tiles):
        inside = jnp.max(jnp.where(names == first + t, 1.0, 0.0), axis=1, keepdims=True)
        power = (1 << bit).astype(F32)
        member[t] = jnp.sum(inside * power).astype(jnp.int32)
        member[tiles + t] = jnp.sum(inside).astype(jnp.int32)
    m_ref[...] = jnp.full(m_ref.shape, NEG, F32)
    acc_ref[...] = jnp.zeros(acc_ref.shape, F32)

    def for_each_tile(body):
        @pl.loop(0, tiles)
        def _(t):
            held_by = member[t]
            number = member[tiles + t]
            for n in range(1, size // STEP + 1):
                fits = lengths[t] > (n - 1) * STEP
                if n * STEP < size:
                    fits = fits & (lengths[t] <= n * STEP)

                @pl.when(fits & (number > FEW))
                def _():
                    every = [(slice(i * part, (i + 1) * part), (held_by >> i) & 1 > 0) for i in range(count)]
                    body(t, n * STEP, q_ref[:, :rows, :].reshape(homes * rows, width), slice(None), every)

                @pl.when(fits & (number > 0) & (number <= FEW))
                def _():
                    @pl.loop(0, count)
                    def _(i):
                        @pl.when((held_by >> i) & 1 > 0)
                        def _():
                            q = q_ref[i // halves, pl.ds(pl.multiple_of(i % halves * part, part), part), :]
                            body(t, n * STEP, q, pl.ds(pl.multiple_of(i * part, part), part), [(slice(None), True)])

    def score(t, wide, q, span, blocks):
        s = jnp.dot(q, k_ref[t, :, :wide], preferred_element_type=F32)
        s_ref[t, span, :wide] = s
        for here, inside in blocks:
            x = s[here, :128]
            for j in range(128, wide, 128):
                x = jnp.maximum(x, s[here, j : j + 128])
            if inside is True:
                m_ref[span, :] = jnp.maximum(m_ref[span, :], x)
            else:
                m_ref[here, :] = jnp.maximum(m_ref[here, :], jnp.where(inside, x, NEG))

    for_each_tile(score)
    peak = jnp.max(m_ref[...], axis=1, keepdims=True) * scale
    m_ref[...] = jnp.broadcast_to(peak, m_ref.shape)

    def weigh(t, wide, q, span, blocks):
        weights = []
        for here, inside in blocks:
            rows_here = span if inside is True else here
            shift = m_ref[rows_here, :]
            if inside is not True:
                shift = jnp.where(inside, shift, -NEG)
            weights.append(
                jnp.concatenate(
                    [jnp.exp2(s_ref[t, rows_here, j : j + 128] * scale - shift).astype(BF16) for j in range(0, wide, 128)],
                    axis=1,
                )
            )
        weights = weights[0] if len(weights) == 1 else jnp.concatenate(weights, axis=0)
        acc_ref[span, :] += jnp.dot(weights, v_ref[t, :wide, :], preferred_element_type=F32)

    for_each_tile(weigh)
    for h in range(homes):
        here = slice(h * rows, (h + 1) * rows)
        total = acc_ref[here, width:]
        o_refs[h][:rows, :] = (acc_ref[here, :width] / jnp.maximum(total, -1.0 / NEG)).astype(BF16)
        sums = jnp.concatenate(to_lanes(total, rows), axis=0)
        peaks = jnp.concatenate(to_lanes(m_ref[here, :], rows), axis=0)
        level = jnp.where(sums > 0.0, peaks + jnp.log(jnp.maximum(sums, -1.0 / NEG)) * LOG2, NEG)
        o_refs[h][rows:, :] = in_parts([level[b : b + 1] for b in range(rows // 128)])


def attend(q, keys, values, lengths, scale, halves, pieces):
    homes, held, width = q.shape
    tiles, _, size = keys.shape
    rows = held - META
    return pl.pallas_call(
        functools.partial(attend_kernel, scale, halves),
        out_shape=[jax.ShapeDtypeStruct((piece, held, width), BF16) for piece in pieces],
        in_specs=[SMEM, VMEM, VMEM, VMEM],
        out_specs=[VMEM] * len(pieces),
        scratch_shapes=[
            pltpu.VMEM((tiles, homes * rows, size), F32),
            pltpu.VMEM((homes * rows, 128), F32),
            pltpu.VMEM((homes * rows, 2 * width), F32),
            pltpu.SMEM((2 * tiles,), jnp.int32),
        ],
        compiler_params=pltpu.CompilerParams(vmem_limit_bytes=44 << 20),
        cost_estimate=pl.CostEstimate(flops=1 << 20, bytes_accessed=1 << 18, transcendentals=0),
        name="attend",
    )(lengths, q, keys, values)


def weights_of(lines):
    level = jnp.concatenate(lines + [jnp.full((128 - len(lines), 128), 2 * NEG, F32)], axis=0)
    top = jnp.max(level, axis=0, keepdims=True)
    weight = jnp.exp2(level - top)
    total = jnp.sum(weight, axis=0, keepdims=True)
    return (weight / total).T, top + jnp.log(total) * LOG2


def merge_kernel(first, one_ref, two_ref, *refs):
    homes, held, _ = two_ref.shape
    copy = None
    if first is not None:
        w_ref, *refs, part_ref, sem = refs
        copy = pltpu.make_async_copy(w_ref.at[:, pl.ds(first, part_ref.shape[1])], part_ref, sem)
        copy.start()
    o_refs = [ref.at[i] for ref in refs for i in range(ref.shape[0])]
    rows = held - META
    for h in range(homes):
        given = [one_ref.at[h], two_ref.at[h]]
        metas = [a[rows:, :].astype(F32) for a in given]
        lines = []
        for b in range(rows // 128):
            weight, line = weights_of([levels(meta, b) for meta in metas])
            lines.append(line)
            here = slice(b * 128, (b + 1) * 128)
            acc = given[0][here, :].astype(F32) * weight[:, 0:1] + given[1][here, :].astype(F32) * weight[:, 1:2]
            o_refs[h][here, :] = acc.astype(BF16)
        o_refs[h][rows:, :] = in_parts(lines)
    if copy is not None:
        copy.wait()


def merge(one, two, pieces, weight=None, first=None):
    _, held, width = two.shape
    out = [jax.ShapeDtypeStruct((piece, held, width), BF16) for piece in pieces]
    extra = []
    if weight is not None:
        out.append(jax.ShapeDtypeStruct((weight.shape[0], FETCH), BF16))
        extra = [pltpu.with_memory_space_constraint(weight, pltpu.HBM)]
    return pl.pallas_call(
        functools.partial(merge_kernel, first),
        out_shape=out,
        in_specs=[VMEM] * 2 + [ANY] * len(extra),
        out_specs=[VMEM] * len(out),
        scratch_shapes=[pltpu.SemaphoreType.DMA] * len(extra),
        compiler_params=pltpu.CompilerParams(vmem_limit_bytes=16 << 20),
        cost_estimate=pl.CostEstimate(flops=1 << 30, bytes_accessed=1 << 18, transcendentals=0),
        name="merge",
    )(one, two, *extra)


def project_kernel(group, ranks, cores, ahead, *refs):
    a_refs, (own_ref, w_ref, keep_ref, give_ref, sum_ref, all_ref, flat_ref, held_ref, sems) = refs[:-9], refs[-9:]
    ready, a_refs = a_refs[:ahead], [a.at[0] for a in a_refs[ahead:]]
    blocks, _, block = held_ref.shape
    begin = ahead * FETCH
    copies = [
        pltpu.make_async_copy(w_ref.at[:, pl.ds(begin + j * block, block)], held_ref.at[j], sems.at[j])
        for j in range(blocks)
    ]
    for copy in copies:
        copy.start()
    rows, width = sum_ref.shape
    metas = [a[rows:, :].astype(F32) for a in a_refs]
    for b in range(rows // 128):
        weight, _ = weights_of([own_ref[rows + b : rows + b + 1, :]] + [levels(meta, b) for meta in metas])
        here = slice(b * 128, (b + 1) * 128)
        acc = own_ref[here, :] * weight[:, 0:1]
        for i, a in enumerate(a_refs):
            acc = acc + a[here, :].astype(F32) * weight[:, i + 1 : i + 2]
        sum_ref[here, :] = acc
    tokens = rows // group
    for g in range(group):
        all_ref[:, g * width : (g + 1) * width] = sum_ref[pl.ds(g, tokens, stride=group), :]
    chips = ranks // cores
    share = tokens // ranks
    rank = lax.axis_index("kvh")
    chip, core = rank // cores, rank % cores
    for i in range(cores):
        for d in range(chips):
            to = ((chip + d) % chips) * cores + (core + i) % cores
            at = (i * chips + d) * share
            flat_ref[at : at + share, :] = all_ref[pl.ds(pl.multiple_of(to * share, share), share), :]
    flat = flat_ref[...].astype(BF16)
    half = tokens // cores

    def multiply(columns, at):
        out = jnp.dot(flat, columns, preferred_element_type=F32).astype(BF16)
        keep_ref[:, at : at + block] = out[:half]
        give_ref[:, at : at + block] = out[half:]

    for i, ref in enumerate(ready):
        for j in range(0, FETCH, block):
            multiply(ref[:, j : j + block], i * FETCH + j)
    for j, copy in enumerate(copies):
        copy.wait()
        multiply(held_ref[j], begin + j * block)


def project(ready, parts, own, weight, group, ranks, cores):
    _, held, width = parts[0].shape
    rows = held - META
    depth, columns = weight.shape
    tokens = rows // group
    block = 1024
    blocks = (columns - len(ready) * FETCH) // block
    return pl.pallas_call(
        functools.partial(project_kernel, group, ranks, cores, len(ready)),
        out_shape=[jax.ShapeDtypeStruct((tokens // cores, columns), BF16)] * 2,
        in_specs=[VMEM] * (len(ready) + len(parts) + 1) + [ANY],
        out_specs=[VMEM] * 2,
        scratch_shapes=[
            pltpu.VMEM((rows, width), F32),
            pltpu.VMEM((tokens, depth), F32),
            pltpu.VMEM((tokens, depth), F32),
            pltpu.VMEM((blocks, depth, block), BF16),
            pltpu.SemaphoreType.DMA((blocks,)),
        ],
        compiler_params=pltpu.CompilerParams(vmem_limit_bytes=24 << 20),
        cost_estimate=pl.CostEstimate(flops=1 << 30, bytes_accessed=18 << 20, transcendentals=1 << 14),
        name="project",
    )(*ready, *parts, own, pltpu.with_memory_space_constraint(weight, pltpu.HBM))


def local(
    queries, new_keys, new_values, ancestors, tile_keys, tile_values, tile_lengths, out_weight
):
    owners = lax.axis_size("owner")
    ranks = lax.axis_size("kvh")
    cores = 2
    chips = ranks // cores
    side = math.isqrt(owners)
    parts, new, group, width = queries.shape
    per_owner = tile_keys.shape[0]
    scale = width**-0.5 * LOG2
    rows = parts * new * group

    def along(x, *steps):
        pairs = []
        for o in range(owners):
            for k in range(ranks):
                dz, dy = steps if k % cores == 0 else steps[::-1]
                y, z = (o // side + dy) % side, (o + dz) % side
                pairs.append((o * ranks + k, (y * side + z) * ranks + k))
        return lax.ppermute(x, ("owner", "kvh"), pairs)

    home = pack(queries.reshape(rows, width), ancestors)
    near = [along(home, d, 0) for d in range(1, side)]
    keys, values, own = prepare(
        tile_lengths,
        queries.reshape(parts, new * group, width),
        new_keys[:, :, 0],
        new_values[:, :, 0],
        tile_keys[:, 0],
        tile_values[:, 0],
        scale,
        group,
    )
    row, keys, values = lax.optimization_barrier((jnp.stack(near + [home]), keys, values))
    order = sorted(range(side), key=lambda e: min(e, side - e))
    blocks = {e: along(row, 0, e) if e else row for e in order[:-1]}
    outs = None
    for i, e in enumerate(order):
        if i == 1:
            late, outs = lax.optimization_barrier((row, outs))
            blocks[order[-1]] = along(late, 0, order[-1])
        block = blocks[e]
        if e:
            block, outs = lax.optimization_barrier((block, outs))
        last = i == side - 1
        pieces = (side - 2, 1, 1) if last else (side,)
        outs = attend(block, keys, values, tile_lengths, scale, parts, pieces)
        if i == 0:
            merged = outs
        elif e == order[-2]:
            merged = merge(merged[0], along(outs[0], 0, -e), (side - 2, 1, 1))
        elif not last:
            merged = merge(merged[0], along(outs[0], 0, -e), (side,))
    two, three, here = outs
    far = along(merged[1], 1 - side, 0)
    straight = along(three, 1 - side, -e)
    here = merge(merged[2], along(here, 0, -e), (1,))[0]
    near = merge(merged[0], along(two, 0, -e), (1,) * (side - 2))
    beside, more = merge(far, straight, (1,), out_weight, 0)
    final = [here, beside] + [along(near[d - 1], -d, 0) for d in range(1, side - 1)]
    keep, give = project([more], final, own, out_weight, group, ranks, cores)
    got = lax.ppermute(give, "kvh", [(k, k // cores * cores + (k + 1) % cores) for k in range(ranks)])
    share = keep.shape[0] // chips
    pieces = [
        keep[d * share : (d + 1) * share].astype(F32) + got[d * share : (d + 1) * share].astype(F32) for d in range(chips)
    ]
    result = pieces[0]
    for d in sorted(range(1, chips), key=lambda d: min(d, chips - d)):
        pairs = [(k, (k + d * cores) % ranks) for k in range(ranks)]
        result = result + lax.ppermute(pieces[d].astype(BF16), "kvh", pairs).astype(F32)
    return result.astype(BF16)


def solution(mesh):
    return jax.shard_map(
        local,
        mesh=mesh,
        in_specs=(
            P("owner", None, "kvh", None),
            P("owner", None, "kvh", None),
            P("owner", None, "kvh", None),
            P("owner", None),
            P("owner", "kvh", None, None),
            P("owner", "kvh", None, None),
            P("owner"),
            P("kvh", None),
        ),
        out_specs=P(("owner", "kvh"), None),
        check_vma=False,
    )
```
